128 devices in a mesh: gcm: 8 (over y, core), crm: 16 (over x, z).
Axes of the slice: x: 4, y: 4, z: 4, core: 2. Of those that a mesh axis runs over, the one named last changes fastest.
Arguments:
- tracer: float32 [72, 64, 4096], P(None, 'gcm', 'crm'), may hold values from -6 to 6
- wind_x: float32 [72, 64, 4096], P(None, 'gcm', 'crm'), may hold values from -4 to 4
- wind_y: float32 [72, 64, 4096], P(None, 'gcm', 'crm'), may hold values from -4 to 4
- drops: bfloat16 [16384, 33, 256], P(('gcm', 'crm')), may hold values from 0 to 1
- owner: int32 [16384, 1], P(('gcm', 'crm')), may hold values from 0 to 127, as said below
- counts: int32 [16384], P(('gcm', 'crm')), may hold values from 0 to 4, as said below
- collision: bfloat16 [33, 1089], replicated, may hold values from -0.1875 to 0.1875
- growth: float32 [33], replicated, may hold values from -4 to 4
Outputs:
- tracer_next: float32 [72, 64, 4096], P(None, 'gcm', 'crm')
- drops_next: bfloat16 [16384, 33, 256], P(('gcm', 'crm'))
- power: float32 [16, 32768], P(None, ('gcm', 'crm'))
The draws below stay inside these ranges and needn't reach their ends.
Inputs may be any that keep to these rules, and one draw needn't show every extreme that they name: Owner index in gcm-then-crm device order; among the 128 columns of one device no owner appears more than 2 times, and some owner appears exactly 2 times. `counts`: how cloudy the columns are differs from device to device.
All inputs are finite; a program needn't handle non-finite values.
Results may differ from the reference program's by a relative error of at most 0.0018.
Values may be sent and summed in bfloat16 or wider, within the bound.
A program may use at most 128 MiB of HBM per device.

```python
import jax
import jax.numpy as jnp
import numpy as np
from jax import lax

NPTS = 4
LEV = 72
BINS = 33
CRM_X = 16
CRM_LEV = 16
SUB_MAX = 4
DYN_STEPS = 2
SLOT_BLOCK = 16
EX_DEV = 2
EY_DEV = 64
CELLS = 256
COL_DEV = 128
CAP = 2
SLOTS = 256
COLS = 16384
N_GCM = 8
N_CRM = 16


def draw_owner(key, part):
    devices = COLS // COL_DEV
    order_key, choose_key = jax.random.split(jax.random.fold_in(key, 17), 2)
    device_keys = jax.random.split(order_key, devices)
    choose_keys = jax.random.split(choose_key, devices)
    orders = jax.vmap(lambda k: jax.random.permutation(k, COL_DEV))(device_keys)
    picks = jax.vmap(lambda k: jax.random.permutation(k, devices))(choose_keys)
    groups = (orders.astype(jnp.int32) // CAP).astype(jnp.int32)
    values = jnp.take_along_axis(picks.astype(jnp.int32), groups, axis=1)
    return values.reshape(COLS, 1).astype(jnp.int32)


def draw_counts(key, part):
    devices = COLS // COL_DEV
    flag_key, pick_key, cloudy_key, clear_key = jax.random.split(key, 4)
    flagged = jax.random.randint(flag_key, (devices, 1), 0, 8) == 0
    chosen = jax.random.randint(pick_key, (), 0, devices)
    flagged = flagged | (jnp.arange(devices)[:, None] == chosen)
    column_index = jnp.arange(COL_DEV)[None, :]
    lowered = (jax.random.randint(cloudy_key, (devices, COL_DEV), 0, 4) == 0) & (column_index > 0)
    cloudy_values = SUB_MAX - lowered.astype(jnp.int32)
    clear_values = jax.random.randint(clear_key, (devices, COL_DEV), 0, 2)
    values = jnp.where(flagged, cloudy_values, clear_values)
    return values.reshape(COLS).astype(jnp.int32)


def steps_of(stream_key, shape, cuts, smallest, high):
    def one(axis_at, shards_of):
        draws = jax.random.uniform(jax.random.fold_in(jax.random.fold_in(stream_key, 6), axis_at), (shards_of,), jnp.float32, smallest / len(cuts), high / len(cuts))
        return jnp.repeat(jnp.exp(draws), shape[axis_at] // shards_of).reshape((-1,) + (1,) * (len(shape) - axis_at - 1))

    gain = one(*cuts[0])
    for cut in cuts[1:]:
        gain = gain * one(*cut)
    return gain


def normal_values(own_key, extent, scale, most, cuts=(), kind=jnp.bfloat16):
    values = jax.random.normal(own_key, extent, jnp.float32) * scale
    if len(cuts) > 0:
        values = steps_of(own_key, extent, cuts, -0.22, 0.18) * values
    return jnp.clip(values, min=-most, max=most).astype(kind)


def setup_inputs(seed: int = 0) -> dict:
    splits = jax.random.split(jax.random.key(seed), 9)
    tracer = normal_values(splits[0], (LEV, NPTS * EX_DEV * N_GCM, NPTS * EY_DEV * N_CRM), 1.0, 6.0, ((1, 8), (2, 16)), jnp.float32)
    wind_x = normal_values(splits[1], (LEV, NPTS * EX_DEV * N_GCM, NPTS * EY_DEV * N_CRM), 1.0, 4.0, ((1, 8), (2, 16)), jnp.float32)
    wind_y = normal_values(splits[2], (LEV, NPTS * EX_DEV * N_GCM, NPTS * EY_DEV * N_CRM), 1.0, 4.0, ((1, 8), (2, 16)), jnp.float32)
    drops = jnp.clip(1.0 * jax.random.uniform(splits[3], (COLS, BINS, CELLS), jnp.float32) ** steps_of(splits[3], (COLS, BINS, CELLS), ((0, 128),), -0.2, 0.2), 0.0, 1.0).astype(jnp.bfloat16)
    owner = draw_owner(jax.random.fold_in(splits[8], 71), 0)
    counts = draw_counts(jax.random.fold_in(splits[8], 71), 0)
    collision = normal_values(splits[6], (BINS, BINS * BINS), (BINS * BINS) ** -0.5, 0.1875)
    growth = normal_values(splits[7], (BINS,), 1.0, 4.0, (), jnp.float32)
    return dict(tracer=tracer, wind_x=wind_x, wind_y=wind_y, drops=drops, owner=owner, counts=counts, collision=collision, growth=growth)


DT_DYN = 0.04
DT_CRM = 0.05
DT_PHYS = 0.5
HIGH = lax.Precision.HIGHEST

def gll_tables():
    inv_root = 1.0 / np.sqrt(5.0)
    gll_nodes = np.array([-1.0, -inv_root, inv_root, 1.0])
    weights = np.array([1.0, 5.0, 5.0, 1.0]) / 6.0
    legendre = (5.0 * gll_nodes ** 3 - 3.0 * gll_nodes) / 2.0
    derivative = np.zeros((4, 4))
    for i in range(4):
        for j in range(4):
            if i != j:
                derivative[i, j] = legendre[i] / (legendre[j] * (gll_nodes[i] - gll_nodes[j]))
    derivative[0, 0] = -3.0
    derivative[3, 3] = 3.0
    return (2.0 * derivative, weights)

def level_tables(levels, crm_levels):
    spacing = levels / crm_levels
    centres = (np.arange(crm_levels) + 0.5) * spacing - 0.5
    hats = np.maximum(0.0, 1.0 - np.abs(np.arange(levels)[None, :] - centres[:, None]) / spacing)
    down_map = hats / hats.sum(axis=1, keepdims=True)
    up_map = hats.T / hats.T.sum(axis=1, keepdims=True)
    return (down_map, up_map)

def sum_rows(padded):
    row_count = padded.shape[1] - 2
    phase = (jnp.arange(row_count) % 4)[None, :, None]
    middle = padded[:, 1:-1]
    return middle + jnp.where(phase == 3, padded[:, 2:], 0.0) + jnp.where(phase == 0, padded[:, :-2], 0.0)

def sum_cols(padded):
    col_count = padded.shape[2] - 2
    phase = (jnp.arange(col_count) % 4)[None, None, :]
    middle = padded[:, :, 1:-1]
    return middle + jnp.where(phase == 3, padded[:, :, 2:], 0.0) + jnp.where(phase == 0, padded[:, :, :-2], 0.0)

def wrap_sum(field):
    return sum_cols(sum_rows(jnp.pad(field, ((0, 0), (1, 1), (1, 1)), mode='wrap')))

def advect(tracer, wind_x, wind_y, derivative):
    levels, row_count, col_count = tracer.shape
    by_rows = tracer.reshape(levels, row_count // 4, 4, col_count)
    grad_x = jnp.einsum('ij,lejc->leic', derivative, by_rows, precision=HIGH).reshape(tracer.shape)
    by_cols = tracer.reshape(levels, row_count, col_count // 4, 4)
    grad_y = jnp.einsum('ij,lrej->lrei', derivative, by_cols, precision=HIGH).reshape(tracer.shape)
    return -(wind_x * grad_x + wind_y * grad_y)

def crm_substep(state, cell_forcing, growth, collision):
    grown = state + DT_CRM * cell_forcing[:, None, :] * growth[None, :, None]
    slot_count, bin_count, cell_count = grown.shape
    pairs = (grown[:, :, None, :] * grown[:, None, :, :]).reshape(slot_count, bin_count * bin_count, cell_count)
    pairs = lax.optimization_barrier(pairs.astype(jnp.bfloat16)).astype(state.dtype)
    change = jnp.einsum('kq,sqc->skc', collision.astype(state.dtype), pairs)
    return grown + DT_CRM * change

def summarize(final, initial):
    slot_count, bin_count, cell_count = final.shape
    mass = (jnp.arange(bin_count).astype(final.dtype) + 1.0) / bin_count
    heat = jnp.einsum('b,sbc->sc', mass, final - initial, precision=HIGH)
    echo = jnp.einsum('b,sbc->sc', mass * mass, final * final, precision=HIGH)
    heat = heat.reshape(slot_count, cell_count // CRM_X, CRM_X).mean(axis=2)
    echo = echo.reshape(slot_count, cell_count // CRM_X, CRM_X).mean(axis=2)
    return (heat, jnp.log(1.0 + echo))

def reference(tracer, wind_x, wind_y, drops, owner, counts, collision, growth):
    ftype = tracer.dtype
    devices = N_GCM * N_CRM
    derivative, gll_weights = gll_tables()
    derivative = jnp.asarray(derivative, ftype)
    gll_weights = jnp.asarray(gll_weights, ftype)
    levels, row_count, col_count = tracer.shape
    mass_pattern = jnp.outer(jnp.tile(gll_weights, row_count // 4), jnp.tile(gll_weights, col_count // 4))[None]
    denominator = wrap_sum(mass_pattern)
    state = tracer
    for step in range(DYN_STEPS):
        state = state + DT_DYN * wrap_sum(advect(state, wind_x, wind_y, derivative) * mass_pattern) / denominator
    blocks = ((state - tracer) / (DYN_STEPS * DT_DYN)).reshape(levels, row_count // 4, 4, col_count // 4, 4)
    means = jnp.einsum('laibj,i,j->abl', blocks, gll_weights, gll_weights, precision=HIGH) / 4.0
    means = means.reshape(N_GCM, EX_DEV, N_CRM, EY_DEV, levels).transpose(0, 2, 1, 3, 4).reshape(COLS, levels)
    down_map, up_map = level_tables(levels, CRM_LEV)
    forcing = jnp.dot(means, jnp.asarray(down_map.T, ftype), precision=HIGH).astype(jnp.bfloat16)

    def run_block(block):
        block_drops, block_forcing, block_counts = block
        initial = block_drops.astype(ftype)
        cell_forcing = jnp.repeat(block_forcing.astype(ftype), CRM_X, axis=1)

        def advance(step, current):
            moved = crm_substep(current, cell_forcing, growth, collision)
            return jnp.where((step < block_counts)[:, None, None], moved, current)
        final = lax.fori_loop(jnp.int32(0), jnp.max(block_counts).astype(jnp.int32), advance, initial)
        heat, echo_power = summarize(final, initial)
        return (final.astype(jnp.bfloat16), heat.astype(jnp.bfloat16), echo_power)
    nblock = COLS // SLOT_BLOCK
    finals, heats, powers = lax.map(run_block, (drops.reshape((nblock, SLOT_BLOCK) + drops.shape[1:]), forcing.reshape(nblock, SLOT_BLOCK, CRM_LEV), counts.reshape(nblock, SLOT_BLOCK)))
    drops_next = finals.reshape(drops.shape)
    heat = lax.optimization_barrier(heats.reshape(COLS, CRM_LEV)).astype(ftype)
    echo_power = powers.reshape(COLS, CRM_LEV)
    back = jnp.dot(heat, jnp.asarray(up_map.T, ftype), precision=HIGH)
    back = back.reshape(N_GCM, N_CRM, EX_DEV, EY_DEV, levels).transpose(0, 2, 1, 3, 4).reshape(EX_DEV * N_GCM, EY_DEV * N_CRM, levels)
    grid = jnp.transpose(back, (2, 0, 1))[:, :, None, :, None]
    spread = jnp.broadcast_to(grid, (levels, row_count // 4, 4, col_count // 4, 4)).reshape(tracer.shape)
    tracer_next = wrap_sum((state + DT_PHYS * spread) * mass_pattern) / denominator
    owners = owner[:, 0]
    onehot = (owners.reshape(devices, COL_DEV)[:, :, None] == jnp.arange(devices, dtype=jnp.int32)[None, None, :]).astype(jnp.int32)
    earlier = jnp.cumsum(onehot, axis=1) - onehot
    position = lax.optimization_barrier(jnp.sum(earlier * onehot, axis=2)).reshape(COLS)
    sources = (jnp.arange(COLS, dtype=jnp.int32) // COL_DEV).astype(jnp.int32)
    slot_index = (owners * SLOTS + sources * CAP + position).astype(jnp.int32)
    power = jnp.zeros((CRM_LEV, devices * SLOTS), ftype).at[:, slot_index].set(echo_power.T)
    return (tracer_next, drops_next, power)
```

```python
import functools

import jax
import jax.numpy as jnp
import ml_dtypes
import numpy as np
from jax import lax
from jax.experimental import pallas as pl
from jax.experimental.pallas import tpu as pltpu
from jax.sharding import PartitionSpec as P

BF = jnp.bfloat16
F32 = jnp.float32
MESH = pl.DeviceIdType.MESH
HIGH = lax.Precision.HIGHEST
VMEM = pl.BlockSpec(memory_space=pltpu.VMEM)
SMEM = pl.BlockSpec(memory_space=pltpu.SMEM)

NG = 8
NC = 16
LEV = 72
BINS = 33
CLEV = 16
COLS = 128
PTS = LEV * 8
PAIRS = 576
DT_DYN = 0.04
DT_CRM = 0.05
DT_PHYS = 0.5
BATCH = 4


def gll_tables():
    inv_root = 1.0 / np.sqrt(5.0)
    gll_nodes = np.array([-1.0, -inv_root, inv_root, 1.0])
    weights = np.array([1.0, 5.0, 5.0, 1.0]) / 6.0
    legendre = (5.0 * gll_nodes**3 - 3.0 * gll_nodes) / 2.0
    derivative = np.zeros((4, 4))
    for i in range(4):
        for j in range(4):
            if i != j:
                derivative[i, j] = legendre[i] / (legendre[j] * (gll_nodes[i] - gll_nodes[j]))
    derivative[0, 0] = -3.0
    derivative[3, 3] = 3.0
    return (2.0 * derivative, weights)


def level_tables(levels, crm_levels):
    spacing = levels / crm_levels
    centres = (np.arange(crm_levels) + 0.5) * spacing - 0.5
    hats = np.maximum(0.0, 1.0 - np.abs(np.arange(levels)[None, :] - centres[:, None]) / spacing)
    down_map = hats / hats.sum(axis=1, keepdims=True)
    up_map = hats.T / hats.T.sum(axis=1, keepdims=True)
    return (down_map, up_map)


def stencil_table():
    derivative, _ = gll_tables()
    out = np.zeros((14, 8, 128), np.float32)
    for s in range(-3, 4):
        for i in range(4):
            if 0 <= i + s < 4:
                out[s + 3, i::4, :] = -derivative[i, i + s]
                out[s + 10, :, i::4] = -derivative[i, i + s]
    return out


def forcing_tables():
    _, weights = gll_tables()
    down_map, _ = level_tables(LEV, CLEV)
    rows = np.zeros((2, CLEV, LEV, 8))
    for r in range(8):
        rows[r // 4, :, :, r] = down_map * weights[r % 4] / 2.0 * 0.5
    cols = np.zeros((64, 256))
    for c in range(256):
        cols[c // 4, c] = weights[c % 4] / 2.0
    return rows.reshape(32, PTS).astype(np.float32), cols.astype(np.float32)


def spread_cells():
    out = np.zeros((CLEV, 256), np.float32)
    for c in range(256):
        out[c // 16, c] = 1.0
    return out.astype(ml_dtypes.bfloat16)


def group_matrix():
    out = np.zeros((256, 128), np.float32)
    for c in range(256):
        out[c, c // 16] = 1.0 / 16.0
    return out.astype(ml_dtypes.bfloat16)


def heating_table():
    _, up_map = level_tables(LEV, CLEV)
    half = (DT_PHYS * up_map).astype(np.float32)
    first = half.astype(ml_dtypes.bfloat16)
    second = (half - first.astype(np.float32)).astype(ml_dtypes.bfloat16)
    out = np.zeros((LEV, 8, 2, 2, CLEV), ml_dtypes.bfloat16)
    for r in range(8):
        out[:, r, 0, r // 4, :] = first
        out[:, r, 1, r // 4, :] = second
    return out.reshape(PTS, 64)


def spread_columns():
    out = np.zeros((64, 256), np.float32)
    for c in range(256):
        out[c // 4, c] = 1.0
    return out.astype(ml_dtypes.bfloat16)


def slot_table():
    out = np.zeros((2, 128, 256), np.float32)
    for d in range(128):
        for r in range(2):
            out[r, d, 2 * d + r] = 1.0
    return out.reshape(256, 256).astype(ml_dtypes.bfloat16)


def pair_list():
    out = []
    for d in range(16):
        for i in range(32):
            out.append((i, (i + d) % 32))
    for i in range(16):
        out.append((i, i + 16))
    for i in range(32):
        out.append((i, 32))
    out.append((32, 32))
    return out


def pair_selector():
    out = np.zeros((BINS * BINS, PAIRS), np.float32)
    for q, (i, j) in enumerate(pair_list()):
        out[i * BINS + j, q] = 1.0
        out[j * BINS + i, q] = 1.0
    return out.astype(ml_dtypes.bfloat16)


def split3(x):
    hi = x.astype(BF)
    rest = x - hi.astype(F32)
    mid = rest.astype(BF)
    return hi, mid, (rest - mid.astype(F32)).astype(BF)


def dot_exact(onehot, x):
    acc = None
    for part in split3(x):
        y = jnp.dot(onehot, part, preferred_element_type=F32)
        acc = y if acc is None else acc + y
    return acc


def tendency(q, wind_x, wind_y, table):
    grad_x = table[3][None] * q
    grad_y = table[10][None] * q
    for s in (-3, -2, -1, 1, 2, 3):
        grad_x = grad_x + table[s + 3][None] * pltpu.roll(q, (-s) % 8, 1)
        grad_y = grad_y + table[s + 10][None] * pltpu.roll(q, (-s) % 128, 2)
    return wind_x * grad_x + wind_y * grad_y


def neighbours():
    g = lax.axis_index("gcm")
    c = lax.axis_index("crm")
    up, down = lax.rem(g + NG - 1, NG), lax.rem(g + 1, NG)
    left, right = lax.rem(c + NC - 1, NC), lax.rem(c + 1, NC)
    return g, c, up, down, left, right


def pack_edges(field, packs, rows):
    lane = lax.broadcasted_iota(jnp.int32, (8, 128), 1)

    def one(i, carry):
        low, high = carry
        low, high = pltpu.roll(low, 120, 1), pltpu.roll(high, 120, 1)
        for k in range(8):
            at = pl.multiple_of(i * 64, 64) + 8 * k
            first, last = field[pl.ds(at, 8), :], field[pl.ds(PTS + at, 8), :]
            both = pltpu.roll(jnp.where(lane == 0, first, last), k + 1, 1)
            high = jnp.where(lane == k, both, high)
            low = jnp.where(lane == k + 1, both, low)
        return low, high

    zero = jnp.zeros((8, 128), F32)
    low, high = lax.fori_loop(0, 9, one, (zero, zero))
    packs[0] = pltpu.roll(low, 63, 1)
    packs[1] = pltpu.roll(high, 64, 1)
    for half in range(2):
        rows[0, half * LEV : (half + 1) * LEV, :] = field[pl.ds(half * PTS, LEV, stride=8), :]
        rows[1, half * LEV : (half + 1) * LEV, :] = field[pl.ds(half * PTS + 7, LEV, stride=8), :]


def halo_copies(packs, rows, got_packs, got_rows, send, recv):
    g, c, up, down, left, right = neighbours()
    plan = [
        (rows.at[1], got_rows.at[0], (down, c)),
        (rows.at[0], got_rows.at[1], (up, c)),
        (packs.at[1], got_packs.at[0], (g, right)),
        (packs.at[1], got_packs.at[1], (down, right)),
        (packs.at[1], got_packs.at[2], (up, right)),
        (packs.at[0], got_packs.at[3], (g, left)),
        (packs.at[0], got_packs.at[4], (down, left)),
        (packs.at[0], got_packs.at[5], (up, left)),
    ]
    return [
        pltpu.make_async_remote_copy(
            src_ref=src,
            dst_ref=dst,
            send_sem=send.at[n],
            recv_sem=recv.at[n],
            device_id=to,
            device_id_type=MESH,
        )
        for n, (src, dst, to) in enumerate(plan)
    ]


def assemble_loop(field, got_packs, got_rows, use):
    row = lax.broadcasted_iota(jnp.int32, (8, 128), 0)
    lane = lax.broadcasted_iota(jnp.int32, (8, 128), 1)

    def row_mean(x, above, below):
        up = jnp.where(row == 0, pltpu.roll(above, 1, 0), pltpu.roll(x, 1, 0))
        down = jnp.where(row == 7, pltpu.roll(below, 7, 0), pltpu.roll(x, 7, 0))
        other = jnp.where(row % 4 == 3, down, jnp.where(row % 4 == 0, up, x))
        return 0.5 * (x + other)

    left_halo = row_mean(got_packs[0], got_packs[1], got_packs[2])
    right_halo = row_mean(got_packs[3], got_packs[4], got_packs[5])
    edge_row = ((row == 0) | (row == 7))[None]
    upper = (row < 4)[None]
    is3, is4 = (row == 3)[None], (row == 4)[None]
    lane3, lane0 = (lane % 4 == 3)[None], (lane % 4 == 0)[None]
    first, last = (lane == 0)[None], (lane == 127)[None]

    def one(i, carry):
        left_c, right_c = carry
        means = []
        for half in range(2):
            at = pl.multiple_of(half * PTS + i * 64, 64)
            x = field[pl.ds(at, 64), :].reshape(8, 8, 128)
            lev = pl.multiple_of(half * LEV + i * 8, 8)
            above = jnp.broadcast_to(got_rows[0, pl.ds(lev, 8), :][:, None, :], (8, 8, 128))
            below = jnp.broadcast_to(got_rows[1, pl.ds(lev, 8), :][:, None, :], (8, 8, 128))
            other = jnp.where(is3, pltpu.roll(x, 7, 1), jnp.where(is4, pltpu.roll(x, 1, 1), x))
            other = jnp.where(edge_row, jnp.where(upper, above, below), other)
            means.append(0.5 * (x + other))
        lefts = [pltpu.roll(m, 1, 2) for m in means]
        rights = [pltpu.roll(m, 127, 2) for m in means]
        halo_l = jnp.stack([pltpu.roll(left_c, (128 - k) % 128, 1) if k else left_c for k in range(8)])
        halo_r = jnp.stack([pltpu.roll(right_c, 127 - k, 1) for k in range(8)])
        near_l = [jnp.where(first, halo_l, lefts[0]), jnp.where(first, lefts[0], lefts[1])]
        near_r = [jnp.where(last, rights[1], rights[0]), jnp.where(last, halo_r, rights[1])]
        for half in range(2):
            m = means[half]
            other = jnp.where(lane3, near_r[half], jnp.where(lane0, near_l[half], m))
            use(i, half, 0.5 * (m + other))
        return pltpu.roll(left_c, 120, 1), pltpu.roll(right_c, 120, 1)

    lax.fori_loop(0, 9, one, (left_halo, right_halo))


def chunk_of(ref, i, half):
    return ref[pl.ds(i * 8, 8), :, half * 128 : (half + 1) * 128]


def dynamics_kernel(
    tracer, wind_x, wind_y, counts, collision, table, selector, row_map, col_map, cells,
    state, cell_forcing, pair_coef, order, rank,
    field, total, packs, rows, got_packs, got_rows, send, recv,
):
    g, c, up, down, left, right = neighbours()
    barrier = pltpu.get_barrier_semaphore()
    around = [(up, c), (down, c)]
    around += [(r, s) for s in (left, right) for r in (g, up, down)]
    for to in around:
        pl.semaphore_signal(barrier, inc=1, device_id=to, device_id_type=MESH)

    def first(i, _):
        for half in range(2):
            t = tendency(
                chunk_of(tracer, i, half), chunk_of(wind_x, i, half), chunk_of(wind_y, i, half), table
            )
            field[pl.ds(pl.multiple_of(half * PTS + i * 64, 64), 64), :] = t.reshape(64, 128)
        return 0

    lax.fori_loop(0, 9, first, 0)
    pack_edges(field, packs.at[0], rows.at[0])
    pl.semaphore_wait(barrier, 8)
    copies = halo_copies(packs.at[0], rows.at[0], got_packs.at[0], got_rows.at[0], send.at[0], recv.at[0])
    for copy in copies:
        copy.start()

    pair_coef[0:33, :] = jnp.dot(
        collision[...], selector[...], preferred_element_type=F32
    ).astype(BF)
    pair_coef[33:48, :] = jnp.zeros((15, PAIRS), BF)
    across = jnp.broadcast_to(counts[...], (COLS, COLS)).astype(F32)
    i0 = lax.broadcasted_iota(jnp.int32, (COLS, COLS), 0)
    i1 = lax.broadcasted_iota(jnp.int32, (COLS, COLS), 1)
    along = jnp.sum(jnp.where(i0 == i1, across, 0.0), axis=1, keepdims=True)
    before = (across > along) | ((across == along) & (i1 < i0))
    place = jnp.sum(jnp.where(before, 1.0, 0.0), axis=1, keepdims=True)
    place = jnp.broadcast_to(place, (COLS, COLS)).astype(jnp.int32)
    rank[...] = place
    listed = jnp.sum(jnp.where(place == i1, i0.astype(F32), 0.0), axis=0, keepdims=True)
    order[...] = listed.astype(jnp.int32)

    for copy in copies:
        copy.wait()

    def second(i, half, mean):
        at = pl.multiple_of(half * PTS + i * 64, 64)
        moved = chunk_of(tracer, i, half) + DT_DYN * mean
        state[pl.ds(i * 8, 8), :, half * 128 : (half + 1) * 128] = moved
        total[pl.ds(at, 64), :] = mean.reshape(64, 128)
        t = tendency(moved, chunk_of(wind_x, i, half), chunk_of(wind_y, i, half), table)
        field[pl.ds(at, 64), :] = t.reshape(64, 128)

    assemble_loop(field, got_packs.at[0], got_rows.at[0], second)
    pack_edges(field, packs.at[1], rows.at[1])
    copies = halo_copies(packs.at[1], rows.at[1], got_packs.at[1], got_rows.at[1], send.at[1], recv.at[1])
    for copy in copies:
        copy.start()
    for copy in copies:
        copy.wait()

    def third(i, half, mean):
        at = pl.multiple_of(half * PTS + i * 64, 64)
        state[pl.ds(i * 8, 8), :, half * 128 : (half + 1) * 128] = (
            chunk_of(state, i, half) + DT_DYN * mean
        )
        total[pl.ds(at, 64), :] = total[pl.ds(at, 64), :] + mean.reshape(64, 128)

    assemble_loop(field, got_packs.at[1], got_rows.at[1], third)
    parts = [
        jnp.dot(row_map[...], total[half * PTS : (half + 1) * PTS, :], precision=HIGH, preferred_element_type=F32)
        for half in range(2)
    ]
    by_row = jnp.concatenate(parts, axis=1)
    for e in range(2):
        forcing = lax.dot_general(
            col_map[...], by_row[16 * e : 16 * (e + 1)], (((1,), (1,)), ((), ())),
            precision=HIGH, preferred_element_type=F32,
        ).astype(BF)
        cell_forcing[64 * e : 64 * (e + 1), :] = DT_CRM * jnp.dot(
            forcing, cells[...], preferred_element_type=F32
        )


def dynamics(tracer, wind_x, wind_y, counts_row, collision):
    row_map, col_map = forcing_tables()
    shape = tracer.shape
    return pl.pallas_call(
        dynamics_kernel,
        out_shape=(
            jax.ShapeDtypeStruct(shape, F32),
            jax.ShapeDtypeStruct((COLS, 256), F32),
            jax.ShapeDtypeStruct((48, PAIRS), BF),
            jax.ShapeDtypeStruct((1, COLS), jnp.int32),
            jax.ShapeDtypeStruct((COLS, COLS), jnp.int32),
        ),
        in_specs=[VMEM] * 10,
        out_specs=(VMEM,) * 5,
        scratch_shapes=[
            pltpu.VMEM((2 * PTS, 128), F32),
            pltpu.VMEM((2 * PTS, 128), F32),
            pltpu.VMEM((2, 2, 8, 128), F32),
            pltpu.VMEM((2, 2, 2 * LEV, 128), F32),
            pltpu.VMEM((2, 6, 8, 128), F32),
            pltpu.VMEM((2, 2, 2 * LEV, 128), F32),
            pltpu.SemaphoreType.DMA((2, 8)),
            pltpu.SemaphoreType.DMA((2, 8)),
        ],
        compiler_params=pltpu.CompilerParams(
            collective_id=0, has_side_effects=True, vmem_limit_bytes=40 << 20
        ),
        name="dynamics",
    )(
        tracer, wind_x, wind_y, counts_row, collision,
        jnp.asarray(stencil_table()), jnp.asarray(pair_selector()),
        jnp.asarray(row_map), jnp.asarray(col_map), jnp.asarray(spread_cells()),
    )


def micro_kernel(
    order, counts, drops, cell_forcing, pair_coef, growth, group, rank,
    drops_next, heat_out, echo_out,
    cloud, doubled, grow, heat_rows, echo_rows,
):
    mass = (lax.broadcasted_iota(jnp.int32, (40, 128), 0).astype(F32) + 1.0) / BINS
    srow = lax.broadcasted_iota(jnp.int32, (8, 128), 0)

    def substep(s, p):
        for b in range(BATCH):
            active = s < counts[order[0, p * BATCH + b]]
            blocks, grown, olds = [], [], []
            for half in range(2):
                old = cloud[b, half]
                now = old + grow[b, half]
                doubled[b, half, 0:32, :] = now[0:32]
                doubled[b, half, 32:48, :] = now[0:16]
                near, far = [], []
                for d in range(8):
                    shifted = doubled[b, half, d : d + 40, :]
                    near.append((now[0:32] * shifted[0:32]).astype(BF))
                    far.append((now[0:32] * shifted[8:40]).astype(BF))
                last = jnp.broadcast_to(now[32:33], (32, 128))
                rest = [
                    (now[0:16] * now[16:32]).astype(BF),
                    (now[0:32] * last).astype(BF),
                    (last[0:16] * last[0:16]).astype(BF),
                ]
                blocks.append(jnp.concatenate(near + far + rest, axis=0))
                grown.append(now)
                olds.append(old)
            change = jnp.dot(
                pair_coef[...], jnp.concatenate(blocks, axis=1), preferred_element_type=F32
            )
            for half in range(2):
                moved = grown[half] + DT_CRM * change[0:40, half * 128 : (half + 1) * 128]
                cloud[b, half] = jnp.where(active, moved, olds[half])
        return p

    def batch(p, _):
        for b in range(BATCH):
            col = order[0, p * BATCH + b]
            forced = cell_forcing[pl.ds(col, 1), :]
            for half in range(2):
                at = slice(half * 128, (half + 1) * 128)
                cloud[b, half, 0:32, :] = drops[col, 0:32, at].astype(F32)
                cloud[b, half, 32:40, :] = jnp.broadcast_to(drops[col, 32:33, at].astype(F32), (8, 128))
                grow[b, half] = forced[:, at] * growth[...]
        lax.fori_loop(0, counts[order[0, p * BATCH]], substep, p)
        heats = [jnp.zeros((8, 128), F32)] * 2
        echos = [jnp.zeros((8, 128), F32)] * 2
        for b in range(BATCH):
            col = order[0, p * BATCH + b]
            for half in range(2):
                at = slice(half * 128, (half + 1) * 128)
                final = cloud[b, half]
                drops_next[col, 0:32, at] = final[0:32].astype(BF)
                drops_next[col, 32:33, at] = final[32:33].astype(BF)
                gain = (final[0:32] - drops[col, 0:32, at].astype(F32)) * mass[0:32]
                gain_last = (final[32:33] - drops[col, 32:33, at].astype(F32)) * mass[32:33]
                weighed = final * mass
                square = weighed * weighed
                heats[half] = jnp.where(
                    srow == b, jnp.sum(gain, axis=0, keepdims=True) + gain_last, heats[half]
                )
                echos[half] = jnp.where(
                    srow == b, jnp.sum(square[0:32], axis=0, keepdims=True) + square[32:33], echos[half]
                )
        for half in range(2):
            at = slice(half * 128, (half + 1) * 128)
            heat_rows[p, :, at] = heats[half]
            echo_rows[p, :, at] = echos[half]
        return 0

    lax.fori_loop(0, COLS // BATCH, batch, 0)
    total = COLS // BATCH * 8
    q = lax.broadcasted_iota(jnp.int32, (COLS, total), 1)
    pick = ((q // 8 * BATCH + q % 8 == rank[:, 0:1]) & (q % 8 < BATCH)).astype(F32).astype(BF)

    def group_mean(x):
        acc = None
        for part in split3(x):
            y = jnp.dot(part, group[...], preferred_element_type=F32)
            acc = y if acc is None else acc + y
        return acc

    heat = group_mean(heat_rows[...].reshape(total, 256)).astype(BF)
    heat_out[...] = jnp.dot(pick, heat, preferred_element_type=F32).astype(BF)
    echo_out[...] = jnp.log(1.0 + dot_exact(pick, group_mean(echo_rows[...].reshape(total, 256))))


def microphysics(order, counts, drops, cell_forcing, pair_coef, growth, rank):
    return pl.pallas_call(
        micro_kernel,
        out_shape=(
            jax.ShapeDtypeStruct(drops.shape, BF),
            jax.ShapeDtypeStruct((COLS, 128), BF),
            jax.ShapeDtypeStruct((COLS, 128), F32),
        ),
        in_specs=[SMEM, SMEM] + [VMEM] * 6,
        out_specs=(VMEM,) * 3,
        scratch_shapes=[
            pltpu.VMEM((BATCH, 2, 40, 128), F32),
            pltpu.VMEM((BATCH, 2, 48, 128), F32),
            pltpu.VMEM((BATCH, 2, 40, 128), F32),
            pltpu.VMEM((COLS // BATCH, 8, 256), F32),
            pltpu.VMEM((COLS // BATCH, 8, 256), F32),
        ],
        compiler_params=pltpu.CompilerParams(vmem_limit_bytes=40 << 20),
        name="microphysics",
    )(order, counts, drops, cell_forcing, pair_coef, growth, jnp.asarray(group_matrix()), rank)


def coupling_kernel(
    state, heat, echo, owner, heating, spread, slots,
    tracer_next, power,
    field, packs, rows, got_packs, got_rows, sent, first_in, second_out, second_in,
    send, recv, send1, recv1, send2, recv2,
):
    g, c, up, down, left, right = neighbours()
    barrier = pltpu.get_barrier_semaphore()
    peers = [(lax.rem(g + k, NG), c) for k in range(1, NG)]
    peers += [(g, lax.rem(c + k, NC)) for k in range(1, NC)]
    peers += [(r, s) for s in (left, right) for r in (up, down)]
    for to in peers:
        pl.semaphore_signal(barrier, inc=1, device_id=to, device_id_type=MESH)

    warm = []
    for e in range(2):
        turned = heat[64 * e : 64 * (e + 1), :].astype(F32).T.astype(BF)[0:16]
        warm.append(jnp.dot(turned, spread[...], preferred_element_type=F32).astype(BF))
    warm = jnp.concatenate(warm + warm, axis=0)
    for half in range(2):
        at = slice(half * 128, (half + 1) * 128)
        back = jnp.dot(heating[...], warm[:, at], preferred_element_type=F32)
        field[half * PTS : (half + 1) * PTS, :] = back + state[:, :, at].reshape(PTS, 128)
    pack_edges(field, packs, rows)
    pl.semaphore_wait(barrier, len(peers))
    copies = halo_copies(packs, rows, got_packs, got_rows, send, recv)
    for copy in copies:
        copy.start()

    across = jnp.broadcast_to(owner[...], (COLS, COLS))
    i0 = lax.broadcasted_iota(jnp.int32, (COLS, COLS), 0)
    i1 = lax.broadcasted_iota(jnp.int32, (COLS, COLS), 1)
    along = jnp.sum(jnp.where(i0 == i1, across.astype(F32), 0.0), axis=1, keepdims=True)
    earlier = (along == across.astype(F32)) & (i0 < i1)
    turn = jnp.sum(jnp.where(earlier, 1.0, 0.0), axis=0, keepdims=True)
    key = across % NC * NG + across // NC
    onehot = jnp.concatenate(
        [jnp.where((key == i0) & (turn == float(r)), 1.0, 0.0) for r in range(2)], axis=1
    ).astype(BF)
    sums = echo[...]
    sums = jnp.concatenate([sums, pltpu.roll(sums, 16, 1)], axis=0)
    sent[...] = dot_exact(onehot, sums).reshape(NC, NG, 128)
    first = []
    for k in range(1, NC):
        to = lax.rem(c + k, NC)
        copy = pltpu.make_async_remote_copy(
            src_ref=sent.at[to],
            dst_ref=first_in.at[c],
            send_sem=send1.at[k],
            recv_sem=recv1.at[c],
            device_id=(g, to),
            device_id_type=MESH,
        )
        copy.start()
        first.append(copy)
    first_in[c] = sent[c]

    for copy in copies:
        copy.wait()

    def last(i, half, mean):
        tracer_next[pl.ds(i * 8, 8), :, half * 128 : (half + 1) * 128] = mean

    assemble_loop(field, got_packs, got_rows, last)

    for k, copy in enumerate(first, 1):
        copy.wait_send()
        source = lax.rem(c + k, NC)
        pltpu.make_async_remote_copy(
            src_ref=sent.at[source],
            dst_ref=first_in.at[source],
            send_sem=send1.at[k],
            recv_sem=recv1.at[source],
            device_id=(g, source),
            device_id_type=MESH,
        ).wait_recv()
    every = first_in[...]
    for to in range(NG):
        second_out[to] = every[:, to, :]
    second = []
    for k in range(1, NG):
        to = lax.rem(g + k, NG)
        copy = pltpu.make_async_remote_copy(
            src_ref=second_out.at[to],
            dst_ref=second_in.at[g],
            send_sem=send2.at[k],
            recv_sem=recv2.at[g],
            device_id=(to, c),
            device_id_type=MESH,
        )
        copy.start()
        second.append(copy)
    second_in[g] = second_out[g]
    for k, copy in enumerate(second, 1):
        copy.wait_send()
        source = lax.rem(g + k, NG)
        pltpu.make_async_remote_copy(
            src_ref=second_out.at[source],
            dst_ref=second_in.at[source],
            send_sem=send2.at[k],
            recv_sem=recv2.at[source],
            device_id=(source, c),
            device_id_type=MESH,
        ).wait_recv()
    turned = second_in[...].reshape(COLS, 128).T
    turned = jnp.concatenate([turned[0:16], turned[16:32]], axis=1)
    acc = None
    for part in split3(turned):
        y = jnp.dot(part, slots[...], preferred_element_type=F32)
        acc = y if acc is None else acc + y
    power[...] = acc


def coupling(state, heat, echo, owner_row):
    return pl.pallas_call(
        coupling_kernel,
        out_shape=(
            jax.ShapeDtypeStruct(state.shape, F32),
            jax.ShapeDtypeStruct((CLEV, 256), F32),
        ),
        in_specs=[VMEM] * 7,
        out_specs=(VMEM,) * 2,
        scratch_shapes=[
            pltpu.VMEM((2 * PTS, 128), F32),
            pltpu.VMEM((2, 8, 128), F32),
            pltpu.VMEM((2, 2 * LEV, 128), F32),
            pltpu.VMEM((6, 8, 128), F32),
            pltpu.VMEM((2, 2 * LEV, 128), F32),
            pltpu.VMEM((NC, NG, 128), F32),
            pltpu.VMEM((NC, NG, 128), F32),
            pltpu.VMEM((NG, NC, 128), F32),
            pltpu.VMEM((NG, NC, 128), F32),
            pltpu.SemaphoreType.DMA((8,)),
            pltpu.SemaphoreType.DMA((8,)),
            pltpu.SemaphoreType.DMA((NC,)),
            pltpu.SemaphoreType.DMA((NC,)),
            pltpu.SemaphoreType.DMA((NG,)),
            pltpu.SemaphoreType.DMA((NG,)),
        ],
        compiler_params=pltpu.CompilerParams(
            collective_id=1, has_side_effects=True, vmem_limit_bytes=40 << 20
        ),
        name="coupling",
    )(
        state, heat, echo, owner_row,
        jnp.asarray(heating_table()), jnp.asarray(spread_columns()), jnp.asarray(slot_table()),
    )


def shards(tracer, wind_x, wind_y, drops, owner, counts, collision, growth):
    state, cell_forcing, pair_coef, order, rank = dynamics(
        tracer, wind_x, wind_y, counts.reshape(1, COLS), collision
    )
    column = jnp.broadcast_to(jnp.pad(growth, (0, 7))[:, None], (40, 128))
    drops_next, heat, echo = microphysics(
        order, counts, drops, cell_forcing, pair_coef, column, rank
    )
    tracer_next, power = coupling(state, heat, echo, owner.reshape(1, COLS))
    return (tracer_next, drops_next, power)


def solution(mesh):
    return jax.shard_map(
        shards,
        mesh=mesh,
        in_specs=(
            P(None, "gcm", "crm"),
            P(None, "gcm", "crm"),
            P(None, "gcm", "crm"),
            P(("gcm", "crm"), None, None),
            P(("gcm", "crm"), None),
            P(("gcm", "crm")),
            P(),
            P(),
        ),
        out_specs=(P(None, "gcm", "crm"), P(("gcm", "crm"), None, None), P(None, ("gcm", "crm"))),
        check_vma=False,
    )
```

```python
import functools

import jax
import jax.numpy as jnp
import ml_dtypes
import numpy as np
from jax import lax
from jax.experimental import pallas as pl
from jax.experimental.pallas import tpu as pltpu
from jax.sharding import PartitionSpec as P

BF = jnp.bfloat16
F32 = jnp.float32
MESH = pl.DeviceIdType.MESH
HIGH = lax.Precision.HIGHEST
VMEM = pl.BlockSpec(memory_space=pltpu.VMEM)
SMEM = pl.BlockSpec(memory_space=pltpu.SMEM)
HBM = pl.BlockSpec(memory_space=pltpu.HBM)

NG = 8
NC = 16
LEV = 72
BINS = 33
CLEV = 16
COLS = 128
PTS = LEV * 8
PAIRS = 576
DT_DYN = 0.04
DT_CRM = 0.05
DT_PHYS = 0.5
BATCH = 16
ROWS = 40


def gll_tables():
    inv_root = 1.0 / np.sqrt(5.0)
    gll_nodes = np.array([-1.0, -inv_root, inv_root, 1.0])
    weights = np.array([1.0, 5.0, 5.0, 1.0]) / 6.0
    legendre = (5.0 * gll_nodes**3 - 3.0 * gll_nodes) / 2.0
    derivative = np.zeros((4, 4))
    for i in range(4):
        for j in range(4):
            if i != j:
                derivative[i, j] = legendre[i] / (legendre[j] * (gll_nodes[i] - gll_nodes[j]))
    derivative[0, 0] = -3.0
    derivative[3, 3] = 3.0
    return (2.0 * derivative, weights)


def level_tables(levels, crm_levels):
    spacing = levels / crm_levels
    centres = (np.arange(crm_levels) + 0.5) * spacing - 0.5
    hats = np.maximum(0.0, 1.0 - np.abs(np.arange(levels)[None, :] - centres[:, None]) / spacing)
    down_map = hats / hats.sum(axis=1, keepdims=True)
    up_map = hats.T / hats.T.sum(axis=1, keepdims=True)
    return (down_map, up_map)


def stencil_table():
    derivative, _ = gll_tables()
    out = np.zeros((14, 8, 128), np.float32)
    for s in range(-3, 4):
        for i in range(4):
            if 0 <= i + s < 4:
                out[s + 3, i::4, :] = -derivative[i, i + s]
                out[s + 10, :, i::4] = -derivative[i, i + s]
    return out


def forcing_tables():
    _, weights = gll_tables()
    down_map, _ = level_tables(LEV, CLEV)
    rows = np.zeros((2, CLEV, LEV, 8))
    for r in range(8):
        rows[r // 4, :, :, r] = down_map * weights[r % 4] / 2.0 * 0.5
    cols = np.zeros((64, 256))
    for c in range(256):
        cols[c // 4, c] = weights[c % 4] / 2.0
    return rows.reshape(32, PTS).astype(np.float32), cols.astype(np.float32)


def spread_cells():
    out = np.zeros((CLEV, 256), np.float32)
    for c in range(256):
        out[c // 16, c] = 1.0
    return out.astype(ml_dtypes.bfloat16)


def group_matrix():
    out = np.zeros((256, 128), np.float32)
    for c in range(256):
        out[c, c // 16] = 1.0 / 16.0
    return out.astype(ml_dtypes.bfloat16)


def heating_table():
    _, up_map = level_tables(LEV, CLEV)
    half = (DT_PHYS * up_map).astype(np.float32)
    first = half.astype(ml_dtypes.bfloat16)
    second = (half - first.astype(np.float32)).astype(ml_dtypes.bfloat16)
    out = np.zeros((LEV, 8, 2, 2, CLEV), ml_dtypes.bfloat16)
    for r in range(8):
        out[:, r, 0, r // 4, :] = first
        out[:, r, 1, r // 4, :] = second
    return out.reshape(PTS, 64)


def spread_columns():
    out = np.zeros((64, 256), np.float32)
    for c in range(256):
        out[c // 4, c] = 1.0
    return out.astype(ml_dtypes.bfloat16)


def slot_table():
    out = np.zeros((2, 128, 256), np.float32)
    for d in range(128):
        for r in range(2):
            out[r, d, 2 * d + r] = 1.0
    return out.reshape(256, 256).astype(ml_dtypes.bfloat16)


def pair_list():
    out = []
    for d in range(16):
        for i in range(32):
            out.append((i, (i + d) % 32))
    for i in range(16):
        out.append((i, i + 16))
    for i in range(32):
        out.append((i, 32))
    out.append((32, 32))
    return out


def pair_selector():
    out = np.zeros((BINS * BINS, PAIRS), np.float32)
    for q, (i, j) in enumerate(pair_list()):
        out[i * BINS + j, q] = 1.0
        out[j * BINS + i, q] = 1.0
    return out.astype(ml_dtypes.bfloat16)


def split3(x):
    hi = x.astype(BF)
    rest = x - hi.astype(F32)
    mid = rest.astype(BF)
    return hi, mid, (rest - mid.astype(F32)).astype(BF)


def dot_exact(onehot, x):
    acc = None
    for part in split3(x):
        y = jnp.dot(onehot, part, preferred_element_type=F32)
        acc = y if acc is None else acc + y
    return acc


def tendency(q, wind_x, wind_y, table):
    grad_x = table[3][None] * q
    grad_y = table[10][None] * q
    for s in (-3, -2, -1, 1, 2, 3):
        grad_x = grad_x + table[s + 3][None] * pltpu.roll(q, (-s) % 8, 1)
        grad_y = grad_y + table[s + 10][None] * pltpu.roll(q, (-s) % 128, 2)
    return wind_x * grad_x + wind_y * grad_y


def neighbours():
    g = lax.axis_index("gcm")
    c = lax.axis_index("crm")
    up, down = lax.rem(g + NG - 1, NG), lax.rem(g + 1, NG)
    left, right = lax.rem(c + NC - 1, NC), lax.rem(c + 1, NC)
    return g, c, up, down, left, right


def pack_edges(field, packs, rows):
    lane = lax.broadcasted_iota(jnp.int32, (8, 128), 1)

    def one(i, carry):
        low, high = carry
        low, high = pltpu.roll(low, 120, 1), pltpu.roll(high, 120, 1)
        for k in range(8):
            at = pl.multiple_of(i * 64, 64) + 8 * k
            first, last = field[pl.ds(at, 8), :], field[pl.ds(PTS + at, 8), :]
            both = pltpu.roll(jnp.where(lane == 0, first, last), k + 1, 1)
            high = jnp.where(lane == k, both, high)
            low = jnp.where(lane == k + 1, both, low)
        return low, high

    zero = jnp.zeros((8, 128), F32)
    low, high = lax.fori_loop(0, 9, one, (zero, zero))
    packs[0] = pltpu.roll(low, 63, 1)
    packs[1] = pltpu.roll(high, 64, 1)
    for half in range(2):
        rows[0, half * LEV : (half + 1) * LEV, :] = field[pl.ds(half * PTS, LEV, stride=8), :]
        rows[1, half * LEV : (half + 1) * LEV, :] = field[pl.ds(half * PTS + 7, LEV, stride=8), :]


def halo_copies(packs, rows, got_packs, got_rows, send, recv):
    g, c, up, down, left, right = neighbours()
    plan = [
        (rows.at[1], got_rows.at[0], (down, c)),
        (rows.at[0], got_rows.at[1], (up, c)),
        (packs.at[1], got_packs.at[0], (g, right)),
        (packs.at[1], got_packs.at[1], (down, right)),
        (packs.at[1], got_packs.at[2], (up, right)),
        (packs.at[0], got_packs.at[3], (g, left)),
        (packs.at[0], got_packs.at[4], (down, left)),
        (packs.at[0], got_packs.at[5], (up, left)),
    ]
    return [
        pltpu.make_async_remote_copy(
            src_ref=src,
            dst_ref=dst,
            send_sem=send.at[n],
            recv_sem=recv.at[n],
            device_id=to,
            device_id_type=MESH,
        )
        for n, (src, dst, to) in enumerate(plan)
    ]


def assemble_loop(field, got_packs, got_rows, use):
    row = lax.broadcasted_iota(jnp.int32, (8, 128), 0)
    lane = lax.broadcasted_iota(jnp.int32, (8, 128), 1)

    def row_mean(x, above, below):
        up = jnp.where(row == 0, pltpu.roll(above, 1, 0), pltpu.roll(x, 1, 0))
        down = jnp.where(row == 7, pltpu.roll(below, 7, 0), pltpu.roll(x, 7, 0))
        other = jnp.where(row % 4 == 3, down, jnp.where(row % 4 == 0, up, x))
        return 0.5 * (x + other)

    left_halo = row_mean(got_packs[0], got_packs[1], got_packs[2])
    right_halo = row_mean(got_packs[3], got_packs[4], got_packs[5])
    edge_row = ((row == 0) | (row == 7))[None]
    upper = (row < 4)[None]
    is3, is4 = (row == 3)[None], (row == 4)[None]
    lane3, lane0 = (lane % 4 == 3)[None], (lane % 4 == 0)[None]
    first, last = (lane == 0)[None], (lane == 127)[None]

    def one(i, carry):
        left_c, right_c = carry
        means = []
        for half in range(2):
            at = pl.multiple_of(half * PTS + i * 64, 64)
            x = field[pl.ds(at, 64), :].reshape(8, 8, 128)
            lev = pl.multiple_of(half * LEV + i * 8, 8)
            above = jnp.broadcast_to(got_rows[0, pl.ds(lev, 8), :][:, None, :], (8, 8, 128))
            below = jnp.broadcast_to(got_rows[1, pl.ds(lev, 8), :][:, None, :], (8, 8, 128))
            other = jnp.where(is3, pltpu.roll(x, 7, 1), jnp.where(is4, pltpu.roll(x, 1, 1), x))
            other = jnp.where(edge_row, jnp.where(upper, above, below), other)
            means.append(0.5 * (x + other))
        lefts = [pltpu.roll(m, 1, 2) for m in means]
        rights = [pltpu.roll(m, 127, 2) for m in means]
        halo_l = jnp.stack([pltpu.roll(left_c, (128 - k) % 128, 1) if k else left_c for k in range(8)])
        halo_r = jnp.stack([pltpu.roll(right_c, 127 - k, 1) for k in range(8)])
        near_l = [jnp.where(first, halo_l, lefts[0]), jnp.where(first, lefts[0], lefts[1])]
        near_r = [jnp.where(last, rights[1], rights[0]), jnp.where(last, halo_r, rights[1])]
        for half in range(2):
            m = means[half]
            other = jnp.where(lane3, near_r[half], jnp.where(lane0, near_l[half], m))
            use(i, half, 0.5 * (m + other))
        return pltpu.roll(left_c, 120, 1), pltpu.roll(right_c, 120, 1)

    lax.fori_loop(0, 9, one, (left_halo, right_halo))


def chunk_of(ref, i, half):
    return ref[pl.ds(i * 8, 8), :, half * 128 : (half + 1) * 128]


def dynamics_kernel(
    tracer_h, wind_x_h, wind_y_h, drops_h, counts_h, growth_h, collision_h, table_h, selector_h,
    row_map_h, col_map_h, cells_h,
    state, cell_forcing, pair_coef, growth_col, start, counts_out, unsort,
    tracer, wind_x, wind_y, drops, counts, growth, collision, table, selector, row_map, col_map, cells,
    loads, field, total, packs, rows, got_packs, got_rows, send, recv,
):
    g, c, up, down, left, right = neighbours()
    barrier = pltpu.get_barrier_semaphore()
    around = [(up, c), (down, c)]
    around += [(r, s) for s in (left, right) for r in (g, up, down)]
    sources = [table_h, tracer_h, wind_x_h, wind_y_h, counts_h, growth_h, collision_h, selector_h, drops_h,
               row_map_h, col_map_h, cells_h]
    targets = [table, tracer, wind_x, wind_y, counts, growth, collision, selector, drops,
               row_map, col_map, cells]
    fetch = [
        pltpu.make_async_copy(source, target, loads.at[n])
        for n, (source, target) in enumerate(zip(sources, targets))
    ]
    for copy in fetch:
        copy.start()
    for to in around:
        pl.semaphore_signal(barrier, inc=1, device_id=to, device_id_type=MESH)
    for copy in fetch[0:4]:
        copy.wait()

    def first(i, _):
        for half in range(2):
            t = tendency(
                chunk_of(tracer, i, half), chunk_of(wind_x, i, half), chunk_of(wind_y, i, half), table
            )
            field[pl.ds(pl.multiple_of(half * PTS + i * 64, 64), 64), :] = t.reshape(64, 128)
        return 0

    lax.fori_loop(0, 9, first, 0)
    pack_edges(field, packs.at[0], rows.at[0])
    pl.semaphore_wait(barrier, 8)
    copies = halo_copies(packs.at[0], rows.at[0], got_packs.at[0], got_rows.at[0], send.at[0], recv.at[0])
    for copy in copies:
        copy.start()

    for copy in fetch[4:]:
        copy.wait()
    pair_coef[0:33, :] = jnp.dot(
        collision[...], selector[...], preferred_element_type=F32
    ).astype(BF)
    pair_coef[33:48, :] = jnp.zeros((15, PAIRS), BF)
    i0 = lax.broadcasted_iota(jnp.int32, (COLS, COLS), 0)
    i1 = lax.broadcasted_iota(jnp.int32, (COLS, COLS), 1)
    wide = jnp.concatenate([growth[...], jnp.zeros((1, COLS - BINS), F32)], axis=1)
    growth_col[...] = jnp.broadcast_to(
        jnp.sum(
            jnp.where((i0 == i1)[0:ROWS], jnp.broadcast_to(wide, (ROWS, COLS)), 0.0), axis=1, keepdims=True
        ),
        (ROWS, COLS),
    )
    across = jnp.broadcast_to(counts[...], (COLS, COLS)).astype(F32)
    along = jnp.sum(jnp.where(i0 == i1, across, 0.0), axis=1, keepdims=True)
    before = (across > along) | ((across == along) & (i1 < i0))
    place = jnp.sum(jnp.where(before, 1.0, 0.0), axis=1, keepdims=True).astype(jnp.int32)
    after = (along > across) | ((along == across) & (i0 < i1))
    place_row = jnp.sum(jnp.where(after, 1.0, 0.0), axis=0, keepdims=True).astype(jnp.int32)
    counts_out[...] = jnp.sum(jnp.where(place == i1, along, 0.0), axis=0, keepdims=True).astype(jnp.int32)
    unsort[...] = jnp.where(place == i1, 1.0, 0.0).astype(BF)
    sort = jnp.where(place_row == i0, 1.0, 0.0).astype(BF)
    for b in range(BINS):
        sorted_bin = jnp.dot(sort, drops[b], preferred_element_type=F32)
        for half in range(2):
            start[pl.ds(half * COLS * ROWS + b, COLS, stride=ROWS), :] = sorted_bin[
                :, half * 128 : (half + 1) * 128
            ]

    for copy in copies:
        copy.wait()

    def second(i, half, mean):
        at = pl.multiple_of(half * PTS + i * 64, 64)
        moved = chunk_of(tracer, i, half) + DT_DYN * mean
        state[pl.ds(i * 8, 8), :, half * 128 : (half + 1) * 128] = moved
        total[pl.ds(at, 64), :] = mean.reshape(64, 128)
        t = tendency(moved, chunk_of(wind_x, i, half), chunk_of(wind_y, i, half), table)
        field[pl.ds(at, 64), :] = t.reshape(64, 128)

    assemble_loop(field, got_packs.at[0], got_rows.at[0], second)
    pack_edges(field, packs.at[1], rows.at[1])
    copies = halo_copies(packs.at[1], rows.at[1], got_packs.at[1], got_rows.at[1], send.at[1], recv.at[1])
    for copy in copies:
        copy.start()
    for copy in copies:
        copy.wait()

    def third(i, half, mean):
        at = pl.multiple_of(half * PTS + i * 64, 64)
        state[pl.ds(i * 8, 8), :, half * 128 : (half + 1) * 128] = (
            chunk_of(state, i, half) + DT_DYN * mean
        )
        total[pl.ds(at, 64), :] = total[pl.ds(at, 64), :] + mean.reshape(64, 128)

    assemble_loop(field, got_packs.at[1], got_rows.at[1], third)
    parts = [
        jnp.dot(row_map[...], total[half * PTS : (half + 1) * PTS, :], precision=HIGH, preferred_element_type=F32)
        for half in range(2)
    ]
    by_row = jnp.concatenate(parts, axis=1)
    forcing = [
        lax.dot_general(
            col_map[...], by_row[16 * e : 16 * (e + 1)], (((1,), (1,)), ((), ())),
            precision=HIGH, preferred_element_type=F32,
        ).astype(BF)
        for e in range(2)
    ]
    by_cell = jnp.dot(
        jnp.concatenate(forcing, axis=0), cells[...], preferred_element_type=F32
    ).astype(BF)
    cell_forcing[...] = DT_CRM * jnp.dot(sort, by_cell, preferred_element_type=F32)


def dynamics(tracer, wind_x, wind_y, drops, counts_row, growth_row, collision):
    row_map, col_map = forcing_tables()
    shape = tracer.shape
    operands = (
        tracer, wind_x, wind_y, drops, counts_row, growth_row, collision,
        jnp.asarray(stencil_table()), jnp.asarray(pair_selector()),
        jnp.asarray(row_map), jnp.asarray(col_map), jnp.asarray(spread_cells()),
    )
    return pl.pallas_call(
        dynamics_kernel,
        out_shape=(
            jax.ShapeDtypeStruct(shape, F32),
            jax.ShapeDtypeStruct((COLS, 256), F32),
            jax.ShapeDtypeStruct((48, PAIRS), BF),
            jax.ShapeDtypeStruct((ROWS, 128), F32),
            jax.ShapeDtypeStruct((2 * COLS * ROWS, 128), F32),
            jax.ShapeDtypeStruct((1, COLS), jnp.int32),
            jax.ShapeDtypeStruct((COLS, COLS), BF),
        ),
        in_specs=[HBM] * 12,
        out_specs=(VMEM,) * 7,
        scratch_shapes=[pltpu.VMEM(x.shape, x.dtype) for x in operands]
        + [
            pltpu.SemaphoreType.DMA((12,)),
            pltpu.VMEM((2 * PTS, 128), F32),
            pltpu.VMEM((2 * PTS, 128), F32),
            pltpu.VMEM((2, 2, 8, 128), F32),
            pltpu.VMEM((2, 2, 2 * LEV, 128), F32),
            pltpu.VMEM((2, 6, 8, 128), F32),
            pltpu.VMEM((2, 2, 2 * LEV, 128), F32),
            pltpu.SemaphoreType.DMA((2, 8)),
            pltpu.SemaphoreType.DMA((2, 8)),
        ],
        compiler_params=pltpu.CompilerParams(
            collective_id=0, has_side_effects=True, vmem_limit_bytes=40 << 20
        ),
        name="dynamics",
    )(*operands)


def micro_kernel(
    counts, start, cell_forcing, pair_coef, growth, group, unsort,
    drops_next, heat_out, echo_out,
    cloud, doubled, grow, heat_rows, echo_rows,
):
    mass = (lax.broadcasted_iota(jnp.int32, (ROWS, 128), 0).astype(F32) + 1.0) / BINS
    srow = lax.broadcasted_iota(jnp.int32, (8, 128), 0)

    def place(p, b, half):
        return pl.ds(pl.multiple_of((half * COLS + p * BATCH + b) * ROWS, 8), ROWS)

    def substep(s, p):
        for b in range(BATCH):
            active = s < counts[0, p * BATCH + b]
            blocks, grown, olds = [], [], []
            for half in range(2):
                old = cloud[place(p, b, half), :]
                now = old + grow[b, half]
                doubled[b, half, 0:32, :] = now[0:32]
                doubled[b, half, 32:48, :] = now[0:16]
                near, far = [], []
                for d in range(8):
                    shifted = doubled[b, half, d : d + 40, :]
                    near.append((now[0:32] * shifted[0:32]).astype(BF))
                    far.append((now[0:32] * shifted[8:40]).astype(BF))
                last = jnp.broadcast_to(now[32:33], (32, 128))
                rest = [
                    (now[0:16] * now[16:32]).astype(BF),
                    (now[0:32] * last).astype(BF),
                    (last[0:16] * last[0:16]).astype(BF),
                ]
                blocks.append(jnp.concatenate(near + far + rest, axis=0))
                grown.append(now)
                olds.append(old)
            change = jnp.dot(
                pair_coef[...], jnp.concatenate(blocks, axis=1), preferred_element_type=F32
            )
            for half in range(2):
                moved = grown[half] + DT_CRM * change[0:ROWS, half * 128 : (half + 1) * 128]
                cloud[place(p, b, half), :] = jnp.where(active, moved, olds[half])
        return p

    def batch(p, _):
        for b in range(BATCH):
            forced = cell_forcing[pl.ds(p * BATCH + b, 1), :]
            for half in range(2):
                cloud[place(p, b, half), :] = start[place(p, b, half), :]
                grow[b, half] = forced[:, half * 128 : (half + 1) * 128] * growth[...]
        lax.fori_loop(0, counts[0, p * BATCH], substep, p)
        for half in range(2):
            at = slice(half * 128, (half + 1) * 128)
            for eight in range(BATCH // 8):
                heats = jnp.zeros((8, 128), F32)
                echos = jnp.zeros((8, 128), F32)
                for b in range(8):
                    where = place(p, eight * 8 + b, half)
                    final = cloud[where, :]
                    gain = (final - start[where, :]) * mass
                    weighed = final * mass
                    square = weighed * weighed
                    heats = jnp.where(
                        srow == b, jnp.sum(gain[0:32], axis=0, keepdims=True) + gain[32:33], heats
                    )
                    echos = jnp.where(
                        srow == b, jnp.sum(square[0:32], axis=0, keepdims=True) + square[32:33], echos
                    )
                rows = pl.ds(pl.multiple_of(p * BATCH + eight * 8, 8), 8)
                heat_rows[rows, at] = heats
                echo_rows[rows, at] = echos
        return 0

    lax.fori_loop(0, COLS // BATCH, batch, 0)

    def group_mean(x):
        acc = None
        for part in split3(x):
            y = jnp.dot(part, group[...], preferred_element_type=F32)
            acc = y if acc is None else acc + y
        return acc

    back = unsort[...]
    heat = group_mean(heat_rows[...]).astype(BF)
    heat_out[...] = jnp.dot(back, heat, preferred_element_type=F32).astype(BF)
    echo_out[...] = jnp.log(1.0 + dot_exact(back, group_mean(echo_rows[...])))
    for b in range(BINS):
        halves = [cloud[pl.ds(half * COLS * ROWS + b, COLS, stride=ROWS), :] for half in range(2)]
        drops_next[b] = jnp.dot(
            back, jnp.concatenate(halves, axis=1).astype(BF), preferred_element_type=F32
        ).astype(BF)


def microphysics(counts, start, cell_forcing, pair_coef, growth, unsort):
    return pl.pallas_call(
        micro_kernel,
        out_shape=(
            jax.ShapeDtypeStruct((BINS, COLS, 256), BF),
            jax.ShapeDtypeStruct((COLS, 128), BF),
            jax.ShapeDtypeStruct((COLS, 128), F32),
        ),
        in_specs=[SMEM] + [VMEM] * 6,
        out_specs=(VMEM,) * 3,
        scratch_shapes=[
            pltpu.VMEM((2 * COLS * ROWS, 128), F32),
            pltpu.VMEM((BATCH, 2, 48, 128), F32),
            pltpu.VMEM((BATCH, 2, ROWS, 128), F32),
            pltpu.VMEM((COLS, 256), F32),
            pltpu.VMEM((COLS, 256), F32),
        ],
        compiler_params=pltpu.CompilerParams(vmem_limit_bytes=40 << 20),
        name="microphysics",
    )(counts, start, cell_forcing, pair_coef, growth, jnp.asarray(group_matrix()), unsort)


def coupling_kernel(
    state, heat, echo, owner, heating, spread, slots,
    tracer_next, power,
    field, packs, rows, got_packs, got_rows, sent, first_in, second_out, second_in,
    send, recv, send1, recv1, send2, recv2,
):
    g, c, up, down, left, right = neighbours()
    barrier = pltpu.get_barrier_semaphore()
    peers = [(lax.rem(g + k, NG), c) for k in range(1, NG)]
    peers += [(g, lax.rem(c + k, NC)) for k in range(1, NC)]
    peers += [(r, s) for s in (left, right) for r in (up, down)]
    for to in peers:
        pl.semaphore_signal(barrier, inc=1, device_id=to, device_id_type=MESH)

    warm = []
    for e in range(2):
        turned = heat[64 * e : 64 * (e + 1), :].astype(F32).T.astype(BF)[0:16]
        warm.append(jnp.dot(turned, spread[...], preferred_element_type=F32).astype(BF))
    warm = jnp.concatenate(warm + warm, axis=0)
    for half in range(2):
        at = slice(half * 128, (half + 1) * 128)
        back = jnp.dot(heating[...], warm[:, at], preferred_element_type=F32)
        field[half * PTS : (half + 1) * PTS, :] = back + state[:, :, at].reshape(PTS, 128)
    pack_edges(field, packs, rows)
    pl.semaphore_wait(barrier, len(peers))
    copies = halo_copies(packs, rows, got_packs, got_rows, send, recv)
    for copy in copies:
        copy.start()

    across = jnp.broadcast_to(owner[...], (COLS, COLS))
    i0 = lax.broadcasted_iota(jnp.int32, (COLS, COLS), 0)
    i1 = lax.broadcasted_iota(jnp.int32, (COLS, COLS), 1)
    along = jnp.sum(jnp.where(i0 == i1, across.astype(F32), 0.0), axis=1, keepdims=True)
    earlier = (along == across.astype(F32)) & (i0 < i1)
    turn = jnp.sum(jnp.where(earlier, 1.0, 0.0), axis=0, keepdims=True)
    key = across % NC * NG + across // NC
    onehot = jnp.concatenate(
        [jnp.where((key == i0) & (turn == float(r)), 1.0, 0.0) for r in range(2)], axis=1
    ).astype(BF)
    sums = echo[...]
    sums = jnp.concatenate([sums, pltpu.roll(sums, 16, 1)], axis=0)
    sent[...] = dot_exact(onehot, sums).reshape(NC, NG, 128)
    first = []
    for k in range(1, NC):
        to = lax.rem(c + k, NC)
        copy = pltpu.make_async_remote_copy(
            src_ref=sent.at[to],
            dst_ref=first_in.at[c],
            send_sem=send1.at[k],
            recv_sem=recv1.at[c],
            device_id=(g, to),
            device_id_type=MESH,
        )
        copy.start()
        first.append(copy)
    first_in[c] = sent[c]

    for copy in copies:
        copy.wait()

    def last(i, half, mean):
        tracer_next[pl.ds(i * 8, 8), :, half * 128 : (half + 1) * 128] = mean

    assemble_loop(field, got_packs, got_rows, last)

    for k, copy in enumerate(first, 1):
        copy.wait_send()
        source = lax.rem(c + k, NC)
        pltpu.make_async_remote_copy(
            src_ref=sent.at[source],
            dst_ref=first_in.at[source],
            send_sem=send1.at[k],
            recv_sem=recv1.at[source],
            device_id=(g, source),
            device_id_type=MESH,
        ).wait_recv()
    every = first_in[...]
    for to in range(NG):
        second_out[to] = every[:, to, :]
    second = []
    for k in range(1, NG):
        to = lax.rem(g + k, NG)
        copy = pltpu.make_async_remote_copy(
            src_ref=second_out.at[to],
            dst_ref=second_in.at[g],
            send_sem=send2.at[k],
            recv_sem=recv2.at[g],
            device_id=(to, c),
            device_id_type=MESH,
        )
        copy.start()
        second.append(copy)
    second_in[g] = second_out[g]
    for k, copy in enumerate(second, 1):
        copy.wait_send()
        source = lax.rem(g + k, NG)
        pltpu.make_async_remote_copy(
            src_ref=second_out.at[source],
            dst_ref=second_in.at[source],
            send_sem=send2.at[k],
            recv_sem=recv2.at[source],
            device_id=(source, c),
            device_id_type=MESH,
        ).wait_recv()
    turned = second_in[...].reshape(COLS, 128).T
    turned = jnp.concatenate([turned[0:16], turned[16:32]], axis=1)
    acc = None
    for part in split3(turned):
        y = jnp.dot(part, slots[...], preferred_element_type=F32)
        acc = y if acc is None else acc + y
    power[...] = acc


def coupling(state, heat, echo, owner_row):
    return pl.pallas_call(
        coupling_kernel,
        out_shape=(
            jax.ShapeDtypeStruct(state.shape, F32),
            jax.ShapeDtypeStruct((CLEV, 256), F32),
        ),
        in_specs=[VMEM] * 7,
        out_specs=(VMEM,) * 2,
        scratch_shapes=[
            pltpu.VMEM((2 * PTS, 128), F32),
            pltpu.VMEM((2, 8, 128), F32),
            pltpu.VMEM((2, 2 * LEV, 128), F32),
            pltpu.VMEM((6, 8, 128), F32),
            pltpu.VMEM((2, 2 * LEV, 128), F32),
            pltpu.VMEM((NC, NG, 128), F32),
            pltpu.VMEM((NC, NG, 128), F32),
            pltpu.VMEM((NG, NC, 128), F32),
            pltpu.VMEM((NG, NC, 128), F32),
            pltpu.SemaphoreType.DMA((8,)),
            pltpu.SemaphoreType.DMA((8,)),
            pltpu.SemaphoreType.DMA((NC,)),
            pltpu.SemaphoreType.DMA((NC,)),
            pltpu.SemaphoreType.DMA((NG,)),
            pltpu.SemaphoreType.DMA((NG,)),
        ],
        compiler_params=pltpu.CompilerParams(
            collective_id=1, has_side_effects=True, vmem_limit_bytes=40 << 20
        ),
        name="coupling",
    )(
        state, heat, echo, owner_row,
        jnp.asarray(heating_table()), jnp.asarray(spread_columns()), jnp.asarray(slot_table()),
    )


def shards(tracer, wind_x, wind_y, drops, owner, counts, collision, growth):
    state, cell_forcing, pair_coef, growth_col, start, sorted_counts, unsort = dynamics(
        tracer, wind_x, wind_y, drops.transpose(1, 0, 2),
        counts.reshape(1, COLS), growth.reshape(1, BINS), collision,
    )
    drops_next, heat, echo = microphysics(
        sorted_counts, start, cell_forcing, pair_coef, growth_col, unsort
    )
    tracer_next, power = coupling(state, heat, echo, owner.reshape(1, COLS))
    return (tracer_next, drops_next.transpose(1, 0, 2), power)


def solution(mesh):
    return jax.shard_map(
        shards,
        mesh=mesh,
        in_specs=(
            P(None, "gcm", "crm"),
            P(None, "gcm", "crm"),
            P(None, "gcm", "crm"),
            P(("gcm", "crm"), None, None),
            P(("gcm", "crm"), None),
            P(("gcm", "crm")),
            P(),
            P(),
        ),
        out_specs=(P(None, "gcm", "crm"), P(("gcm", "crm"), None, None), P(None, ("gcm", "crm"))),
        check_vma=False,
    )
```

```python
import functools

import jax
import jax.numpy as jnp
import ml_dtypes
import numpy as np
from jax import lax
from jax.experimental import pallas as pl
from jax.experimental.pallas import tpu as pltpu
from jax.sharding import PartitionSpec as P

BF = jnp.bfloat16
F32 = jnp.float32
MESH = pl.DeviceIdType.MESH
HIGH = lax.Precision.HIGHEST
VMEM = pl.BlockSpec(memory_space=pltpu.VMEM)
SMEM = pl.BlockSpec(memory_space=pltpu.SMEM)
HBM = pl.BlockSpec(memory_space=pltpu.HBM)

NG = 8
NC = 16
LEV = 72
BINS = 33
CLEV = 16
COLS = 128
PTS = LEV * 8
PAIRS = 576
DT_DYN = 0.04
DT_CRM = 0.05
DT_PHYS = 0.5
BATCH = 16
ROWS = 40


def gll_tables():
    inv_root = 1.0 / np.sqrt(5.0)
    gll_nodes = np.array([-1.0, -inv_root, inv_root, 1.0])
    weights = np.array([1.0, 5.0, 5.0, 1.0]) / 6.0
    legendre = (5.0 * gll_nodes**3 - 3.0 * gll_nodes) / 2.0
    derivative = np.zeros((4, 4))
    for i in range(4):
        for j in range(4):
            if i != j:
                derivative[i, j] = legendre[i] / (legendre[j] * (gll_nodes[i] - gll_nodes[j]))
    derivative[0, 0] = -3.0
    derivative[3, 3] = 3.0
    return (2.0 * derivative, weights)


def level_tables(levels, crm_levels):
    spacing = levels / crm_levels
    centres = (np.arange(crm_levels) + 0.5) * spacing - 0.5
    hats = np.maximum(0.0, 1.0 - np.abs(np.arange(levels)[None, :] - centres[:, None]) / spacing)
    down_map = hats / hats.sum(axis=1, keepdims=True)
    up_map = hats.T / hats.T.sum(axis=1, keepdims=True)
    return (down_map, up_map)


def stencil_table():
    derivative, _ = gll_tables()
    out = np.zeros((14, 8, 128), np.float32)
    for s in range(-3, 4):
        for i in range(4):
            if 0 <= i + s < 4:
                out[s + 3, i::4, :] = -derivative[i, i + s]
                out[s + 10, :, i::4] = -derivative[i, i + s]
    return out


def forcing_tables():
    _, weights = gll_tables()
    down_map, _ = level_tables(LEV, CLEV)
    rows = np.zeros((2, CLEV, LEV, 8))
    for r in range(8):
        rows[r // 4, :, :, r] = down_map * weights[r % 4] / 2.0 * 0.5
    cols = np.zeros((64, 256))
    for c in range(256):
        cols[c // 4, c] = weights[c % 4] / 2.0
    return rows.reshape(32, PTS).astype(np.float32), cols.astype(np.float32)


def spread_cells():
    out = np.zeros((CLEV, 256), np.float32)
    for c in range(256):
        out[c // 16, c] = 1.0
    return out.astype(ml_dtypes.bfloat16)


def group_matrix():
    out = np.zeros((256, 128), np.float32)
    for c in range(256):
        out[c, c // 16] = 1.0 / 16.0
    return out.astype(ml_dtypes.bfloat16)


def heating_table():
    _, up_map = level_tables(LEV, CLEV)
    half = (DT_PHYS * up_map).astype(np.float32)
    first = half.astype(ml_dtypes.bfloat16)
    second = (half - first.astype(np.float32)).astype(ml_dtypes.bfloat16)
    out = np.zeros((LEV, 8, 2, 2, CLEV), ml_dtypes.bfloat16)
    for r in range(8):
        out[:, r, 0, r // 4, :] = first
        out[:, r, 1, r // 4, :] = second
    return out.reshape(PTS, 64)


def spread_columns():
    out = np.zeros((64, 256), np.float32)
    for c in range(256):
        out[c // 4, c] = 1.0
    return out.astype(ml_dtypes.bfloat16)


def slot_table():
    out = np.zeros((2, 128, 256), np.float32)
    for d in range(128):
        for r in range(2):
            out[r, d, 2 * d + r] = 1.0
    return out.reshape(256, 256).astype(ml_dtypes.bfloat16)


def pair_list():
    out = []
    for d in range(16):
        for i in range(32):
            out.append((i, (i + d) % 32))
    for i in range(16):
        out.append((i, i + 16))
    for i in range(32):
        out.append((i, 32))
    out.append((32, 32))
    return out


def pair_selector():
    out = np.zeros((BINS * BINS, PAIRS), np.float32)
    for q, (i, j) in enumerate(pair_list()):
        out[i * BINS + j, q] = 1.0
        out[j * BINS + i, q] = 1.0
    return out.astype(ml_dtypes.bfloat16)


def split3(x):
    hi = x.astype(BF)
    rest = x - hi.astype(F32)
    mid = rest.astype(BF)
    return hi, mid, (rest - mid.astype(F32)).astype(BF)


def dot_exact(onehot, x):
    acc = None
    for part in split3(x):
        y = jnp.dot(onehot, part, preferred_element_type=F32)
        acc = y if acc is None else acc + y
    return acc


def tendency(q, wind_x, wind_y, table):
    grad_x = table[3][None] * q
    grad_y = table[10][None] * q
    for s in (-3, -2, -1, 1, 2, 3):
        grad_x = grad_x + table[s + 3][None] * pltpu.roll(q, (-s) % 8, 1)
        grad_y = grad_y + table[s + 10][None] * pltpu.roll(q, (-s) % 128, 2)
    return wind_x * grad_x + wind_y * grad_y


def neighbours():
    g = lax.axis_index("gcm")
    c = lax.axis_index("crm")
    up, down = lax.rem(g + NG - 1, NG), lax.rem(g + 1, NG)
    left, right = lax.rem(c + NC - 1, NC), lax.rem(c + 1, NC)
    return g, c, up, down, left, right


def pack_edges(field, packs, rows):
    lane = lax.broadcasted_iota(jnp.int32, (8, 128), 1)

    def one(i, carry):
        low, high = carry
        low, high = pltpu.roll(low, 120, 1), pltpu.roll(high, 120, 1)
        for k in range(8):
            at = pl.multiple_of(i * 64, 64) + 8 * k
            first, last = field[pl.ds(at, 8), :], field[pl.ds(PTS + at, 8), :]
            both = pltpu.roll(jnp.where(lane == 0, first, last), k + 1, 1)
            high = jnp.where(lane == k, both, high)
            low = jnp.where(lane == k + 1, both, low)
        return low, high

    zero = jnp.zeros((8, 128), F32)
    low, high = lax.fori_loop(0, 9, one, (zero, zero))
    packs[0] = pltpu.roll(low, 63, 1)
    packs[1] = pltpu.roll(high, 64, 1)
    for half in range(2):
        rows[0, half * LEV : (half + 1) * LEV, :] = field[pl.ds(half * PTS, LEV, stride=8), :]
        rows[1, half * LEV : (half + 1) * LEV, :] = field[pl.ds(half * PTS + 7, LEV, stride=8), :]


def halo_copies(packs, rows, got_packs, got_rows, send, recv):
    g, c, up, down, left, right = neighbours()
    plan = [
        (rows.at[1], got_rows.at[0], (down, c)),
        (rows.at[0], got_rows.at[1], (up, c)),
        (packs.at[1], got_packs.at[0], (g, right)),
        (packs.at[1], got_packs.at[1], (down, right)),
        (packs.at[1], got_packs.at[2], (up, right)),
        (packs.at[0], got_packs.at[3], (g, left)),
        (packs.at[0], got_packs.at[4], (down, left)),
        (packs.at[0], got_packs.at[5], (up, left)),
    ]
    return [
        pltpu.make_async_remote_copy(
            src_ref=src,
            dst_ref=dst,
            send_sem=send.at[n],
            recv_sem=recv.at[n],
            device_id=to,
            device_id_type=MESH,
        )
        for n, (src, dst, to) in enumerate(plan)
    ]


def assemble_loop(field, got_packs, got_rows, use):
    row = lax.broadcasted_iota(jnp.int32, (8, 128), 0)
    lane = lax.broadcasted_iota(jnp.int32, (8, 128), 1)

    def row_mean(x, above, below):
        up = jnp.where(row == 0, pltpu.roll(above, 1, 0), pltpu.roll(x, 1, 0))
        down = jnp.where(row == 7, pltpu.roll(below, 7, 0), pltpu.roll(x, 7, 0))
        other = jnp.where(row % 4 == 3, down, jnp.where(row % 4 == 0, up, x))
        return 0.5 * (x + other)

    left_halo = row_mean(got_packs[0], got_packs[1], got_packs[2])
    right_halo = row_mean(got_packs[3], got_packs[4], got_packs[5])
    edge_row = ((row == 0) | (row == 7))[None]
    upper = (row < 4)[None]
    is3, is4 = (row == 3)[None], (row == 4)[None]
    lane3, lane0 = (lane % 4 == 3)[None], (lane % 4 == 0)[None]
    first, last = (lane == 0)[None], (lane == 127)[None]

    def one(i, carry):
        left_c, right_c = carry
        means = []
        for half in range(2):
            at = pl.multiple_of(half * PTS + i * 64, 64)
            x = field[pl.ds(at, 64), :].reshape(8, 8, 128)
            lev = pl.multiple_of(half * LEV + i * 8, 8)
            above = jnp.broadcast_to(got_rows[0, pl.ds(lev, 8), :][:, None, :], (8, 8, 128))
            below = jnp.broadcast_to(got_rows[1, pl.ds(lev, 8), :][:, None, :], (8, 8, 128))
            other = jnp.where(is3, pltpu.roll(x, 7, 1), jnp.where(is4, pltpu.roll(x, 1, 1), x))
            other = jnp.where(edge_row, jnp.where(upper, above, below), other)
            means.append(0.5 * (x + other))
        lefts = [pltpu.roll(m, 1, 2) for m in means]
        rights = [pltpu.roll(m, 127, 2) for m in means]
        halo_l = jnp.stack([pltpu.roll(left_c, (128 - k) % 128, 1) if k else left_c for k in range(8)])
        halo_r = jnp.stack([pltpu.roll(right_c, 127 - k, 1) for k in range(8)])
        near_l = [jnp.where(first, halo_l, lefts[0]), jnp.where(first, lefts[0], lefts[1])]
        near_r = [jnp.where(last, rights[1], rights[0]), jnp.where(last, halo_r, rights[1])]
        for half in range(2):
            m = means[half]
            other = jnp.where(lane3, near_r[half], jnp.where(lane0, near_l[half], m))
            use(i, half, 0.5 * (m + other))
        return pltpu.roll(left_c, 120, 1), pltpu.roll(right_c, 120, 1)

    lax.fori_loop(0, 9, one, (left_halo, right_halo))


def chunk_of(ref, i, half):
    return ref[pl.ds(i * 8, 8), :, half * 128 : (half + 1) * 128]


def dynamics_kernel(
    tracer_h, wind_x_h, wind_y_h, drops_h, counts_h, growth_h, collision_h, table_h, selector_h,
    row_map_h, col_map_h, cells_h,
    state, cell_forcing, pair_coef, growth_col, start, counts_out, unsort,
    tracer, wind_x, wind_y, drops, counts, growth, collision, table, selector, row_map, col_map, cells,
    loads, field, total, packs, rows, got_packs, got_rows, send, recv,
):
    g, c, up, down, left, right = neighbours()
    barrier = pltpu.get_barrier_semaphore()
    around = [(up, c), (down, c)]
    around += [(r, s) for s in (left, right) for r in (g, up, down)]
    sources = [table_h, tracer_h, wind_x_h, wind_y_h, counts_h, growth_h, collision_h, selector_h, drops_h,
               row_map_h, col_map_h, cells_h]
    targets = [table, tracer, wind_x, wind_y, counts, growth, collision, selector, drops,
               row_map, col_map, cells]
    fetch = [
        pltpu.make_async_copy(source, target, loads.at[n])
        for n, (source, target) in enumerate(zip(sources, targets))
    ]
    for copy in fetch:
        copy.start()
    for to in around:
        pl.semaphore_signal(barrier, inc=1, device_id=to, device_id_type=MESH)
    for copy in fetch[0:4]:
        copy.wait()

    def first(i, _):
        for half in range(2):
            t = tendency(
                chunk_of(tracer, i, half), chunk_of(wind_x, i, half), chunk_of(wind_y, i, half), table
            )
            field[pl.ds(pl.multiple_of(half * PTS + i * 64, 64), 64), :] = t.reshape(64, 128)
        return 0

    lax.fori_loop(0, 9, first, 0)
    pack_edges(field, packs.at[0], rows.at[0])
    pl.semaphore_wait(barrier, 8)
    copies = halo_copies(packs.at[0], rows.at[0], got_packs.at[0], got_rows.at[0], send.at[0], recv.at[0])
    for copy in copies:
        copy.start()

    for copy in fetch[4:]:
        copy.wait()
    pair_coef[0:33, :] = jnp.dot(
        collision[...], selector[...], preferred_element_type=F32
    ).astype(BF)
    pair_coef[33:48, :] = jnp.zeros((15, PAIRS), BF)
    i0 = lax.broadcasted_iota(jnp.int32, (COLS, COLS), 0)
    i1 = lax.broadcasted_iota(jnp.int32, (COLS, COLS), 1)
    wide = jnp.concatenate([growth[...], jnp.zeros((1, COLS - BINS), F32)], axis=1)
    growth_col[...] = jnp.broadcast_to(
        jnp.sum(
            jnp.where((i0 == i1)[0:ROWS], jnp.broadcast_to(wide, (ROWS, COLS)), 0.0), axis=1, keepdims=True
        ),
        (ROWS, COLS),
    )
    across = jnp.broadcast_to(counts[...], (COLS, COLS)).astype(F32)
    along = jnp.sum(jnp.where(i0 == i1, across, 0.0), axis=1, keepdims=True)
    before = (across > along) | ((across == along) & (i1 < i0))
    place = jnp.sum(jnp.where(before, 1.0, 0.0), axis=1, keepdims=True).astype(jnp.int32)
    after = (along > across) | ((along == across) & (i0 < i1))
    place_row = jnp.sum(jnp.where(after, 1.0, 0.0), axis=0, keepdims=True).astype(jnp.int32)
    counts_out[...] = jnp.sum(jnp.where(place == i1, along, 0.0), axis=0, keepdims=True).astype(jnp.int32)
    unsort[...] = jnp.where(place == i1, 1.0, 0.0).astype(BF)
    sort = jnp.where(place_row == i0, 1.0, 0.0).astype(BF)
    for b in range(BINS):
        sorted_bin = jnp.dot(sort, drops[b], preferred_element_type=F32)
        for half in range(2):
            start[pl.ds(half * COLS * ROWS + b, COLS, stride=ROWS), :] = sorted_bin[
                :, half * 128 : (half + 1) * 128
            ]

    for copy in copies:
        copy.wait()

    def second(i, half, mean):
        at = pl.multiple_of(half * PTS + i * 64, 64)
        moved = chunk_of(tracer, i, half) + DT_DYN * mean
        state[pl.ds(i * 8, 8), :, half * 128 : (half + 1) * 128] = moved
        total[pl.ds(at, 64), :] = mean.reshape(64, 128)
        t = tendency(moved, chunk_of(wind_x, i, half), chunk_of(wind_y, i, half), table)
        field[pl.ds(at, 64), :] = t.reshape(64, 128)

    assemble_loop(field, got_packs.at[0], got_rows.at[0], second)
    pack_edges(field, packs.at[1], rows.at[1])
    copies = halo_copies(packs.at[1], rows.at[1], got_packs.at[1], got_rows.at[1], send.at[1], recv.at[1])
    for copy in copies:
        copy.start()
    for copy in copies:
        copy.wait()

    def third(i, half, mean):
        at = pl.multiple_of(half * PTS + i * 64, 64)
        state[pl.ds(i * 8, 8), :, half * 128 : (half + 1) * 128] = (
            chunk_of(state, i, half) + DT_DYN * mean
        )
        total[pl.ds(at, 64), :] = total[pl.ds(at, 64), :] + mean.reshape(64, 128)

    assemble_loop(field, got_packs.at[1], got_rows.at[1], third)
    parts = [
        jnp.dot(row_map[...], total[half * PTS : (half + 1) * PTS, :], precision=HIGH, preferred_element_type=F32)
        for half in range(2)
    ]
    by_row = jnp.concatenate(parts, axis=1)
    forcing = [
        lax.dot_general(
            col_map[...], by_row[16 * e : 16 * (e + 1)], (((1,), (1,)), ((), ())),
            precision=HIGH, preferred_element_type=F32,
        ).astype(BF)
        for e in range(2)
    ]
    by_cell = jnp.dot(
        jnp.concatenate(forcing, axis=0), cells[...], preferred_element_type=F32
    ).astype(BF)
    cell_forcing[...] = DT_CRM * jnp.dot(sort, by_cell, preferred_element_type=F32)


def dynamics(tracer, wind_x, wind_y, drops, counts_row, growth_row, collision):
    row_map, col_map = forcing_tables()
    shape = tracer.shape
    operands = (
        tracer, wind_x, wind_y, drops, counts_row, growth_row, collision,
        jnp.asarray(stencil_table()), jnp.asarray(pair_selector()),
        jnp.asarray(row_map), jnp.asarray(col_map), jnp.asarray(spread_cells()),
    )
    return pl.pallas_call(
        dynamics_kernel,
        out_shape=(
            jax.ShapeDtypeStruct(shape, F32),
            jax.ShapeDtypeStruct((COLS, 256), F32),
            jax.ShapeDtypeStruct((48, PAIRS), BF),
            jax.ShapeDtypeStruct((ROWS, 128), F32),
            jax.ShapeDtypeStruct((2 * COLS * ROWS, 128), F32),
            jax.ShapeDtypeStruct((1, COLS), jnp.int32),
            jax.ShapeDtypeStruct((COLS, COLS), BF),
        ),
        in_specs=[HBM] * 12,
        out_specs=(VMEM,) * 7,
        scratch_shapes=[pltpu.VMEM(x.shape, x.dtype) for x in operands]
        + [
            pltpu.SemaphoreType.DMA((12,)),
            pltpu.VMEM((2 * PTS, 128), F32),
            pltpu.VMEM((2 * PTS, 128), F32),
            pltpu.VMEM((2, 2, 8, 128), F32),
            pltpu.VMEM((2, 2, 2 * LEV, 128), F32),
            pltpu.VMEM((2, 6, 8, 128), F32),
            pltpu.VMEM((2, 2, 2 * LEV, 128), F32),
            pltpu.SemaphoreType.DMA((2, 8)),
            pltpu.SemaphoreType.DMA((2, 8)),
        ],
        compiler_params=pltpu.CompilerParams(
            collective_id=0, has_side_effects=True, vmem_limit_bytes=40 << 20
        ),
        name="dynamics",
    )(*[pltpu.with_memory_space_constraint(x, pltpu.HBM) for x in operands])


def micro_kernel(
    counts, start, cell_forcing, pair_coef, growth, group, unsort,
    drops_next, heat_out, echo_out,
    cloud, doubled, grow, heat_rows, echo_rows,
):
    mass = (lax.broadcasted_iota(jnp.int32, (ROWS, 128), 0).astype(F32) + 1.0) / BINS
    srow = lax.broadcasted_iota(jnp.int32, (8, 128), 0)

    def place(p, b, half):
        return pl.ds(pl.multiple_of((half * COLS + p * BATCH + b) * ROWS, 8), ROWS)

    def substep(s, p):
        for b in range(BATCH):
            active = s < counts[0, p * BATCH + b]
            blocks, grown, olds = [], [], []
            for half in range(2):
                old = cloud[place(p, b, half), :]
                now = old + grow[b, half]
                doubled[b, half, 0:32, :] = now[0:32]
                doubled[b, half, 32:48, :] = now[0:16]
                near, far = [], []
                for d in range(8):
                    shifted = doubled[b, half, d : d + 40, :]
                    near.append((now[0:32] * shifted[0:32]).astype(BF))
                    far.append((now[0:32] * shifted[8:40]).astype(BF))
                last = jnp.broadcast_to(now[32:33], (32, 128))
                rest = [
                    (now[0:16] * now[16:32]).astype(BF),
                    (now[0:32] * last).astype(BF),
                    (last[0:16] * last[0:16]).astype(BF),
                ]
                blocks.append(jnp.concatenate(near + far + rest, axis=0))
                grown.append(now)
                olds.append(old)
            change = jnp.dot(
                pair_coef[...], jnp.concatenate(blocks, axis=1), preferred_element_type=F32
            )
            for half in range(2):
                moved = grown[half] + DT_CRM * change[0:ROWS, half * 128 : (half + 1) * 128]
                cloud[place(p, b, half), :] = jnp.where(active, moved, olds[half])
        return p

    def batch(p, _):
        for b in range(BATCH):
            forced = cell_forcing[pl.ds(p * BATCH + b, 1), :]
            for half in range(2):
                cloud[place(p, b, half), :] = start[place(p, b, half), :]
                grow[b, half] = forced[:, half * 128 : (half + 1) * 128] * growth[...]
        lax.fori_loop(0, counts[0, p * BATCH], substep, p)
        for half in range(2):
            at = slice(half * 128, (half + 1) * 128)
            for eight in range(BATCH // 8):
                heats = jnp.zeros((8, 128), F32)
                echos = jnp.zeros((8, 128), F32)
                for b in range(8):
                    where = place(p, eight * 8 + b, half)
                    final = cloud[where, :]
                    gain = (final - start[where, :]) * mass
                    weighed = final * mass
                    square = weighed * weighed
                    heats = jnp.where(
                        srow == b, jnp.sum(gain[0:32], axis=0, keepdims=True) + gain[32:33], heats
                    )
                    echos = jnp.where(
                        srow == b, jnp.sum(square[0:32], axis=0, keepdims=True) + square[32:33], echos
                    )
                rows = pl.ds(pl.multiple_of(p * BATCH + eight * 8, 8), 8)
                heat_rows[rows, at] = heats
                echo_rows[rows, at] = echos
        return 0

    lax.fori_loop(0, COLS // BATCH, batch, 0)

    def group_mean(x):
        acc = None
        for part in split3(x):
            y = jnp.dot(part, group[...], preferred_element_type=F32)
            acc = y if acc is None else acc + y
        return acc

    back = unsort[...]
    heat = group_mean(heat_rows[...]).astype(BF)
    heat_out[...] = jnp.dot(back, heat, preferred_element_type=F32).astype(BF)
    echo_out[...] = jnp.log(1.0 + dot_exact(back, group_mean(echo_rows[...])))
    for b in range(BINS):
        halves = [cloud[pl.ds(half * COLS * ROWS + b, COLS, stride=ROWS), :] for half in range(2)]
        drops_next[b] = jnp.dot(
            back, jnp.concatenate(halves, axis=1).astype(BF), preferred_element_type=F32
        ).astype(BF)


def microphysics(counts, start, cell_forcing, pair_coef, growth, unsort):
    return pl.pallas_call(
        micro_kernel,
        out_shape=(
            jax.ShapeDtypeStruct((BINS, COLS, 256), BF),
            jax.ShapeDtypeStruct((COLS, 128), BF),
            jax.ShapeDtypeStruct((COLS, 128), F32),
        ),
        in_specs=[SMEM] + [VMEM] * 6,
        out_specs=(VMEM,) * 3,
        scratch_shapes=[
            pltpu.VMEM((2 * COLS * ROWS, 128), F32),
            pltpu.VMEM((BATCH, 2, 48, 128), F32),
            pltpu.VMEM((BATCH, 2, ROWS, 128), F32),
            pltpu.VMEM((COLS, 256), F32),
            pltpu.VMEM((COLS, 256), F32),
        ],
        compiler_params=pltpu.CompilerParams(vmem_limit_bytes=40 << 20),
        name="microphysics",
    )(counts, start, cell_forcing, pair_coef, growth, jnp.asarray(group_matrix()), unsort)


def coupling_kernel(
    state, heat, echo, owner, heating, spread, slots,
    tracer_next, power,
    field, packs, rows, got_packs, got_rows, sent, first_in, second_out, second_in,
    send, recv, send1, recv1, send2, recv2,
):
    g, c, up, down, left, right = neighbours()
    barrier = pltpu.get_barrier_semaphore()
    peers = [(lax.rem(g + k, NG), c) for k in range(1, NG)]
    peers += [(g, lax.rem(c + k, NC)) for k in range(1, NC)]
    peers += [(r, s) for s in (left, right) for r in (up, down)]
    for to in peers:
        pl.semaphore_signal(barrier, inc=1, device_id=to, device_id_type=MESH)

    warm = []
    for e in range(2):
        turned = heat[64 * e : 64 * (e + 1), :].astype(F32).T.astype(BF)[0:16]
        warm.append(jnp.dot(turned, spread[...], preferred_element_type=F32).astype(BF))
    warm = jnp.concatenate(warm + warm, axis=0)
    for half in range(2):
        at = slice(half * 128, (half + 1) * 128)
        back = jnp.dot(heating[...], warm[:, at], preferred_element_type=F32)
        field[half * PTS : (half + 1) * PTS, :] = back + state[:, :, at].reshape(PTS, 128)
    pack_edges(field, packs, rows)
    pl.semaphore_wait(barrier, len(peers))
    copies = halo_copies(packs, rows, got_packs, got_rows, send, recv)
    for copy in copies:
        copy.start()

    across = jnp.broadcast_to(owner[...], (COLS, COLS))
    i0 = lax.broadcasted_iota(jnp.int32, (COLS, COLS), 0)
    i1 = lax.broadcasted_iota(jnp.int32, (COLS, COLS), 1)
    along = jnp.sum(jnp.where(i0 == i1, across.astype(F32), 0.0), axis=1, keepdims=True)
    earlier = (along == across.astype(F32)) & (i0 < i1)
    turn = jnp.sum(jnp.where(earlier, 1.0, 0.0), axis=0, keepdims=True)
    key = across % NC * NG + across // NC
    onehot = jnp.concatenate(
        [jnp.where((key == i0) & (turn == float(r)), 1.0, 0.0) for r in range(2)], axis=1
    ).astype(BF)
    sums = echo[...]
    sums = jnp.concatenate([sums, pltpu.roll(sums, 16, 1)], axis=0)
    sent[...] = dot_exact(onehot, sums).reshape(NC, NG, 128)
    first = []
    for k in range(1, NC):
        to = lax.rem(c + k, NC)
        copy = pltpu.make_async_remote_copy(
            src_ref=sent.at[to],
            dst_ref=first_in.at[c],
            send_sem=send1.at[k],
            recv_sem=recv1.at[c],
            device_id=(g, to),
            device_id_type=MESH,
        )
        copy.start()
        first.append(copy)
    first_in[c] = sent[c]

    for copy in copies:
        copy.wait()

    def last(i, half, mean):
        tracer_next[pl.ds(i * 8, 8), :, half * 128 : (half + 1) * 128] = mean

    assemble_loop(field, got_packs, got_rows, last)

    for k, copy in enumerate(first, 1):
        copy.wait_send()
        source = lax.rem(c + k, NC)
        pltpu.make_async_remote_copy(
            src_ref=sent.at[source],
            dst_ref=first_in.at[source],
            send_sem=send1.at[k],
            recv_sem=recv1.at[source],
            device_id=(g, source),
            device_id_type=MESH,
        ).wait_recv()
    every = first_in[...]
    for to in range(NG):
        second_out[to] = every[:, to, :]
    second = []
    for k in range(1, NG):
        to = lax.rem(g + k, NG)
        copy = pltpu.make_async_remote_copy(
            src_ref=second_out.at[to],
            dst_ref=second_in.at[g],
            send_sem=send2.at[k],
            recv_sem=recv2.at[g],
            device_id=(to, c),
            device_id_type=MESH,
        )
        copy.start()
        second.append(copy)
    second_in[g] = second_out[g]
    for k, copy in enumerate(second, 1):
        copy.wait_send()
        source = lax.rem(g + k, NG)
        pltpu.make_async_remote_copy(
            src_ref=second_out.at[source],
            dst_ref=second_in.at[source],
            send_sem=send2.at[k],
            recv_sem=recv2.at[source],
            device_id=(source, c),
            device_id_type=MESH,
        ).wait_recv()
    turned = second_in[...].reshape(COLS, 128).T
    turned = jnp.concatenate([turned[0:16], turned[16:32]], axis=1)
    acc = None
    for part in split3(turned):
        y = jnp.dot(part, slots[...], preferred_element_type=F32)
        acc = y if acc is None else acc + y
    power[...] = acc


def coupling(state, heat, echo, owner_row):
    return pl.pallas_call(
        coupling_kernel,
        out_shape=(
            jax.ShapeDtypeStruct(state.shape, F32),
            jax.ShapeDtypeStruct((CLEV, 256), F32),
        ),
        in_specs=[VMEM] * 7,
        out_specs=(VMEM,) * 2,
        scratch_shapes=[
            pltpu.VMEM((2 * PTS, 128), F32),
            pltpu.VMEM((2, 8, 128), F32),
            pltpu.VMEM((2, 2 * LEV, 128), F32),
            pltpu.VMEM((6, 8, 128), F32),
            pltpu.VMEM((2, 2 * LEV, 128), F32),
            pltpu.VMEM((NC, NG, 128), F32),
            pltpu.VMEM((NC, NG, 128), F32),
            pltpu.VMEM((NG, NC, 128), F32),
            pltpu.VMEM((NG, NC, 128), F32),
            pltpu.SemaphoreType.DMA((8,)),
            pltpu.SemaphoreType.DMA((8,)),
            pltpu.SemaphoreType.DMA((NC,)),
            pltpu.SemaphoreType.DMA((NC,)),
            pltpu.SemaphoreType.DMA((NG,)),
            pltpu.SemaphoreType.DMA((NG,)),
        ],
        compiler_params=pltpu.CompilerParams(
            collective_id=1, has_side_effects=True, vmem_limit_bytes=40 << 20
        ),
        name="coupling",
    )(
        state, heat, echo, owner_row,
        jnp.asarray(heating_table()), jnp.asarray(spread_columns()), jnp.asarray(slot_table()),
    )


def shards(tracer, wind_x, wind_y, drops, owner, counts, collision, growth):
    state, cell_forcing, pair_coef, growth_col, start, sorted_counts, unsort = dynamics(
        tracer, wind_x, wind_y, drops.transpose(1, 0, 2),
        counts.reshape(1, COLS), growth.reshape(1, BINS), collision,
    )
    drops_next, heat, echo = microphysics(
        sorted_counts, start, cell_forcing, pair_coef, growth_col, unsort
    )
    tracer_next, power = coupling(state, heat, echo, owner.reshape(1, COLS))
    return (tracer_next, drops_next.transpose(1, 0, 2), power)


def solution(mesh):
    return jax.shard_map(
        shards,
        mesh=mesh,
        in_specs=(
            P(None, "gcm", "crm"),
            P(None, "gcm", "crm"),
            P(None, "gcm", "crm"),
            P(("gcm", "crm"), None, None),
            P(("gcm", "crm"), None),
            P(("gcm", "crm")),
            P(),
            P(),
        ),
        out_specs=(P(None, "gcm", "crm"), P(("gcm", "crm"), None, None), P(None, ("gcm", "crm"))),
        check_vma=False,
    )
```

```python
import functools

import jax
import jax.numpy as jnp
import ml_dtypes
import numpy as np
from jax import lax
from jax.experimental import pallas as pl
from jax.experimental.pallas import tpu as pltpu
from jax.sharding import PartitionSpec as P

BF = jnp.bfloat16
F32 = jnp.float32
MESH = pl.DeviceIdType.MESH
HIGH = lax.Precision.HIGHEST
VMEM = pl.BlockSpec(memory_space=pltpu.VMEM)
SMEM = pl.BlockSpec(memory_space=pltpu.SMEM)
HBM = pl.BlockSpec(memory_space=pltpu.HBM)

NG = 8
NC = 16
LEV = 72
BINS = 33
CLEV = 16
COLS = 128
PTS = LEV * 8
PAIRS = 576
DT_DYN = 0.04
DT_CRM = 0.05
DT_PHYS = 0.5
BATCH = 32
ROWS = 40


def gll_tables():
    inv_root = 1.0 / np.sqrt(5.0)
    gll_nodes = np.array([-1.0, -inv_root, inv_root, 1.0])
    weights = np.array([1.0, 5.0, 5.0, 1.0]) / 6.0
    legendre = (5.0 * gll_nodes**3 - 3.0 * gll_nodes) / 2.0
    derivative = np.zeros((4, 4))
    for i in range(4):
        for j in range(4):
            if i != j:
                derivative[i, j] = legendre[i] / (legendre[j] * (gll_nodes[i] - gll_nodes[j]))
    derivative[0, 0] = -3.0
    derivative[3, 3] = 3.0
    return (2.0 * derivative, weights)


def level_tables(levels, crm_levels):
    spacing = levels / crm_levels
    centres = (np.arange(crm_levels) + 0.5) * spacing - 0.5
    hats = np.maximum(0.0, 1.0 - np.abs(np.arange(levels)[None, :] - centres[:, None]) / spacing)
    down_map = hats / hats.sum(axis=1, keepdims=True)
    up_map = hats.T / hats.T.sum(axis=1, keepdims=True)
    return (down_map, up_map)


def stencil_tables():
    derivative, _ = gll_tables()
    out = []
    for size in (64, 128):
        whole = np.kron(np.eye(size // 4), -derivative).astype(np.float32)
        if size == 128:
            whole = whole.T
        near = whole.astype(ml_dtypes.bfloat16)
        out += [near, (whole - near.astype(np.float32)).astype(ml_dtypes.bfloat16)]
    by_rows = np.concatenate([out[0], out[0], out[1]], axis=1)
    by_cols = np.block([[out[2], out[3]], [out[2], np.zeros_like(out[2])]])
    return by_rows, by_cols


def forcing_tables():
    _, weights = gll_tables()
    down_map, _ = level_tables(LEV, CLEV)
    rows = np.zeros((2, CLEV, LEV, 8))
    for r in range(8):
        rows[r // 4, :, :, r] = down_map * weights[r % 4] / 2.0 * 0.5
    cols = np.zeros((64, 256))
    for c in range(256):
        cols[c // 4, c] = weights[c % 4] / 2.0
    return rows.reshape(32, PTS).astype(np.float32), cols.astype(np.float32)


def spread_cells():
    out = np.zeros((CLEV, 256), np.float32)
    for c in range(256):
        out[c // 16, c] = 1.0
    return out.astype(ml_dtypes.bfloat16)


def group_matrix():
    out = np.zeros((256, 128), np.float32)
    for c in range(256):
        out[c, c // 16] = 1.0 / 16.0
    return out.astype(ml_dtypes.bfloat16)


def heating_table():
    _, up_map = level_tables(LEV, CLEV)
    half = (DT_PHYS * up_map).astype(np.float32)
    first = half.astype(ml_dtypes.bfloat16)
    second = (half - first.astype(np.float32)).astype(ml_dtypes.bfloat16)
    out = np.zeros((LEV, 8, 2, 2, CLEV), ml_dtypes.bfloat16)
    for r in range(8):
        out[:, r, 0, r // 4, :] = first
        out[:, r, 1, r // 4, :] = second
    return out.reshape(PTS, 64)


def spread_columns():
    out = np.zeros((64, 256), np.float32)
    for c in range(256):
        out[c // 4, c] = 1.0
    return out.astype(ml_dtypes.bfloat16)


def slot_table():
    out = np.zeros((2, 128, 256), np.float32)
    for d in range(128):
        for r in range(2):
            out[r, d, 2 * d + r] = 1.0
    return out.reshape(256, 256).astype(ml_dtypes.bfloat16)


def pair_list():
    out = []
    for d in range(16):
        for i in range(32):
            out.append((i, (i + d) % 32))
    for i in range(16):
        out.append((i, i + 16))
    for i in range(32):
        out.append((i, 32))
    out.append((32, 32))
    return out


def pair_selector():
    out = np.zeros((BINS * BINS, PAIRS), np.float32)
    for q, (i, j) in enumerate(pair_list()):
        out[i * BINS + j, q] = 1.0
        out[j * BINS + i, q] = 1.0
    return out.astype(ml_dtypes.bfloat16)


def split3(x):
    hi = x.astype(BF)
    rest = x - hi.astype(F32)
    mid = rest.astype(BF)
    return hi, mid, (rest - mid.astype(F32)).astype(BF)


def dot_exact(onehot, x):
    acc = None
    for part in split3(x):
        y = jnp.dot(onehot, part, preferred_element_type=F32)
        acc = y if acc is None else acc + y
    return acc


def tendency(q, wind_x, wind_y, by_rows, by_cols):
    near = q.astype(BF)
    rest = (q - near.astype(F32)).astype(BF)
    grad_x = jnp.dot(by_rows, jnp.concatenate([near, rest, near], axis=0), preferred_element_type=F32)
    grad_y = []
    for at in (slice(0, 128), slice(128, 256)):
        both = jnp.concatenate([near[:, at], rest[:, at]], axis=1)
        y = jnp.dot(both, by_cols, preferred_element_type=F32)
        grad_y.append(y[:, 0:128] + y[:, 128:256])
    return wind_x * grad_x + wind_y * jnp.concatenate(grad_y, axis=1)


def neighbours():
    g = lax.axis_index("gcm")
    c = lax.axis_index("crm")
    up, down = lax.rem(g + NG - 1, NG), lax.rem(g + 1, NG)
    left, right = lax.rem(c + NC - 1, NC), lax.rem(c + 1, NC)
    return g, c, up, down, left, right


def pack_edges(field, packs, rows):
    lane = lax.broadcasted_iota(jnp.int32, (8, 128), 1)

    def one(i, carry):
        low, high = carry
        low, high = pltpu.roll(low, 120, 1), pltpu.roll(high, 120, 1)
        for k in range(8):
            at = pl.multiple_of(i * 64, 64) + 8 * k
            first, last = field[pl.ds(at, 8), :], field[pl.ds(PTS + at, 8), :]
            both = pltpu.roll(jnp.where(lane == 0, first, last), k + 1, 1)
            high = jnp.where(lane == k, both, high)
            low = jnp.where(lane == k + 1, both, low)
        return low, high

    zero = jnp.zeros((8, 128), F32)
    low, high = lax.fori_loop(0, 9, one, (zero, zero))
    packs[0] = pltpu.roll(low, 63, 1)
    packs[1] = pltpu.roll(high, 64, 1)
    for half in range(2):
        rows[0, half * LEV : (half + 1) * LEV, :] = field[pl.ds(half * PTS, LEV, stride=8), :]
        rows[1, half * LEV : (half + 1) * LEV, :] = field[pl.ds(half * PTS + 7, LEV, stride=8), :]


def halo_copies(packs, rows, got_packs, got_rows, send, recv):
    g, c, up, down, left, right = neighbours()
    plan = [
        (rows.at[1], got_rows.at[0], (down, c)),
        (rows.at[0], got_rows.at[1], (up, c)),
        (packs.at[1], got_packs.at[0], (g, right)),
        (packs.at[1], got_packs.at[1], (down, right)),
        (packs.at[1], got_packs.at[2], (up, right)),
        (packs.at[0], got_packs.at[3], (g, left)),
        (packs.at[0], got_packs.at[4], (down, left)),
        (packs.at[0], got_packs.at[5], (up, left)),
    ]
    return [
        pltpu.make_async_remote_copy(
            src_ref=src,
            dst_ref=dst,
            send_sem=send.at[0 if n < 2 else 1],
            recv_sem=recv.at[0 if n < 2 else 1],
            device_id=to,
            device_id_type=MESH,
        )
        for n, (src, dst, to) in enumerate(plan)
    ]


def wait_bytes(ref, sem):
    pltpu.make_async_copy(ref, ref, sem).wait()


def halo_wait(got_packs, got_rows, send, recv):
    for sems in (recv, send):
        wait_bytes(got_rows, sems.at[0])
        wait_bytes(got_packs, sems.at[1])


def assemble_loop(field, got_packs, got_rows, use):
    row = lax.broadcasted_iota(jnp.int32, (8, 128), 0)
    lane = lax.broadcasted_iota(jnp.int32, (8, 128), 1)

    def row_mean(x, above, below):
        up = jnp.where(row == 0, pltpu.roll(above, 1, 0), pltpu.roll(x, 1, 0))
        down = jnp.where(row == 7, pltpu.roll(below, 7, 0), pltpu.roll(x, 7, 0))
        other = jnp.where(row % 4 == 3, down, jnp.where(row % 4 == 0, up, x))
        return 0.5 * (x + other)

    left_halo = row_mean(got_packs[0], got_packs[1], got_packs[2])
    right_halo = row_mean(got_packs[3], got_packs[4], got_packs[5])
    edge_row = ((row == 0) | (row == 7))[None]
    upper = (row < 4)[None]
    is3, is4 = (row == 3)[None], (row == 4)[None]
    lane3, lane0 = (lane % 4 == 3)[None], (lane % 4 == 0)[None]
    first, last = (lane == 0)[None], (lane == 127)[None]

    def one(i, carry):
        left_c, right_c = carry
        means = []
        for half in range(2):
            at = pl.multiple_of(half * PTS + i * 64, 64)
            x = field[pl.ds(at, 64), :].reshape(8, 8, 128)
            lev = pl.multiple_of(half * LEV + i * 8, 8)
            above = jnp.broadcast_to(got_rows[0, pl.ds(lev, 8), :][:, None, :], (8, 8, 128))
            below = jnp.broadcast_to(got_rows[1, pl.ds(lev, 8), :][:, None, :], (8, 8, 128))
            other = jnp.where(is3, pltpu.roll(x, 7, 1), jnp.where(is4, pltpu.roll(x, 1, 1), x))
            other = jnp.where(edge_row, jnp.where(upper, above, below), other)
            means.append(0.5 * (x + other))
        lefts = [pltpu.roll(m, 1, 2) for m in means]
        rights = [pltpu.roll(m, 127, 2) for m in means]
        halo_l = jnp.stack([pltpu.roll(left_c, (128 - k) % 128, 1) if k else left_c for k in range(8)])
        halo_r = jnp.stack([pltpu.roll(right_c, 127 - k, 1) for k in range(8)])
        near_l = [jnp.where(first, halo_l, lefts[0]), jnp.where(first, lefts[0], lefts[1])]
        near_r = [jnp.where(last, rights[1], rights[0]), jnp.where(last, halo_r, rights[1])]
        done = []
        for half in range(2):
            m = means[half]
            other = jnp.where(lane3, near_r[half], jnp.where(lane0, near_l[half], m))
            done.append((0.5 * (m + other)).reshape(64, 128))
        use(i, done)
        return pltpu.roll(left_c, 120, 1), pltpu.roll(right_c, 120, 1)

    lax.fori_loop(0, 9, one, (left_halo, right_halo))


def chunk_of(ref, i):
    return ref[pl.ds(i * 8, 8), :, :].reshape(64, 256)


def put_halves(ref, i, x):
    for half in range(2):
        at = pl.multiple_of(half * PTS + i * 64, 64)
        ref[pl.ds(at, 64), :] = x[:, half * 128 : (half + 1) * 128]


def dynamics_kernel(
    tracer_h, wind_x_h, wind_y_h, drops_h, counts_h, growth_h, collision_h, by_rows_h, by_cols_h, selector_h,
    row_map_h, col_map_h, cells_h, owner_h,
    state, cell_forcing, pair_coef, growth_col, start, counts_out, unsort, sender,
    tracer, wind_x, wind_y, drops, counts, growth, collision, by_rows, by_cols, selector,
    row_map, col_map, cells, owner,
    loads, field, total, packs, rows, got_packs, got_rows, send, recv,
):
    g, c, up, down, left, right = neighbours()
    barrier = pltpu.get_barrier_semaphore()
    around = [(up, c), (down, c)]
    around += [(r, s) for s in (left, right) for r in (g, up, down)]
    sources = [tracer_h, by_rows_h, by_cols_h, wind_x_h, wind_y_h, drops_h, counts_h, owner_h, collision_h,
               selector_h, growth_h, row_map_h, col_map_h, cells_h]
    targets = [tracer, by_rows, by_cols, wind_x, wind_y, drops, counts, owner, collision,
               selector, growth, row_map, col_map, cells]
    fetch = [
        pltpu.make_async_copy(source, target, loads.at[n])
        for n, (source, target) in enumerate(zip(sources, targets))
    ]
    for copy in fetch:
        copy.start()
    for to in around:
        pl.semaphore_signal(barrier, inc=1, device_id=to, device_id_type=MESH)
    for copy in fetch[0:5]:
        copy.wait()

    def first(n, _):
        for k in range(3):
            i = n * 3 + k
            put_halves(
                field, i,
                tendency(
                    chunk_of(tracer, i), chunk_of(wind_x, i), chunk_of(wind_y, i), by_rows[...], by_cols[...]
                ),
            )
        return 0

    lax.fori_loop(0, 3, first, 0)
    pack_edges(field, packs.at[0], rows.at[0])
    pl.semaphore_wait(barrier, 8)
    copies = halo_copies(packs.at[0], rows.at[0], got_packs.at[0], got_rows.at[0], send.at[0], recv.at[0])
    for copy in copies:
        copy.start()

    for copy in fetch[5:]:
        copy.wait()
    pair_coef[0:33, :] = jnp.dot(
        collision[...], selector[...], preferred_element_type=F32
    ).astype(BF)
    pair_coef[33:48, :] = jnp.zeros((15, PAIRS), BF)
    i0 = lax.broadcasted_iota(jnp.int32, (COLS, COLS), 0)
    i1 = lax.broadcasted_iota(jnp.int32, (COLS, COLS), 1)
    wide = jnp.concatenate([growth[...], jnp.zeros((1, COLS - BINS), F32)], axis=1)
    growth_col[...] = jnp.broadcast_to(
        jnp.sum(
            jnp.where((i0 == i1)[0:ROWS], jnp.broadcast_to(wide, (ROWS, COLS)), 0.0), axis=1, keepdims=True
        ),
        (ROWS, COLS),
    )
    across = jnp.broadcast_to(counts[...], (COLS, COLS)).astype(F32)
    along = jnp.sum(jnp.where(i0 == i1, across, 0.0), axis=1, keepdims=True)
    before = (across > along) | ((across == along) & (i1 < i0))
    place = jnp.sum(jnp.where(before, 1.0, 0.0), axis=1, keepdims=True).astype(jnp.int32)
    after = (along > across) | ((along == across) & (i0 < i1))
    place_row = jnp.sum(jnp.where(after, 1.0, 0.0), axis=0, keepdims=True).astype(jnp.int32)
    counts_out[...] = jnp.sum(jnp.where(place == i1, along, 0.0), axis=0, keepdims=True).astype(jnp.int32)
    unsort[...] = jnp.where(place == i1, 1.0, 0.0).astype(BF)
    sort = jnp.where(place_row == i0, 1.0, 0.0).astype(BF)
    for b in range(BINS):
        sorted_bin = jnp.dot(sort, drops[b], preferred_element_type=F32)
        for half in range(2):
            start[pl.ds(half * COLS * ROWS + b, COLS, stride=ROWS), :] = sorted_bin[
                :, half * 128 : (half + 1) * 128
            ]

    for b in range(BINS, ROWS):
        for half in range(2):
            start[pl.ds(half * COLS * ROWS + b, COLS, stride=ROWS), :] = jnp.zeros((COLS, 128), F32)
    owners = jnp.broadcast_to(owner[...], (COLS, COLS))
    owned = jnp.sum(jnp.where(i0 == i1, owners.astype(F32), 0.0), axis=1, keepdims=True)
    earlier = (owned == owners.astype(F32)) & (i0 < i1)
    turn = jnp.sum(jnp.where(earlier, 1.0, 0.0), axis=0, keepdims=True)
    key = owners % NC * NG + owners // NC
    sender[...] = jnp.concatenate(
        [jnp.where((key == i0) & (turn == float(r)), 1.0, 0.0) for r in range(2)], axis=1
    ).astype(BF)

    halo_wait(got_packs.at[0], got_rows.at[0], send.at[0], recv.at[0])

    def second(i, means):
        mean = jnp.concatenate(means, axis=1)
        moved = chunk_of(tracer, i) + DT_DYN * mean
        state[pl.ds(i * 8, 8), :, :] = moved.reshape(8, 8, 256)
        put_halves(total, i, mean)
        put_halves(
            field, i,
            tendency(moved, chunk_of(wind_x, i), chunk_of(wind_y, i), by_rows[...], by_cols[...]),
        )

    assemble_loop(field, got_packs.at[0], got_rows.at[0], second)
    pack_edges(field, packs.at[1], rows.at[1])
    copies = halo_copies(packs.at[1], rows.at[1], got_packs.at[1], got_rows.at[1], send.at[1], recv.at[1])
    for copy in copies:
        copy.start()
    halo_wait(got_packs.at[1], got_rows.at[1], send.at[1], recv.at[1])

    def third(i, means):
        mean = jnp.concatenate(means, axis=1)
        state[pl.ds(i * 8, 8), :, :] = (chunk_of(state, i) + DT_DYN * mean).reshape(8, 8, 256)
        for half in range(2):
            at = pl.multiple_of(half * PTS + i * 64, 64)
            total[pl.ds(at, 64), :] = total[pl.ds(at, 64), :] + means[half]

    assemble_loop(field, got_packs.at[1], got_rows.at[1], third)
    parts = [
        jnp.dot(row_map[...], total[half * PTS : (half + 1) * PTS, :], precision=HIGH, preferred_element_type=F32)
        for half in range(2)
    ]
    by_row = jnp.concatenate(parts, axis=1)
    forcing = [
        lax.dot_general(
            col_map[...], by_row[16 * e : 16 * (e + 1)], (((1,), (1,)), ((), ())),
            precision=HIGH, preferred_element_type=F32,
        ).astype(BF)
        for e in range(2)
    ]
    by_cell = jnp.dot(
        jnp.concatenate(forcing, axis=0), cells[...], preferred_element_type=F32
    ).astype(BF)
    cell_forcing[...] = DT_CRM * jnp.dot(sort, by_cell, preferred_element_type=F32)


def dynamics(tracer, wind_x, wind_y, drops, counts_row, growth_row, collision, owner_row):
    row_map, col_map = forcing_tables()
    by_rows, by_cols = stencil_tables()
    shape = tracer.shape
    operands = (
        tracer, wind_x, wind_y, drops, counts_row, growth_row, collision,
        jnp.asarray(by_rows), jnp.asarray(by_cols), jnp.asarray(pair_selector()),
        jnp.asarray(row_map), jnp.asarray(col_map), jnp.asarray(spread_cells()), owner_row,
    )
    return pl.pallas_call(
        dynamics_kernel,
        out_shape=(
            jax.ShapeDtypeStruct(shape, F32),
            jax.ShapeDtypeStruct((COLS, 256), F32),
            jax.ShapeDtypeStruct((48, PAIRS), BF),
            jax.ShapeDtypeStruct((ROWS, 128), F32),
            jax.ShapeDtypeStruct((2 * COLS * ROWS, 128), F32),
            jax.ShapeDtypeStruct((1, COLS), jnp.int32),
            jax.ShapeDtypeStruct((COLS, COLS), BF),
            jax.ShapeDtypeStruct((COLS, 2 * COLS), BF),
        ),
        in_specs=[HBM] * 14,
        out_specs=(VMEM,) * 8,
        scratch_shapes=[pltpu.VMEM(x.shape, x.dtype) for x in operands]
        + [
            pltpu.SemaphoreType.DMA((14,)),
            pltpu.VMEM((2 * PTS, 128), F32),
            pltpu.VMEM((2 * PTS, 128), F32),
            pltpu.VMEM((2, 2, 8, 128), F32),
            pltpu.VMEM((2, 2, 2 * LEV, 128), F32),
            pltpu.VMEM((2, 6, 8, 128), F32),
            pltpu.VMEM((2, 2, 2 * LEV, 128), F32),
            pltpu.SemaphoreType.DMA((2, 2)),
            pltpu.SemaphoreType.DMA((2, 2)),
        ],
        compiler_params=pltpu.CompilerParams(
            collective_id=0, has_side_effects=True, vmem_limit_bytes=40 << 20
        ),
        name="dynamics",
    )(*[pltpu.with_memory_space_constraint(x, pltpu.HBM) for x in operands])


def micro_kernel(
    counts, start, cell_forcing, pair_coef, growth, group, unsort,
    drops_next, heat_out, echo_out,
    cloud, doubled, grow, heat_rows, echo_rows, drops_out, stores,
):
    bins = lax.broadcasted_iota(jnp.int32, (ROWS, 128), 0)
    mass = jnp.where(bins < BINS, (bins.astype(F32) + 1.0) / BINS, 0.0)
    srow = lax.broadcasted_iota(jnp.int32, (8, 128), 0)

    def place(p, b, half):
        return pl.ds(pl.multiple_of((half * COLS + p * BATCH + b) * ROWS, 8), ROWS)

    def substep(s, p):
        for b in range(BATCH):
            active = s < counts[0, p * BATCH + b]
            blocks, grown, olds = [], [], []
            for half in range(2):
                old = cloud[place(p, b, half), :]
                now = old + grow[b, half]
                doubled[b, half, 0:32, :] = now[0:32]
                doubled[b, half, 32:48, :] = now[0:16]
                near, far = [], []
                for d in range(8):
                    shifted = doubled[b, half, d : d + 40, :]
                    near.append((now[0:32] * shifted[0:32]).astype(BF))
                    far.append((now[0:32] * shifted[8:40]).astype(BF))
                last = jnp.broadcast_to(now[32:33], (32, 128))
                rest = [
                    (now[0:16] * now[16:32]).astype(BF),
                    (now[0:32] * last).astype(BF),
                    (last[0:16] * last[0:16]).astype(BF),
                ]
                blocks.append(jnp.concatenate(near + far + rest, axis=0))
                grown.append(now)
                olds.append(old)
            change = jnp.dot(
                pair_coef[...], jnp.concatenate(blocks, axis=1), preferred_element_type=F32
            )
            for half in range(2):
                moved = grown[half] + DT_CRM * change[0:ROWS, half * 128 : (half + 1) * 128]
                cloud[place(p, b, half), :] = jnp.where(active, moved, olds[half])
        return p

    def batch(p, _):
        for b in range(BATCH):
            forced = cell_forcing[pl.ds(p * BATCH + b, 1), :]
            for half in range(2):
                cloud[place(p, b, half), :] = start[place(p, b, half), :]
                grow[b, half] = forced[:, half * 128 : (half + 1) * 128] * growth[...]
        lax.fori_loop(0, counts[0, p * BATCH], substep, p)
        for half in range(2):
            at = slice(half * 128, (half + 1) * 128)
            for eight in range(BATCH // 8):
                heats = jnp.zeros((8, 128), F32)
                echos = jnp.zeros((8, 128), F32)
                for b in range(8):
                    where = place(p, eight * 8 + b, half)
                    final = cloud[where, :]
                    gain = (final - start[where, :]) * mass
                    weighed = final * mass
                    square = weighed * weighed
                    heats = jnp.where(srow == b, jnp.sum(gain, axis=0, keepdims=True), heats)
                    echos = jnp.where(srow == b, jnp.sum(square, axis=0, keepdims=True), echos)
                rows = pl.ds(pl.multiple_of(p * BATCH + eight * 8, 8), 8)
                heat_rows[rows, at] = heats
                echo_rows[rows, at] = echos
        return 0

    lax.fori_loop(0, COLS // BATCH, batch, 0)

    def group_mean(x):
        acc = None
        for part in split3(x):
            y = jnp.dot(part, group[...], preferred_element_type=F32)
            acc = y if acc is None else acc + y
        return acc

    back = unsort[...]
    pieces = []
    for n in range(3):
        for b in range(11 * n, 11 * n + 11):
            halves = [cloud[pl.ds(half * COLS * ROWS + b, COLS, stride=ROWS), :] for half in range(2)]
            drops_out[b] = jnp.dot(
                back, jnp.concatenate(halves, axis=1).astype(BF), preferred_element_type=F32
            ).astype(BF)
        part = pl.ds(11 * n, 11)
        piece = pltpu.make_async_copy(drops_out.at[part], drops_next.at[part], stores.at[n])
        piece.start()
        pieces.append(piece)
    heat = group_mean(heat_rows[...]).astype(BF)
    heat_out[...] = jnp.dot(back, heat, preferred_element_type=F32).astype(BF)
    echo_out[...] = jnp.log(1.0 + dot_exact(back, group_mean(echo_rows[...])))
    for piece in pieces:
        piece.wait()


def microphysics(counts, start, cell_forcing, pair_coef, growth, unsort):
    return pl.pallas_call(
        micro_kernel,
        out_shape=(
            jax.ShapeDtypeStruct((BINS, COLS, 256), BF),
            jax.ShapeDtypeStruct((COLS, 128), BF),
            jax.ShapeDtypeStruct((COLS, 128), F32),
        ),
        in_specs=[SMEM] + [VMEM] * 6,
        out_specs=(HBM, VMEM, VMEM),
        scratch_shapes=[
            pltpu.VMEM((2 * COLS * ROWS, 128), F32),
            pltpu.VMEM((BATCH, 2, 48, 128), F32),
            pltpu.VMEM((BATCH, 2, ROWS, 128), F32),
            pltpu.VMEM((COLS, 256), F32),
            pltpu.VMEM((COLS, 256), F32),
            pltpu.VMEM((BINS, COLS, 256), BF),
            pltpu.SemaphoreType.DMA((3,)),
        ],
        compiler_params=pltpu.CompilerParams(vmem_limit_bytes=40 << 20),
        name="microphysics",
    )(counts, start, cell_forcing, pair_coef, growth, jnp.asarray(group_matrix()), unsort)


def coupling_kernel(
    state, heat, echo, sender, heating, spread, slots,
    tracer_next, power,
    field, packs, rows, got_packs, got_rows, sent, first_in, second_out, second_in,
    send, recv, power_send, power_recv,
):
    g, c, up, down, left, right = neighbours()
    barrier = pltpu.get_barrier_semaphore()
    peers = [(lax.rem(g + k, NG), c) for k in range(1, NG)]
    peers += [(g, lax.rem(c + k, NC)) for k in range(1, NC)]
    peers += [(r, s) for s in (left, right) for r in (up, down)]
    for to in peers:
        pl.semaphore_signal(barrier, inc=1, device_id=to, device_id_type=MESH)

    sums = echo[...]
    sums = jnp.concatenate([sums, pltpu.roll(sums, 16, 1)], axis=0)
    sent[...] = dot_exact(sender[...], sums).reshape(NC, NG, 128)
    pl.semaphore_wait(barrier, len(peers))
    for k in range(1, NC):
        to = lax.rem(c + k, NC)
        pltpu.make_async_remote_copy(
            src_ref=sent.at[to],
            dst_ref=first_in.at[c],
            send_sem=power_send.at[0],
            recv_sem=power_recv.at[0],
            device_id=(g, to),
            device_id_type=MESH,
        ).start()
    first_in[c] = sent[c]

    warm = []
    for e in range(2):
        turned = heat[64 * e : 64 * (e + 1), :].astype(F32).T.astype(BF)[0:16]
        warm.append(jnp.dot(turned, spread[...], preferred_element_type=F32).astype(BF))
    warm = jnp.concatenate(warm + warm, axis=0)
    for half in range(2):
        at = slice(half * 128, (half + 1) * 128)
        back = jnp.dot(heating[...], warm[:, at], preferred_element_type=F32)
        field[half * PTS : (half + 1) * PTS, :] = back + state[:, :, at].reshape(PTS, 128)
    pack_edges(field, packs, rows)
    for copy in halo_copies(packs, rows, got_packs, got_rows, send, recv):
        copy.start()

    for sems in (power_recv, power_send):
        wait_bytes(first_in.at[0 : NC - 1], sems.at[0])
    every = first_in[...]
    for to in range(NG):
        second_out[to] = every[:, to, :]
    for k in range(1, NG):
        to = lax.rem(g + k, NG)
        pltpu.make_async_remote_copy(
            src_ref=second_out.at[to],
            dst_ref=second_in.at[g],
            send_sem=power_send.at[1],
            recv_sem=power_recv.at[1],
            device_id=(to, c),
            device_id_type=MESH,
        ).start()
    second_in[g] = second_out[g]

    halo_wait(got_packs, got_rows, send, recv)

    def last(i, means):
        for half in range(2):
            tracer_next[pl.ds(i * 8, 8), :, half * 128 : (half + 1) * 128] = means[half].reshape(8, 8, 128)

    assemble_loop(field, got_packs, got_rows, last)

    for sems in (power_recv, power_send):
        wait_bytes(second_in.at[0 : NG - 1], sems.at[1])
    turned = second_in[...].reshape(COLS, 128).T
    turned = jnp.concatenate([turned[0:16], turned[16:32]], axis=1)
    acc = None
    for part in split3(turned):
        y = jnp.dot(part, slots[...], preferred_element_type=F32)
        acc = y if acc is None else acc + y
    power[...] = acc


def coupling(state, heat, echo, sender):
    return pl.pallas_call(
        coupling_kernel,
        out_shape=(
            jax.ShapeDtypeStruct(state.shape, F32),
            jax.ShapeDtypeStruct((CLEV, 256), F32),
        ),
        in_specs=[VMEM] * 7,
        out_specs=(VMEM,) * 2,
        scratch_shapes=[
            pltpu.VMEM((2 * PTS, 128), F32),
            pltpu.VMEM((2, 8, 128), F32),
            pltpu.VMEM((2, 2 * LEV, 128), F32),
            pltpu.VMEM((6, 8, 128), F32),
            pltpu.VMEM((2, 2 * LEV, 128), F32),
            pltpu.VMEM((NC, NG, 128), F32),
            pltpu.VMEM((NC, NG, 128), F32),
            pltpu.VMEM((NG, NC, 128), F32),
            pltpu.VMEM((NG, NC, 128), F32),
            pltpu.SemaphoreType.DMA((2,)),
            pltpu.SemaphoreType.DMA((2,)),
            pltpu.SemaphoreType.DMA((2,)),
            pltpu.SemaphoreType.DMA((2,)),
        ],
        compiler_params=pltpu.CompilerParams(
            collective_id=1, has_side_effects=True, vmem_limit_bytes=40 << 20
        ),
        name="coupling",
    )(
        state, heat, echo, sender,
        jnp.asarray(heating_table()), jnp.asarray(spread_columns()), jnp.asarray(slot_table()),
    )


def shards(tracer, wind_x, wind_y, drops, owner, counts, collision, growth):
    state, cell_forcing, pair_coef, growth_col, start, sorted_counts, unsort, sender = dynamics(
        tracer, wind_x, wind_y, drops.transpose(1, 0, 2),
        counts.reshape(1, COLS), growth.reshape(1, BINS), collision, owner.reshape(1, COLS),
    )
    drops_next, heat, echo = microphysics(
        sorted_counts, start, cell_forcing, pair_coef, growth_col, unsort
    )
    tracer_next, power = coupling(state, heat, echo, sender)
    return (tracer_next, drops_next.transpose(1, 0, 2), power)


def solution(mesh):
    return jax.shard_map(
        shards,
        mesh=mesh,
        in_specs=(
            P(None, "gcm", "crm"),
            P(None, "gcm", "crm"),
            P(None, "gcm", "crm"),
            P(("gcm", "crm"), None, None),
            P(("gcm", "crm"), None),
            P(("gcm", "crm")),
            P(),
            P(),
        ),
        out_specs=(P(None, "gcm", "crm"), P(("gcm", "crm"), None, None), P(None, ("gcm", "crm"))),
        check_vma=False,
    )
```

```python
import functools

import jax
import jax.numpy as jnp
import ml_dtypes
import numpy as np
from jax import lax
from jax.experimental import pallas as pl
from jax.experimental.pallas import tpu as pltpu
from jax.sharding import PartitionSpec as P

BF = jnp.bfloat16
F32 = jnp.float32
MESH = pl.DeviceIdType.MESH
HIGH = lax.Precision.HIGHEST
VMEM = pl.BlockSpec(memory_space=pltpu.VMEM)
SMEM = pl.BlockSpec(memory_space=pltpu.SMEM)
HBM = pl.BlockSpec(memory_space=pltpu.HBM)

NG = 8
NC = 16
LEV = 72
BINS = 33
CLEV = 16
COLS = 128
PTS = LEV * 8
PAIRS = 576
DT_DYN = 0.04
DT_CRM = 0.05
DT_PHYS = 0.5
BATCH = 32
ROWS = 40
EARLY = 3


def gll_tables():
    inv_root = 1.0 / np.sqrt(5.0)
    gll_nodes = np.array([-1.0, -inv_root, inv_root, 1.0])
    weights = np.array([1.0, 5.0, 5.0, 1.0]) / 6.0
    legendre = (5.0 * gll_nodes**3 - 3.0 * gll_nodes) / 2.0
    derivative = np.zeros((4, 4))
    for i in range(4):
        for j in range(4):
            if i != j:
                derivative[i, j] = legendre[i] / (legendre[j] * (gll_nodes[i] - gll_nodes[j]))
    derivative[0, 0] = -3.0
    derivative[3, 3] = 3.0
    return (2.0 * derivative, weights)


def level_tables(levels, crm_levels):
    spacing = levels / crm_levels
    centres = (np.arange(crm_levels) + 0.5) * spacing - 0.5
    hats = np.maximum(0.0, 1.0 - np.abs(np.arange(levels)[None, :] - centres[:, None]) / spacing)
    down_map = hats / hats.sum(axis=1, keepdims=True)
    up_map = hats.T / hats.T.sum(axis=1, keepdims=True)
    return (down_map, up_map)


def stencil_tables():
    derivative, _ = gll_tables()
    out = []
    for size in (64, 128):
        whole = np.kron(np.eye(size // 4), -derivative).astype(np.float32)
        if size == 128:
            whole = whole.T
        near = whole.astype(ml_dtypes.bfloat16)
        out += [near, (whole - near.astype(np.float32)).astype(ml_dtypes.bfloat16)]
    by_rows = np.concatenate([out[0], out[0], out[1]], axis=1)
    by_cols = np.block([[out[2], out[3]], [out[2], np.zeros_like(out[2])]])
    return by_rows, by_cols


def forcing_tables():
    _, weights = gll_tables()
    down_map, _ = level_tables(LEV, CLEV)
    rows = np.zeros((2, CLEV, LEV, 8))
    for r in range(8):
        rows[r // 4, :, :, r] = down_map * weights[r % 4] / 2.0 * 0.5
    cols = np.zeros((64, 256))
    for c in range(256):
        cols[c // 4, c] = weights[c % 4] / 2.0
    return rows.reshape(32, PTS).astype(np.float32), cols.astype(np.float32)


def spread_cells():
    out = np.zeros((CLEV, 256), np.float32)
    for c in range(256):
        out[c // 16, c] = 1.0
    return out.astype(ml_dtypes.bfloat16)


def group_matrix():
    out = np.zeros((256, 128), np.float32)
    for c in range(256):
        out[c, c // 16] = 1.0 / 16.0
    return out.astype(ml_dtypes.bfloat16)


def heating_table():
    _, up_map = level_tables(LEV, CLEV)
    half = (DT_PHYS * up_map).astype(np.float32)
    first = half.astype(ml_dtypes.bfloat16)
    second = (half - first.astype(np.float32)).astype(ml_dtypes.bfloat16)
    out = np.zeros((LEV, 8, 2, 2, CLEV), ml_dtypes.bfloat16)
    for r in range(8):
        out[:, r, 0, r // 4, :] = first
        out[:, r, 1, r // 4, :] = second
    return out.reshape(PTS, 64)


def spread_columns():
    out = np.zeros((64, 256), np.float32)
    for c in range(256):
        out[c // 4, c] = 1.0
    return out.astype(ml_dtypes.bfloat16)


def slot_table():
    out = np.zeros((2, 128, 256), np.float32)
    for d in range(128):
        for r in range(2):
            out[r, d, 2 * d + r] = 1.0
    return out.reshape(256, 256).astype(ml_dtypes.bfloat16)


def pair_list():
    out = []
    for d in range(16):
        for i in range(32):
            out.append((i, (i + d) % 32))
    for i in range(16):
        out.append((i, i + 16))
    for i in range(32):
        out.append((i, 32))
    out.append((32, 32))
    return out


def pair_selector():
    out = np.zeros((BINS * BINS, PAIRS), np.float32)
    for q, (i, j) in enumerate(pair_list()):
        out[i * BINS + j, q] = 1.0
        out[j * BINS + i, q] = 1.0
    return out.astype(ml_dtypes.bfloat16)


def pair_members():
    out = np.zeros((2, PAIRS, 128), np.float32)
    for q, pair in enumerate(pair_list()):
        for side in range(2):
            out[side, q, pair[side]] = 1.0
    return out.astype(ml_dtypes.bfloat16)


def split3(x):
    hi = x.astype(BF)
    rest = x - hi.astype(F32)
    mid = rest.astype(BF)
    return hi, mid, (rest - mid.astype(F32)).astype(BF)


def dot_exact(onehot, x):
    acc = None
    for part in split3(x):
        y = jnp.dot(onehot, part, preferred_element_type=F32)
        acc = y if acc is None else acc + y
    return acc


def tendency(q, wind_x, wind_y, by_rows, by_cols):
    near = q.astype(BF)
    rest = (q - near.astype(F32)).astype(BF)
    grad_x = jnp.dot(by_rows, jnp.concatenate([near, rest, near], axis=0), preferred_element_type=F32)
    grad_y = []
    for at in (slice(0, 128), slice(128, 256)):
        both = jnp.concatenate([near[:, at], rest[:, at]], axis=1)
        y = jnp.dot(both, by_cols, preferred_element_type=F32)
        grad_y.append(y[:, 0:128] + y[:, 128:256])
    return wind_x * grad_x + wind_y * jnp.concatenate(grad_y, axis=1)


def pairs_of(now, doubled):
    doubled[0:32, :] = now[0:32]
    doubled[32:48, :] = now[0:16]
    near, far = [], []
    for d in range(8):
        shifted = doubled[d : d + 40, :]
        near.append((now[0:32] * shifted[0:32]).astype(BF))
        far.append((now[0:32] * shifted[8:40]).astype(BF))
    last = jnp.broadcast_to(now[32:33], (32, 128))
    rest = [
        (now[0:16] * now[16:32]).astype(BF),
        (now[0:32] * last).astype(BF),
        (last[0:16] * last[0:16]).astype(BF),
    ]
    return jnp.concatenate(near + far + rest, axis=0)


def column_rows(col, half):
    return pl.ds(pl.multiple_of((half * COLS + col) * ROWS, 8), ROWS)


def neighbours():
    g = lax.axis_index("gcm")
    c = lax.axis_index("crm")
    up, down = lax.rem(g + NG - 1, NG), lax.rem(g + 1, NG)
    left, right = lax.rem(c + NC - 1, NC), lax.rem(c + 1, NC)
    return g, c, up, down, left, right


def pack_edges(field, packs, rows):
    lane = lax.broadcasted_iota(jnp.int32, (8, 128), 1)

    def one(i, carry):
        low, high = carry
        low, high = pltpu.roll(low, 120, 1), pltpu.roll(high, 120, 1)
        for k in range(8):
            at = pl.multiple_of(i * 64, 64) + 8 * k
            first, last = field[pl.ds(at, 8), :], field[pl.ds(PTS + at, 8), :]
            both = pltpu.roll(jnp.where(lane == 0, first, last), k + 1, 1)
            high = jnp.where(lane == k, both, high)
            low = jnp.where(lane == k + 1, both, low)
        return low, high

    zero = jnp.zeros((8, 128), F32)
    low, high = lax.fori_loop(0, 9, one, (zero, zero))
    packs[0] = pltpu.roll(low, 63, 1)
    packs[1] = pltpu.roll(high, 64, 1)
    for half in range(2):
        rows[0, half * LEV : (half + 1) * LEV, :] = field[pl.ds(half * PTS, LEV, stride=8), :]
        rows[1, half * LEV : (half + 1) * LEV, :] = field[pl.ds(half * PTS + 7, LEV, stride=8), :]


def halo_copies(packs, rows, got_packs, got_rows, send, recv):
    g, c, up, down, left, right = neighbours()
    plan = [
        (rows.at[1], got_rows.at[0], (down, c)),
        (rows.at[0], got_rows.at[1], (up, c)),
        (packs.at[1], got_packs.at[0], (g, right)),
        (packs.at[1], got_packs.at[1], (down, right)),
        (packs.at[1], got_packs.at[2], (up, right)),
        (packs.at[0], got_packs.at[3], (g, left)),
        (packs.at[0], got_packs.at[4], (down, left)),
        (packs.at[0], got_packs.at[5], (up, left)),
    ]
    return [
        pltpu.make_async_remote_copy(
            src_ref=src,
            dst_ref=dst,
            send_sem=send.at[0 if n < 2 else 1],
            recv_sem=recv.at[0 if n < 2 else 1],
            device_id=to,
            device_id_type=MESH,
        )
        for n, (src, dst, to) in enumerate(plan)
    ]


def wait_bytes(ref, sem):
    pltpu.make_async_copy(ref, ref, sem).wait()


def halo_wait(got_packs, got_rows, send, recv):
    for sems in (recv, send):
        wait_bytes(got_rows, sems.at[0])
        wait_bytes(got_packs, sems.at[1])


def assemble_loop(field, got_packs, got_rows, use):
    row = lax.broadcasted_iota(jnp.int32, (8, 128), 0)
    lane = lax.broadcasted_iota(jnp.int32, (8, 128), 1)

    def row_mean(x, above, below):
        up = jnp.where(row == 0, pltpu.roll(above, 1, 0), pltpu.roll(x, 1, 0))
        down = jnp.where(row == 7, pltpu.roll(below, 7, 0), pltpu.roll(x, 7, 0))
        other = jnp.where(row % 4 == 3, down, jnp.where(row % 4 == 0, up, x))
        return 0.5 * (x + other)

    left_halo = row_mean(got_packs[0], got_packs[1], got_packs[2])
    right_halo = row_mean(got_packs[3], got_packs[4], got_packs[5])
    edge_row = ((row == 0) | (row == 7))[None]
    upper = (row < 4)[None]
    is3, is4 = (row == 3)[None], (row == 4)[None]
    lane3, lane0 = (lane % 4 == 3)[None], (lane % 4 == 0)[None]
    first, last = (lane == 0)[None], (lane == 127)[None]

    def one(i, carry):
        left_c, right_c = carry
        means = []
        for half in range(2):
            at = pl.multiple_of(half * PTS + i * 64, 64)
            x = field[pl.ds(at, 64), :].reshape(8, 8, 128)
            lev = pl.multiple_of(half * LEV + i * 8, 8)
            above = jnp.broadcast_to(got_rows[0, pl.ds(lev, 8), :][:, None, :], (8, 8, 128))
            below = jnp.broadcast_to(got_rows[1, pl.ds(lev, 8), :][:, None, :], (8, 8, 128))
            other = jnp.where(is3, pltpu.roll(x, 7, 1), jnp.where(is4, pltpu.roll(x, 1, 1), x))
            other = jnp.where(edge_row, jnp.where(upper, above, below), other)
            means.append(0.5 * (x + other))
        lefts = [pltpu.roll(m, 1, 2) for m in means]
        rights = [pltpu.roll(m, 127, 2) for m in means]
        halo_l = jnp.stack([pltpu.roll(left_c, (128 - k) % 128, 1) if k else left_c for k in range(8)])
        halo_r = jnp.stack([pltpu.roll(right_c, 127 - k, 1) for k in range(8)])
        near_l = [jnp.where(first, halo_l, lefts[0]), jnp.where(first, lefts[0], lefts[1])]
        near_r = [jnp.where(last, rights[1], rights[0]), jnp.where(last, halo_r, rights[1])]
        done = []
        for half in range(2):
            m = means[half]
            other = jnp.where(lane3, near_r[half], jnp.where(lane0, near_l[half], m))
            done.append((0.5 * (m + other)).reshape(64, 128))
        use(i, done)
        return pltpu.roll(left_c, 120, 1), pltpu.roll(right_c, 120, 1)

    lax.fori_loop(0, 9, one, (left_halo, right_halo))


def chunk_of(ref, i):
    return ref[pl.ds(i * 8, 8), :, :].reshape(64, 256)


def put_halves(ref, i, x):
    for half in range(2):
        at = pl.multiple_of(half * PTS + i * 64, 64)
        ref[pl.ds(at, 64), :] = x[:, half * 128 : (half + 1) * 128]


def dynamics_kernel(
    tracer_h, wind_x_h, wind_y_h, drops_h, counts_h, growth_h, collision_h, by_rows_h, by_cols_h, selector_h,
    row_map_h, col_map_h, cells_h, owner_h, members_h,
    state, cell_forcing, pair_coef, growth_col, start, counts_out, unsort, sender, quadratic, linear, constant,
    tracer, wind_x, wind_y, drops, counts, growth, collision, by_rows, by_cols, selector,
    row_map, col_map, cells, owner, members, doubled,
    loads, field, total, packs, rows, got_packs, got_rows, send, recv,
):
    g, c, up, down, left, right = neighbours()
    barrier = pltpu.get_barrier_semaphore()
    around = [(up, c), (down, c)]
    around += [(r, s) for s in (left, right) for r in (g, up, down)]
    sources = [tracer_h, by_rows_h, by_cols_h, wind_x_h, wind_y_h, drops_h, counts_h, owner_h, collision_h,
               selector_h, growth_h, members_h, row_map_h, col_map_h, cells_h]
    targets = [tracer, by_rows, by_cols, wind_x, wind_y, drops, counts, owner, collision,
               selector, growth, members, row_map, col_map, cells]
    fetch = [
        pltpu.make_async_copy(source, target, loads.at[n])
        for n, (source, target) in enumerate(zip(sources, targets))
    ]
    for copy in fetch:
        copy.start()
    for to in around:
        pl.semaphore_signal(barrier, inc=1, device_id=to, device_id_type=MESH)
    for copy in fetch[0:5]:
        copy.wait()

    def first(n, _):
        for k in range(3):
            i = n * 3 + k
            put_halves(
                field, i,
                tendency(
                    chunk_of(tracer, i), chunk_of(wind_x, i), chunk_of(wind_y, i), by_rows[...], by_cols[...]
                ),
            )
        return 0

    lax.fori_loop(0, 3, first, 0)
    pack_edges(field, packs.at[0], rows.at[0])
    pl.semaphore_wait(barrier, 8)
    copies = halo_copies(packs.at[0], rows.at[0], got_packs.at[0], got_rows.at[0], send.at[0], recv.at[0])
    for copy in copies:
        copy.start()

    for copy in fetch[5:]:
        copy.wait()
    coef = jnp.dot(collision[...], selector[...], preferred_element_type=F32)
    coef = jnp.concatenate([coef, jnp.zeros((15, PAIRS), F32)], axis=0)
    pair_coef[...] = coef.astype(BF)
    i0 = lax.broadcasted_iota(jnp.int32, (COLS, COLS), 0)
    i1 = lax.broadcasted_iota(jnp.int32, (COLS, COLS), 1)
    wide = jnp.concatenate([growth[...], jnp.zeros((1, COLS - BINS), F32)], axis=1)
    growth_col[...] = jnp.broadcast_to(
        jnp.sum(
            jnp.where((i0 == i1)[0:ROWS], jnp.broadcast_to(wide, (ROWS, COLS)), 0.0), axis=1, keepdims=True
        ),
        (ROWS, COLS),
    )
    stacked = jnp.concatenate([jnp.broadcast_to(x.astype(F32), (16, COLS)) for x in split3(wide)], axis=0)
    slope = jnp.zeros((96, COLS), F32)
    for side in range(2):
        of_pair = lax.dot_general(
            stacked.astype(BF), members[side], (((1,), (1,)), ((), ())), preferred_element_type=F32
        )
        scaled = coef * (of_pair[0:1] + of_pair[16:17] + of_pair[32:33])
        near = scaled.astype(BF)
        terms = jnp.concatenate([near, (scaled - near.astype(F32)).astype(BF)], axis=0)
        slope = slope + jnp.dot(terms, members[1 - side], preferred_element_type=F32)
    slope = slope[0:48] + slope[48:96]
    constant[...] = jnp.broadcast_to(
        0.5 * jnp.sum(slope[0:ROWS] * wide, axis=1, keepdims=True), (ROWS, COLS)
    )
    near = slope.astype(BF)
    linear[...] = jnp.concatenate([near, (slope - near.astype(F32)).astype(BF)], axis=0)
    across = jnp.broadcast_to(counts[...], (COLS, COLS)).astype(F32)
    along = jnp.sum(jnp.where(i0 == i1, across, 0.0), axis=1, keepdims=True)
    before = (across > along) | ((across == along) & (i1 < i0))
    place = jnp.sum(jnp.where(before, 1.0, 0.0), axis=1, keepdims=True).astype(jnp.int32)
    after = (along > across) | ((along == across) & (i0 < i1))
    place_row = jnp.sum(jnp.where(after, 1.0, 0.0), axis=0, keepdims=True).astype(jnp.int32)
    counts_out[...] = jnp.sum(jnp.where(place == i1, along, 0.0), axis=0, keepdims=True).astype(jnp.int32)
    unsort[...] = jnp.where(place == i1, 1.0, 0.0).astype(BF)
    sort = jnp.where(place_row == i0, 1.0, 0.0).astype(BF)
    for b in range(BINS):
        sorted_bin = jnp.dot(sort, drops[b], preferred_element_type=F32)
        for half in range(2):
            start[pl.ds(half * COLS * ROWS + b, COLS, stride=ROWS), :] = sorted_bin[
                :, half * 128 : (half + 1) * 128
            ]

    for b in range(BINS, ROWS):
        for half in range(2):
            start[pl.ds(half * COLS * ROWS + b, COLS, stride=ROWS), :] = jnp.zeros((COLS, 128), F32)
    owners = jnp.broadcast_to(owner[...], (COLS, COLS))
    owned = jnp.sum(jnp.where(i0 == i1, owners.astype(F32), 0.0), axis=1, keepdims=True)
    earlier = (owned == owners.astype(F32)) & (i0 < i1)
    turn = jnp.sum(jnp.where(earlier, 1.0, 0.0), axis=0, keepdims=True)
    key = owners % NC * NG + owners // NC
    sender[...] = jnp.concatenate(
        [jnp.where((key == i0) & (turn == float(r)), 1.0, 0.0) for r in range(2)], axis=1
    ).astype(BF)

    def square(p, _):
        for b in range(16):
            blocks = [
                pairs_of(start[column_rows(p * 16 + b, half), :], doubled.at[b, half]) for half in range(2)
            ]
            found = jnp.dot(pair_coef[...], jnp.concatenate(blocks, axis=1), preferred_element_type=F32)
            for half in range(2):
                quadratic[column_rows(p * 16 + b, half), :] = found[0:ROWS, half * 128 : (half + 1) * 128]
        return 0

    lax.fori_loop(0, EARLY, square, 0)
    halo_wait(got_packs.at[0], got_rows.at[0], send.at[0], recv.at[0])

    def second(i, means):
        mean = jnp.concatenate(means, axis=1)
        moved = chunk_of(tracer, i) + DT_DYN * mean
        state[pl.ds(i * 8, 8), :, :] = moved.reshape(8, 8, 256)
        put_halves(total, i, mean)
        put_halves(
            field, i,
            tendency(moved, chunk_of(wind_x, i), chunk_of(wind_y, i), by_rows[...], by_cols[...]),
        )

    assemble_loop(field, got_packs.at[0], got_rows.at[0], second)
    pack_edges(field, packs.at[1], rows.at[1])
    copies = halo_copies(packs.at[1], rows.at[1], got_packs.at[1], got_rows.at[1], send.at[1], recv.at[1])
    for copy in copies:
        copy.start()
    lax.fori_loop(EARLY, COLS // 16, square, 0)
    halo_wait(got_packs.at[1], got_rows.at[1], send.at[1], recv.at[1])

    def third(i, means):
        mean = jnp.concatenate(means, axis=1)
        state[pl.ds(i * 8, 8), :, :] = (chunk_of(state, i) + DT_DYN * mean).reshape(8, 8, 256)
        for half in range(2):
            at = pl.multiple_of(half * PTS + i * 64, 64)
            total[pl.ds(at, 64), :] = total[pl.ds(at, 64), :] + means[half]

    assemble_loop(field, got_packs.at[1], got_rows.at[1], third)
    parts = [
        jnp.dot(row_map[...], total[half * PTS : (half + 1) * PTS, :], precision=HIGH, preferred_element_type=F32)
        for half in range(2)
    ]
    by_row = jnp.concatenate(parts, axis=1)
    forcing = [
        lax.dot_general(
            col_map[...], by_row[16 * e : 16 * (e + 1)], (((1,), (1,)), ((), ())),
            precision=HIGH, preferred_element_type=F32,
        ).astype(BF)
        for e in range(2)
    ]
    by_cell = jnp.dot(
        jnp.concatenate(forcing, axis=0), cells[...], preferred_element_type=F32
    ).astype(BF)
    cell_forcing[...] = DT_CRM * jnp.dot(sort, by_cell, preferred_element_type=F32)


def dynamics(tracer, wind_x, wind_y, drops, counts_row, growth_row, collision, owner_row):
    row_map, col_map = forcing_tables()
    by_rows, by_cols = stencil_tables()
    shape = tracer.shape
    operands = (
        tracer, wind_x, wind_y, drops, counts_row, growth_row, collision,
        jnp.asarray(by_rows), jnp.asarray(by_cols), jnp.asarray(pair_selector()),
        jnp.asarray(row_map), jnp.asarray(col_map), jnp.asarray(spread_cells()), owner_row,
        jnp.asarray(pair_members()),
    )
    return pl.pallas_call(
        dynamics_kernel,
        out_shape=(
            jax.ShapeDtypeStruct(shape, F32),
            jax.ShapeDtypeStruct((COLS, 256), F32),
            jax.ShapeDtypeStruct((48, PAIRS), BF),
            jax.ShapeDtypeStruct((ROWS, 128), F32),
            jax.ShapeDtypeStruct((2 * COLS * ROWS, 128), F32),
            jax.ShapeDtypeStruct((1, COLS), jnp.int32),
            jax.ShapeDtypeStruct((COLS, COLS), BF),
            jax.ShapeDtypeStruct((COLS, 2 * COLS), BF),
            jax.ShapeDtypeStruct((2 * COLS * ROWS, 128), F32),
            jax.ShapeDtypeStruct((96, 128), BF),
            jax.ShapeDtypeStruct((ROWS, 128), F32),
        ),
        in_specs=[HBM] * 15,
        out_specs=(VMEM,) * 11,
        scratch_shapes=[pltpu.VMEM(x.shape, x.dtype) for x in operands]
        + [
            pltpu.VMEM((16, 2, 48, 128), F32),
            pltpu.SemaphoreType.DMA((15,)),
            pltpu.VMEM((2 * PTS, 128), F32),
            pltpu.VMEM((2 * PTS, 128), F32),
            pltpu.VMEM((2, 2, 8, 128), F32),
            pltpu.VMEM((2, 2, 2 * LEV, 128), F32),
            pltpu.VMEM((2, 6, 8, 128), F32),
            pltpu.VMEM((2, 2, 2 * LEV, 128), F32),
            pltpu.SemaphoreType.DMA((2, 2)),
            pltpu.SemaphoreType.DMA((2, 2)),
        ],
        compiler_params=pltpu.CompilerParams(
            collective_id=0, has_side_effects=True, vmem_limit_bytes=40 << 20
        ),
        name="dynamics",
    )(*[pltpu.with_memory_space_constraint(x, pltpu.HBM) for x in operands])


def micro_kernel(
    counts, start, cell_forcing, pair_coef, growth, group, unsort, quadratic, linear, constant,
    drops_next, heat_out, echo_out,
    cloud, doubled, grow, heat_rows, echo_rows, drops_out, stores,
):
    bins = lax.broadcasted_iota(jnp.int32, (ROWS, 128), 0)
    mass = jnp.where(bins < BINS, (bins.astype(F32) + 1.0) / BINS, 0.0)
    srow = lax.broadcasted_iota(jnp.int32, (8, 128), 0)

    def place(p, b, half):
        return column_rows(p * BATCH + b, half)

    def substep(s, p):
        for b in range(BATCH):
            active = s < counts[0, p * BATCH + b]
            olds = [cloud[place(p, b, half), :] for half in range(2)]
            grown = [olds[half] + grow[b, half] for half in range(2)]
            blocks = [pairs_of(grown[half], doubled.at[b, half]) for half in range(2)]
            change = jnp.dot(
                pair_coef[...], jnp.concatenate(blocks, axis=1), preferred_element_type=F32
            )
            for half in range(2):
                moved = grown[half] + DT_CRM * change[0:ROWS, half * 128 : (half + 1) * 128]
                cloud[place(p, b, half), :] = jnp.where(active, moved, olds[half])
        return p

    def batch(p, _):
        for b in range(BATCH):
            active = counts[0, p * BATCH + b] > 0
            forced = cell_forcing[pl.ds(p * BATCH + b, 1), :]
            olds = [start[place(p, b, half), :] for half in range(2)]
            rows = [jnp.concatenate([old, old[0:8]], axis=0).astype(BF) for old in olds]
            sloped = jnp.dot(linear[:, 0:48], jnp.concatenate(rows, axis=1), preferred_element_type=F32)
            for half in range(2):
                at = slice(half * 128, (half + 1) * 128)
                f = forced[:, at]
                add = f * growth[...]
                change = quadratic[place(p, b, half), :] + f * (
                    sloped[0:ROWS, at] + sloped[48 : 48 + ROWS, at] + f * constant[...]
                )
                grow[b, half] = add
                moved = olds[half] + add + DT_CRM * change
                cloud[place(p, b, half), :] = jnp.where(active, moved, olds[half])
        lax.fori_loop(1, counts[0, p * BATCH], substep, p)
        for half in range(2):
            at = slice(half * 128, (half + 1) * 128)
            for eight in range(BATCH // 8):
                heats = jnp.zeros((8, 128), F32)
                echos = jnp.zeros((8, 128), F32)
                for b in range(8):
                    where = place(p, eight * 8 + b, half)
                    final = cloud[where, :]
                    gain = (final - start[where, :]) * mass
                    weighed = final * mass
                    square = weighed * weighed
                    heats = jnp.where(srow == b, jnp.sum(gain, axis=0, keepdims=True), heats)
                    echos = jnp.where(srow == b, jnp.sum(square, axis=0, keepdims=True), echos)
                rows = pl.ds(pl.multiple_of(p * BATCH + eight * 8, 8), 8)
                heat_rows[rows, at] = heats
                echo_rows[rows, at] = echos
        return 0

    lax.fori_loop(0, COLS // BATCH, batch, 0)

    def group_mean(x):
        acc = None
        for part in split3(x):
            y = jnp.dot(part, group[...], preferred_element_type=F32)
            acc = y if acc is None else acc + y
        return acc

    back = unsort[...]
    pieces = []
    for n in range(3):
        for b in range(11 * n, 11 * n + 11):
            halves = [cloud[pl.ds(half * COLS * ROWS + b, COLS, stride=ROWS), :] for half in range(2)]
            drops_out[b] = jnp.dot(
                back, jnp.concatenate(halves, axis=1).astype(BF), preferred_element_type=F32
            ).astype(BF)
        part = pl.ds(11 * n, 11)
        piece = pltpu.make_async_copy(drops_out.at[part], drops_next.at[part], stores.at[n])
        piece.start()
        pieces.append(piece)
    heat = group_mean(heat_rows[...]).astype(BF)
    heat_out[...] = jnp.dot(back, heat, preferred_element_type=F32).astype(BF)
    echo_out[...] = jnp.log(1.0 + dot_exact(back, group_mean(echo_rows[...])))
    for piece in pieces:
        piece.wait()


def microphysics(counts, start, cell_forcing, pair_coef, growth, unsort, quadratic, linear, constant):
    return pl.pallas_call(
        micro_kernel,
        out_shape=(
            jax.ShapeDtypeStruct((BINS, COLS, 256), BF),
            jax.ShapeDtypeStruct((COLS, 128), BF),
            jax.ShapeDtypeStruct((COLS, 128), F32),
        ),
        in_specs=[SMEM] + [VMEM] * 9,
        out_specs=(HBM, VMEM, VMEM),
        scratch_shapes=[
            pltpu.VMEM((2 * COLS * ROWS, 128), F32),
            pltpu.VMEM((BATCH, 2, 48, 128), F32),
            pltpu.VMEM((BATCH, 2, ROWS, 128), F32),
            pltpu.VMEM((COLS, 256), F32),
            pltpu.VMEM((COLS, 256), F32),
            pltpu.VMEM((BINS, COLS, 256), BF),
            pltpu.SemaphoreType.DMA((3,)),
        ],
        compiler_params=pltpu.CompilerParams(vmem_limit_bytes=40 << 20),
        name="microphysics",
    )(
        counts, start, cell_forcing, pair_coef, growth, jnp.asarray(group_matrix()), unsort,
        quadratic, linear, constant,
    )


def coupling_kernel(
    state, heat, echo, sender, heating, spread, slots,
    tracer_next, power,
    field, packs, rows, got_packs, got_rows, sent, first_in, second_out, second_in,
    send, recv, power_send, power_recv,
):
    g, c, up, down, left, right = neighbours()
    barrier = pltpu.get_barrier_semaphore()
    peers = [(lax.rem(g + k, NG), c) for k in range(1, NG)]
    peers += [(g, lax.rem(c + k, NC)) for k in range(1, NC)]
    peers += [(r, s) for s in (left, right) for r in (up, down)]
    for to in peers:
        pl.semaphore_signal(barrier, inc=1, device_id=to, device_id_type=MESH)

    sums = echo[...]
    sums = jnp.concatenate([sums, pltpu.roll(sums, 16, 1)], axis=0)
    sent[...] = dot_exact(sender[...], sums).reshape(NC, NG, 128)
    pl.semaphore_wait(barrier, len(peers))
    for k in range(1, NC):
        to = lax.rem(c + k, NC)
        pltpu.make_async_remote_copy(
            src_ref=sent.at[to],
            dst_ref=first_in.at[c],
            send_sem=power_send.at[0],
            recv_sem=power_recv.at[0],
            device_id=(g, to),
            device_id_type=MESH,
        ).start()
    first_in[c] = sent[c]

    warm = []
    for e in range(2):
        turned = heat[64 * e : 64 * (e + 1), :].astype(F32).T.astype(BF)[0:16]
        warm.append(jnp.dot(turned, spread[...], preferred_element_type=F32).astype(BF))
    warm = jnp.concatenate(warm + warm, axis=0)
    for half in range(2):
        at = slice(half * 128, (half + 1) * 128)
        back = jnp.dot(heating[...], warm[:, at], preferred_element_type=F32)
        field[half * PTS : (half + 1) * PTS, :] = back + state[:, :, at].reshape(PTS, 128)
    pack_edges(field, packs, rows)
    for copy in halo_copies(packs, rows, got_packs, got_rows, send, recv):
        copy.start()

    for sems in (power_recv, power_send):
        wait_bytes(first_in.at[0 : NC - 1], sems.at[0])
    every = first_in[...]
    for to in range(NG):
        second_out[to] = every[:, to, :]
    for k in range(1, NG):
        to = lax.rem(g + k, NG)
        pltpu.make_async_remote_copy(
            src_ref=second_out.at[to],
            dst_ref=second_in.at[g],
            send_sem=power_send.at[1],
            recv_sem=power_recv.at[1],
            device_id=(to, c),
            device_id_type=MESH,
        ).start()
    second_in[g] = second_out[g]

    halo_wait(got_packs, got_rows, send, recv)

    def last(i, means):
        for half in range(2):
            tracer_next[pl.ds(i * 8, 8), :, half * 128 : (half + 1) * 128] = means[half].reshape(8, 8, 128)

    assemble_loop(field, got_packs, got_rows, last)

    for sems in (power_recv, power_send):
        wait_bytes(second_in.at[0 : NG - 1], sems.at[1])
    turned = second_in[...].reshape(COLS, 128).T
    turned = jnp.concatenate([turned[0:16], turned[16:32]], axis=1)
    acc = None
    for part in split3(turned):
        y = jnp.dot(part, slots[...], preferred_element_type=F32)
        acc = y if acc is None else acc + y
    power[...] = acc


def coupling(state, heat, echo, sender):
    return pl.pallas_call(
        coupling_kernel,
        out_shape=(
            jax.ShapeDtypeStruct(state.shape, F32),
            jax.ShapeDtypeStruct((CLEV, 256), F32),
        ),
        in_specs=[VMEM] * 7,
        out_specs=(VMEM,) * 2,
        scratch_shapes=[
            pltpu.VMEM((2 * PTS, 128), F32),
            pltpu.VMEM((2, 8, 128), F32),
            pltpu.VMEM((2, 2 * LEV, 128), F32),
            pltpu.VMEM((6, 8, 128), F32),
            pltpu.VMEM((2, 2 * LEV, 128), F32),
            pltpu.VMEM((NC, NG, 128), F32),
            pltpu.VMEM((NC, NG, 128), F32),
            pltpu.VMEM((NG, NC, 128), F32),
            pltpu.VMEM((NG, NC, 128), F32),
            pltpu.SemaphoreType.DMA((2,)),
            pltpu.SemaphoreType.DMA((2,)),
            pltpu.SemaphoreType.DMA((2,)),
            pltpu.SemaphoreType.DMA((2,)),
        ],
        compiler_params=pltpu.CompilerParams(
            collective_id=1, has_side_effects=True, vmem_limit_bytes=40 << 20
        ),
        name="coupling",
    )(
        state, heat, echo, sender,
        jnp.asarray(heating_table()), jnp.asarray(spread_columns()), jnp.asarray(slot_table()),
    )


def shards(tracer, wind_x, wind_y, drops, owner, counts, collision, growth):
    state, cell_forcing, pair_coef, growth_col, start, sorted_counts, unsort, sender, quadratic, linear, constant = dynamics(
        tracer, wind_x, wind_y, drops.transpose(1, 0, 2),
        counts.reshape(1, COLS), growth.reshape(1, BINS), collision, owner.reshape(1, COLS),
    )
    drops_next, heat, echo = microphysics(
        sorted_counts, start, cell_forcing, pair_coef, growth_col, unsort, quadratic, linear, constant
    )
    tracer_next, power = coupling(state, heat, echo, sender)
    return (tracer_next, drops_next.transpose(1, 0, 2), power)


def solution(mesh):
    return jax.shard_map(
        shards,
        mesh=mesh,
        in_specs=(
            P(None, "gcm", "crm"),
            P(None, "gcm", "crm"),
            P(None, "gcm", "crm"),
            P(("gcm", "crm"), None, None),
            P(("gcm", "crm"), None),
            P(("gcm", "crm")),
            P(),
            P(),
        ),
        out_specs=(P(None, "gcm", "crm"), P(("gcm", "crm"), None, None), P(None, ("gcm", "crm"))),
        check_vma=False,
    )
```

```python
import functools

import jax
import jax.numpy as jnp
import ml_dtypes
import numpy as np
from jax import lax
from jax.experimental import pallas as pl
from jax.experimental.pallas import tpu as pltpu
from jax.sharding import PartitionSpec as P

BF = jnp.bfloat16
F32 = jnp.float32
MESH = pl.DeviceIdType.MESH
HIGH = lax.Precision.HIGHEST
VMEM = pl.BlockSpec(memory_space=pltpu.VMEM)
SMEM = pl.BlockSpec(memory_space=pltpu.SMEM)
HBM = pl.BlockSpec(memory_space=pltpu.HBM)

NG = 8
NC = 16
LEV = 72
BINS = 33
CLEV = 16
COLS = 128
PTS = LEV * 8
PAIRS = 576
DT_DYN = 0.04
DT_CRM = 0.05
DT_PHYS = 0.5
BATCH = 32
ROWS = 40
EARLY = 1


def gll_tables():
    inv_root = 1.0 / np.sqrt(5.0)
    gll_nodes = np.array([-1.0, -inv_root, inv_root, 1.0])
    weights = np.array([1.0, 5.0, 5.0, 1.0]) / 6.0
    legendre = (5.0 * gll_nodes**3 - 3.0 * gll_nodes) / 2.0
    derivative = np.zeros((4, 4))
    for i in range(4):
        for j in range(4):
            if i != j:
                derivative[i, j] = legendre[i] / (legendre[j] * (gll_nodes[i] - gll_nodes[j]))
    derivative[0, 0] = -3.0
    derivative[3, 3] = 3.0
    return (2.0 * derivative, weights)


def level_tables(levels, crm_levels):
    spacing = levels / crm_levels
    centres = (np.arange(crm_levels) + 0.5) * spacing - 0.5
    hats = np.maximum(0.0, 1.0 - np.abs(np.arange(levels)[None, :] - centres[:, None]) / spacing)
    down_map = hats / hats.sum(axis=1, keepdims=True)
    up_map = hats.T / hats.T.sum(axis=1, keepdims=True)
    return (down_map, up_map)


def stencil_tables():
    derivative, _ = gll_tables()
    out = []
    for size in (64, 128):
        whole = np.kron(np.eye(size // 4), -derivative).astype(np.float32)
        if size == 128:
            whole = whole.T
        near = whole.astype(ml_dtypes.bfloat16)
        out += [near, (whole - near.astype(np.float32)).astype(ml_dtypes.bfloat16)]
    by_rows = np.concatenate([out[0], out[0], out[1]], axis=1)
    by_cols = np.block([[out[2], out[3]], [out[2], np.zeros_like(out[2])]])
    return by_rows, by_cols


def forcing_tables():
    _, weights = gll_tables()
    down_map, _ = level_tables(LEV, CLEV)
    rows = np.zeros((2, CLEV, LEV, 8))
    for r in range(8):
        rows[r // 4, :, :, r] = down_map * weights[r % 4] / 2.0 * 0.5
    cols = np.zeros((64, 256))
    for c in range(256):
        cols[c // 4, c] = weights[c % 4] / 2.0
    return rows.reshape(32, PTS).astype(np.float32), cols.astype(np.float32)


def spread_cells():
    out = np.zeros((CLEV, 256), np.float32)
    for c in range(256):
        out[c // 16, c] = 1.0
    return out.astype(ml_dtypes.bfloat16)


def group_matrix():
    out = np.zeros((256, 128), np.float32)
    for c in range(256):
        out[c, c // 16] = 1.0 / 16.0
    return out.astype(ml_dtypes.bfloat16)


def heating_table():
    _, up_map = level_tables(LEV, CLEV)
    half = (DT_PHYS * up_map).astype(np.float32)
    first = half.astype(ml_dtypes.bfloat16)
    second = (half - first.astype(np.float32)).astype(ml_dtypes.bfloat16)
    out = np.zeros((LEV, 8, 2, 2, CLEV), ml_dtypes.bfloat16)
    for r in range(8):
        out[:, r, 0, r // 4, :] = first
        out[:, r, 1, r // 4, :] = second
    return out.reshape(PTS, 64)


def spread_columns():
    out = np.zeros((64, 256), np.float32)
    for c in range(256):
        out[c // 4, c] = 1.0
    return out.astype(ml_dtypes.bfloat16)


def slot_table():
    out = np.zeros((2, 128, 256), np.float32)
    for d in range(128):
        for r in range(2):
            out[r, d, 2 * d + r] = 1.0
    return out.reshape(256, 256).astype(ml_dtypes.bfloat16)


def pair_list():
    out = []
    for back in (0, 8):
        for d in range(8):
            for i in range(32):
                out.append(((i - back) % 32, (i + d) % 32))
    for i in range(16):
        out.append((i, i + 16))
    for i in range(32):
        out.append((i, 32))
    out.append((32, 32))
    return out


def pair_selector():
    out = np.zeros((BINS * BINS, PAIRS), np.float32)
    for q, (i, j) in enumerate(pair_list()):
        out[i * BINS + j, q] = 1.0
        out[j * BINS + i, q] = 1.0
    return out.astype(ml_dtypes.bfloat16)


def pair_members():
    out = np.zeros((2, PAIRS, 128), np.float32)
    for q, pair in enumerate(pair_list()):
        for side in range(2):
            out[side, q, pair[side]] = 1.0
    return out.astype(ml_dtypes.bfloat16)


def split3(x):
    hi = x.astype(BF)
    rest = x - hi.astype(F32)
    mid = rest.astype(BF)
    return hi, mid, (rest - mid.astype(F32)).astype(BF)


def dot_exact(onehot, x):
    acc = None
    for part in split3(x):
        y = jnp.dot(onehot, part, preferred_element_type=F32)
        acc = y if acc is None else acc + y
    return acc


def tendency(q, wind_x, wind_y, by_rows, by_cols):
    near = q.astype(BF)
    rest = (q - near.astype(F32)).astype(BF)
    grad_x = jnp.dot(by_rows, jnp.concatenate([near, rest, near], axis=0), preferred_element_type=F32)
    grad_y = []
    for at in (slice(0, 128), slice(128, 256)):
        both = jnp.concatenate([near[:, at], rest[:, at]], axis=1)
        y = jnp.dot(both, by_cols, preferred_element_type=F32)
        grad_y.append(y[:, 0:128] + y[:, 128:256])
    return wind_x * grad_x + wind_y * jnp.concatenate(grad_y, axis=1)


def pairs_of(grown, doubled):
    for half in range(2):
        doubled[half, 0:32, :] = grown[half][0:32]
        doubled[half, 32:40, :] = grown[half][0:8]

    def beside(parts):
        return jnp.concatenate(parts, axis=1)

    here = beside([now[0:32].astype(BF) for now in grown])
    behind = beside([jnp.concatenate([now[24:32], now[0:24]], axis=0).astype(BF) for now in grown])
    ahead = [beside([doubled[half, d : d + 32, :].astype(BF) for half in range(2)]) for d in range(8)]
    last = beside([jnp.broadcast_to(now[32:33], (32, 128)).astype(BF) for now in grown])
    rows = [here * x for x in ahead] + [behind * x for x in ahead]
    rows += [here[0:16] * here[16:32], here * last, last[0:16] * last[0:16]]
    return jnp.concatenate(rows, axis=0)


def rows_of_sums(blocks):
    row = lax.broadcasted_iota(jnp.int32, (8, 128), 0)
    for step in (4, 2, 1):
        mine = row % (2 * step) < step
        merged = []
        for k in range(step):
            a, b = blocks[k], blocks[k + step]
            other = jnp.where(mine, b, a)
            if step == 4:
                moved = pltpu.roll(other, 4, 0)
            else:
                moved = jnp.where(mine, pltpu.roll(other, 8 - step, 0), pltpu.roll(other, step, 0))
            merged.append(jnp.where(mine, a, b) + moved)
        blocks = merged
    return blocks[0]


def column_rows(col, half):
    return pl.ds(pl.multiple_of((half * COLS + col) * ROWS, 8), ROWS)


def neighbours():
    g = lax.axis_index("gcm")
    c = lax.axis_index("crm")
    up, down = lax.rem(g + NG - 1, NG), lax.rem(g + 1, NG)
    left, right = lax.rem(c + NC - 1, NC), lax.rem(c + 1, NC)
    return g, c, up, down, left, right


def pack_edges(field, packs, rows):
    lane = lax.broadcasted_iota(jnp.int32, (8, 128), 1)

    def one(i, carry):
        low, high = carry
        low, high = pltpu.roll(low, 120, 1), pltpu.roll(high, 120, 1)
        for k in range(8):
            at = pl.multiple_of(i * 64, 64) + 8 * k
            first, last = field[pl.ds(at, 8), :], field[pl.ds(PTS + at, 8), :]
            both = pltpu.roll(jnp.where(lane == 0, first, last), k + 1, 1)
            high = jnp.where(lane == k, both, high)
            low = jnp.where(lane == k + 1, both, low)
        return low, high

    zero = jnp.zeros((8, 128), F32)
    low, high = lax.fori_loop(0, 9, one, (zero, zero))
    packs[0] = pltpu.roll(low, 63, 1)
    packs[1] = pltpu.roll(high, 64, 1)
    for half in range(2):
        rows[0, half * LEV : (half + 1) * LEV, :] = field[pl.ds(half * PTS, LEV, stride=8), :]
        rows[1, half * LEV : (half + 1) * LEV, :] = field[pl.ds(half * PTS + 7, LEV, stride=8), :]


def halo_copies(packs, rows, got_packs, got_rows, send, recv):
    g, c, up, down, left, right = neighbours()
    plan = [
        (rows.at[1], got_rows.at[0], (down, c)),
        (rows.at[0], got_rows.at[1], (up, c)),
        (packs.at[1], got_packs.at[0], (g, right)),
        (packs.at[1], got_packs.at[1], (down, right)),
        (packs.at[1], got_packs.at[2], (up, right)),
        (packs.at[0], got_packs.at[3], (g, left)),
        (packs.at[0], got_packs.at[4], (down, left)),
        (packs.at[0], got_packs.at[5], (up, left)),
    ]
    return [
        pltpu.make_async_remote_copy(
            src_ref=src,
            dst_ref=dst,
            send_sem=send.at[0 if n < 2 else 1],
            recv_sem=recv.at[0 if n < 2 else 1],
            device_id=to,
            device_id_type=MESH,
        )
        for n, (src, dst, to) in enumerate(plan)
    ]


def wait_bytes(ref, sem):
    pltpu.make_async_copy(ref, ref, sem).wait()


def halo_wait(got_packs, got_rows, send, recv):
    for sems in (recv, send):
        wait_bytes(got_rows, sems.at[0])
        wait_bytes(got_packs, sems.at[1])


def assemble_loop(field, got_packs, got_rows, use):
    row = lax.broadcasted_iota(jnp.int32, (8, 128), 0)
    lane = lax.broadcasted_iota(jnp.int32, (8, 128), 1)

    def row_mean(x, above, below):
        up = jnp.where(row == 0, pltpu.roll(above, 1, 0), pltpu.roll(x, 1, 0))
        down = jnp.where(row == 7, pltpu.roll(below, 7, 0), pltpu.roll(x, 7, 0))
        other = jnp.where(row % 4 == 3, down, jnp.where(row % 4 == 0, up, x))
        return 0.5 * (x + other)

    left_halo = row_mean(got_packs[0], got_packs[1], got_packs[2])
    right_halo = row_mean(got_packs[3], got_packs[4], got_packs[5])
    edge_row = ((row == 0) | (row == 7))[None]
    upper = (row < 4)[None]
    is3, is4 = (row == 3)[None], (row == 4)[None]
    lane3, lane0 = (lane % 4 == 3)[None], (lane % 4 == 0)[None]
    first, last = (lane == 0)[None], (lane == 127)[None]

    def one(i, carry):
        left_c, right_c = carry
        means = []
        for half in range(2):
            at = pl.multiple_of(half * PTS + i * 64, 64)
            x = field[pl.ds(at, 64), :].reshape(8, 8, 128)
            lev = pl.multiple_of(half * LEV + i * 8, 8)
            above = jnp.broadcast_to(got_rows[0, pl.ds(lev, 8), :][:, None, :], (8, 8, 128))
            below = jnp.broadcast_to(got_rows[1, pl.ds(lev, 8), :][:, None, :], (8, 8, 128))
            other = jnp.where(is3, pltpu.roll(x, 7, 1), jnp.where(is4, pltpu.roll(x, 1, 1), x))
            other = jnp.where(edge_row, jnp.where(upper, above, below), other)
            means.append(0.5 * (x + other))
        lefts = [pltpu.roll(m, 1, 2) for m in means]
        rights = [pltpu.roll(m, 127, 2) for m in means]
        halo_l = jnp.stack([pltpu.roll(left_c, (128 - k) % 128, 1) if k else left_c for k in range(8)])
        halo_r = jnp.stack([pltpu.roll(right_c, 127 - k, 1) for k in range(8)])
        near_l = [jnp.where(first, halo_l, lefts[0]), jnp.where(first, lefts[0], lefts[1])]
        near_r = [jnp.where(last, rights[1], rights[0]), jnp.where(last, halo_r, rights[1])]
        done = []
        for half in range(2):
            m = means[half]
            other = jnp.where(lane3, near_r[half], jnp.where(lane0, near_l[half], m))
            done.append((0.5 * (m + other)).reshape(64, 128))
        use(i, done)
        return pltpu.roll(left_c, 120, 1), pltpu.roll(right_c, 120, 1)

    lax.fori_loop(0, 9, one, (left_halo, right_halo))


def chunk_of(ref, i):
    return ref[pl.ds(i * 8, 8), :, :].reshape(64, 256)


def put_halves(ref, i, x):
    for half in range(2):
        at = pl.multiple_of(half * PTS + i * 64, 64)
        ref[pl.ds(at, 64), :] = x[:, half * 128 : (half + 1) * 128]


def dynamics_kernel(
    tracer_h, wind_x_h, wind_y_h, drops_h, counts_h, growth_h, collision_h, by_rows_h, by_cols_h, selector_h,
    row_map_h, col_map_h, cells_h, owner_h, members_h,
    state, cell_forcing, pair_coef, growth_col, start, counts_out, unsort, sender, quadratic, linear, constant,
    tracer, wind_x, wind_y, drops, counts, growth, collision, by_rows, by_cols, selector,
    row_map, col_map, cells, owner, members, doubled,
    loads, piece_loads, field, total, packs, rows, got_packs, got_rows, send, recv,
):
    g, c, up, down, left, right = neighbours()
    barrier = pltpu.get_barrier_semaphore()
    around = [(up, c), (down, c)]
    around += [(r, s) for s in (left, right) for r in (g, up, down)]
    sources = [tracer_h, wind_x_h, wind_y_h, by_rows_h, by_cols_h, drops_h, counts_h, owner_h, collision_h,
               selector_h, growth_h, members_h, row_map_h, col_map_h, cells_h]
    targets = [tracer, wind_x, wind_y, by_rows, by_cols, drops, counts, owner, collision,
               selector, growth, members, row_map, col_map, cells]
    thirds = [
        [
            pltpu.make_async_copy(source.at[pl.ds(24 * n, 24)], target.at[pl.ds(24 * n, 24)], piece_loads.at[n, m])
            for m, (source, target) in enumerate(zip(sources[0:3], targets[0:3]))
        ]
        for n in range(3)
    ]
    fetch = [
        pltpu.make_async_copy(source, target, loads.at[n])
        for n, (source, target) in enumerate(zip(sources[3:], targets[3:]))
    ]
    for copy in fetch[0:2] + thirds[0] + thirds[1] + thirds[2] + fetch[2:]:
        copy.start()
    for to in around:
        pl.semaphore_signal(barrier, inc=1, device_id=to, device_id_type=MESH)
    for copy in fetch[0:2]:
        copy.wait()
    for n in range(3):
        for copy in thirds[n]:
            copy.wait()
        for k in range(3):
            i = n * 3 + k
            put_halves(
                field, i,
                tendency(
                    chunk_of(tracer, i), chunk_of(wind_x, i), chunk_of(wind_y, i), by_rows[...], by_cols[...]
                ),
            )
    pack_edges(field, packs.at[0], rows.at[0])
    pl.semaphore_wait(barrier, 8)
    copies = halo_copies(packs.at[0], rows.at[0], got_packs.at[0], got_rows.at[0], send.at[0], recv.at[0])
    for copy in copies:
        copy.start()

    for copy in fetch[2:]:
        copy.wait()
    coef = jnp.dot(collision[...], selector[...], preferred_element_type=F32)
    coef = jnp.concatenate([coef, jnp.zeros((15, PAIRS), F32)], axis=0)
    pair_coef[...] = coef.astype(BF)
    i0 = lax.broadcasted_iota(jnp.int32, (COLS, COLS), 0)
    i1 = lax.broadcasted_iota(jnp.int32, (COLS, COLS), 1)
    wide = jnp.concatenate([growth[...], jnp.zeros((1, COLS - BINS), F32)], axis=1)
    growth_col[...] = jnp.broadcast_to(
        jnp.sum(
            jnp.where((i0 == i1)[0:ROWS], jnp.broadcast_to(wide, (ROWS, COLS)), 0.0), axis=1, keepdims=True
        ),
        (ROWS, COLS),
    )
    stacked = jnp.concatenate([jnp.broadcast_to(x.astype(F32), (16, COLS)) for x in split3(wide)], axis=0)
    slope = jnp.zeros((96, COLS), F32)
    for side in range(2):
        of_pair = lax.dot_general(
            stacked.astype(BF), members[side], (((1,), (1,)), ((), ())), preferred_element_type=F32
        )
        scaled = coef * (of_pair[0:1] + of_pair[16:17] + of_pair[32:33])
        near = scaled.astype(BF)
        terms = jnp.concatenate([near, (scaled - near.astype(F32)).astype(BF)], axis=0)
        slope = slope + jnp.dot(terms, members[1 - side], preferred_element_type=F32)
    slope = slope[0:48] + slope[48:96]
    constant[...] = jnp.broadcast_to(
        0.5 * jnp.sum(slope[0:ROWS] * wide, axis=1, keepdims=True), (ROWS, COLS)
    )
    near = slope.astype(BF)
    linear[...] = jnp.concatenate([near, (slope - near.astype(F32)).astype(BF)], axis=0)
    across = jnp.broadcast_to(counts[...], (COLS, COLS)).astype(F32)
    along = jnp.sum(jnp.where(i0 == i1, across, 0.0), axis=1, keepdims=True)
    before = (across > along) | ((across == along) & (i1 < i0))
    place = jnp.sum(jnp.where(before, 1.0, 0.0), axis=1, keepdims=True).astype(jnp.int32)
    after = (along > across) | ((along == across) & (i0 < i1))
    place_row = jnp.sum(jnp.where(after, 1.0, 0.0), axis=0, keepdims=True).astype(jnp.int32)
    counts_out[...] = jnp.sum(jnp.where(place == i1, along, 0.0), axis=0, keepdims=True).astype(jnp.int32)
    unsort[...] = jnp.where(place == i1, 1.0, 0.0).astype(BF)
    sort = jnp.where(place_row == i0, 1.0, 0.0).astype(BF)
    for b in range(BINS):
        sorted_bin = jnp.dot(sort, drops[b], preferred_element_type=F32)
        for half in range(2):
            start[pl.ds(half * COLS * ROWS + b, COLS, stride=ROWS), :] = sorted_bin[
                :, half * 128 : (half + 1) * 128
            ]

    for b in range(BINS, ROWS):
        for half in range(2):
            start[pl.ds(half * COLS * ROWS + b, COLS, stride=ROWS), :] = jnp.zeros((COLS, 128), F32)
    owners = jnp.broadcast_to(owner[...], (COLS, COLS))
    owned = jnp.sum(jnp.where(i0 == i1, owners.astype(F32), 0.0), axis=1, keepdims=True)
    earlier = (owned == owners.astype(F32)) & (i0 < i1)
    turn = jnp.sum(jnp.where(earlier, 1.0, 0.0), axis=0, keepdims=True)
    key = owners % NC * NG + owners // NC
    sender[...] = jnp.concatenate(
        [jnp.where((key == i0) & (turn == float(r)), 1.0, 0.0) for r in range(2)], axis=1
    ).astype(BF)

    def square(p, _):
        for b in range(16):
            drops_of = [start[column_rows(p * 16 + b, half), :] for half in range(2)]
            found = jnp.dot(pair_coef[...], pairs_of(drops_of, doubled.at[b]), preferred_element_type=F32)
            for half in range(2):
                quadratic[column_rows(p * 16 + b, half), :] = found[0:ROWS, half * 128 : (half + 1) * 128]
        return 0

    lax.fori_loop(0, EARLY, square, 0)
    halo_wait(got_packs.at[0], got_rows.at[0], send.at[0], recv.at[0])

    def second(i, means):
        mean = jnp.concatenate(means, axis=1)
        moved = chunk_of(tracer, i) + DT_DYN * mean
        state[pl.ds(i * 8, 8), :, :] = moved.reshape(8, 8, 256)
        put_halves(total, i, mean)
        put_halves(
            field, i,
            tendency(moved, chunk_of(wind_x, i), chunk_of(wind_y, i), by_rows[...], by_cols[...]),
        )

    assemble_loop(field, got_packs.at[0], got_rows.at[0], second)
    pack_edges(field, packs.at[1], rows.at[1])
    copies = halo_copies(packs.at[1], rows.at[1], got_packs.at[1], got_rows.at[1], send.at[1], recv.at[1])
    for copy in copies:
        copy.start()
    lax.fori_loop(EARLY, COLS // 16, square, 0)
    halo_wait(got_packs.at[1], got_rows.at[1], send.at[1], recv.at[1])

    def third(i, means):
        mean = jnp.concatenate(means, axis=1)
        state[pl.ds(i * 8, 8), :, :] = (chunk_of(state, i) + DT_DYN * mean).reshape(8, 8, 256)
        for half in range(2):
            at = pl.multiple_of(half * PTS + i * 64, 64)
            total[pl.ds(at, 64), :] = total[pl.ds(at, 64), :] + means[half]

    assemble_loop(field, got_packs.at[1], got_rows.at[1], third)
    sums = jnp.concatenate([total[0:PTS, :], total[PTS : 2 * PTS, :]], axis=1)
    near = sums.astype(BF)
    rest = (sums - near.astype(F32)).astype(BF)
    by_row = jnp.dot(row_map[...], near, preferred_element_type=F32)
    by_row = by_row[0:32] + by_row[32:64] + jnp.dot(row_map[0:32, :], rest, preferred_element_type=F32)
    forcing = [
        lax.dot_general(
            col_map[...], by_row[16 * e : 16 * (e + 1)], (((1,), (1,)), ((), ())),
            precision=HIGH, preferred_element_type=F32,
        ).astype(BF)
        for e in range(2)
    ]
    by_cell = jnp.dot(
        jnp.concatenate(forcing, axis=0), cells[...], preferred_element_type=F32
    ).astype(BF)
    cell_forcing[...] = DT_CRM * jnp.dot(sort, by_cell, preferred_element_type=F32)


def dynamics(tracer, wind_x, wind_y, drops, counts_row, growth_row, collision, owner_row):
    row_map, col_map = forcing_tables()
    near = row_map.astype(ml_dtypes.bfloat16)
    row_map = np.concatenate([near, (row_map - near.astype(np.float32)).astype(ml_dtypes.bfloat16)])
    by_rows, by_cols = stencil_tables()
    shape = tracer.shape
    operands = (
        tracer, wind_x, wind_y, drops, counts_row, growth_row, collision,
        jnp.asarray(by_rows), jnp.asarray(by_cols), jnp.asarray(pair_selector()),
        jnp.asarray(row_map), jnp.asarray(col_map), jnp.asarray(spread_cells()), owner_row,
        jnp.asarray(pair_members()),
    )
    return pl.pallas_call(
        dynamics_kernel,
        out_shape=(
            jax.ShapeDtypeStruct(shape, F32),
            jax.ShapeDtypeStruct((COLS, 256), F32),
            jax.ShapeDtypeStruct((48, PAIRS), BF),
            jax.ShapeDtypeStruct((ROWS, 128), F32),
            jax.ShapeDtypeStruct((2 * COLS * ROWS, 128), F32),
            jax.ShapeDtypeStruct((1, COLS), jnp.int32),
            jax.ShapeDtypeStruct((COLS, COLS), BF),
            jax.ShapeDtypeStruct((COLS, 2 * COLS), BF),
            jax.ShapeDtypeStruct((2 * COLS * ROWS, 128), F32),
            jax.ShapeDtypeStruct((96, 128), BF),
            jax.ShapeDtypeStruct((ROWS, 128), F32),
        ),
        in_specs=[HBM] * 15,
        out_specs=(VMEM,) * 11,
        scratch_shapes=[pltpu.VMEM(x.shape, x.dtype) for x in operands]
        + [
            pltpu.VMEM((16, 2, 48, 128), F32),
            pltpu.SemaphoreType.DMA((12,)),
            pltpu.SemaphoreType.DMA((3, 3)),
            pltpu.VMEM((2 * PTS, 128), F32),
            pltpu.VMEM((2 * PTS, 128), F32),
            pltpu.VMEM((2, 2, 8, 128), F32),
            pltpu.VMEM((2, 2, 2 * LEV, 128), F32),
            pltpu.VMEM((2, 6, 8, 128), F32),
            pltpu.VMEM((2, 2, 2 * LEV, 128), F32),
            pltpu.SemaphoreType.DMA((2, 2)),
            pltpu.SemaphoreType.DMA((2, 2)),
        ],
        compiler_params=pltpu.CompilerParams(
            collective_id=0, has_side_effects=True, vmem_limit_bytes=40 << 20
        ),
        name="dynamics",
    )(*[pltpu.with_memory_space_constraint(x, pltpu.HBM) for x in operands])


def micro_kernel(
    counts, start, cell_forcing, pair_coef, growth, group, unsort, quadratic, linear, constant,
    drops_next, heat_out, echo_out,
    cloud, doubled, grow, heat_rows, echo_rows, drops_out, stores,
):
    bins = lax.broadcasted_iota(jnp.int32, (ROWS, 128), 0)
    mass = jnp.where(bins < BINS, (bins.astype(F32) + 1.0) / BINS, 0.0)

    def place(p, b, half):
        return column_rows(p * BATCH + b, half)

    def substep(s, p):
        for b in range(BATCH):
            active = s < counts[0, p * BATCH + b]
            olds = [cloud[place(p, b, half), :] for half in range(2)]
            grown = [olds[half] + grow[b, half] for half in range(2)]
            change = jnp.dot(pair_coef[...], pairs_of(grown, doubled.at[b]), preferred_element_type=F32)
            for half in range(2):
                moved = grown[half] + DT_CRM * change[0:ROWS, half * 128 : (half + 1) * 128]
                cloud[place(p, b, half), :] = jnp.where(active, moved, olds[half])
        return p

    def batch(p, _):
        for b in range(BATCH):
            active = counts[0, p * BATCH + b] > 0
            forced = cell_forcing[pl.ds(p * BATCH + b, 1), :]
            olds = [start[place(p, b, half), :] for half in range(2)]
            rows = [jnp.concatenate([old, old[0:8]], axis=0).astype(BF) for old in olds]
            sloped = jnp.dot(linear[:, 0:48], jnp.concatenate(rows, axis=1), preferred_element_type=F32)
            for half in range(2):
                at = slice(half * 128, (half + 1) * 128)
                f = forced[:, at]
                add = f * growth[...]
                change = quadratic[place(p, b, half), :] + f * (
                    sloped[0:ROWS, at] + sloped[48 : 48 + ROWS, at] + f * constant[...]
                )
                grow[b, half] = add
                moved = olds[half] + add + DT_CRM * change
                cloud[place(p, b, half), :] = jnp.where(active, moved, olds[half])
        lax.fori_loop(1, counts[0, p * BATCH], substep, p)
        for half in range(2):
            at = slice(half * 128, (half + 1) * 128)
            for eight in range(BATCH // 8):
                heats, echos = [], []
                for b in range(8):
                    where = place(p, eight * 8 + b, half)
                    final = cloud[where, :]
                    gain = (final - start[where, :]) * mass
                    weighed = final * mass
                    square = weighed * weighed
                    heats.append(sum(gain[8 * k : 8 * k + 8] for k in range(5)))
                    echos.append(sum(square[8 * k : 8 * k + 8] for k in range(5)))
                heats, echos = rows_of_sums(heats), rows_of_sums(echos)
                rows = pl.ds(pl.multiple_of(p * BATCH + eight * 8, 8), 8)
                heat_rows[rows, at] = heats
                echo_rows[rows, at] = echos
        return 0

    lax.fori_loop(0, COLS // BATCH, batch, 0)

    def group_mean(x):
        acc = None
        for part in split3(x):
            y = jnp.dot(part, group[...], preferred_element_type=F32)
            acc = y if acc is None else acc + y
        return acc

    back = unsort[...]
    pieces = []
    for n in range(3):
        for b in range(11 * n, 11 * n + 11):
            halves = [cloud[pl.ds(half * COLS * ROWS + b, COLS, stride=ROWS), :] for half in range(2)]
            drops_out[b] = jnp.dot(
                back, jnp.concatenate(halves, axis=1).astype(BF), preferred_element_type=F32
            ).astype(BF)
        part = pl.ds(11 * n, 11)
        piece = pltpu.make_async_copy(drops_out.at[part], drops_next.at[part], stores.at[n])
        piece.start()
        pieces.append(piece)
    heat = group_mean(heat_rows[...]).astype(BF)
    heat_out[...] = jnp.dot(back, heat, preferred_element_type=F32).astype(BF)
    echo_out[...] = jnp.log(1.0 + dot_exact(back, group_mean(echo_rows[...])))
    for piece in pieces:
        piece.wait()


def microphysics(counts, start, cell_forcing, pair_coef, growth, unsort, quadratic, linear, constant):
    return pl.pallas_call(
        micro_kernel,
        out_shape=(
            jax.ShapeDtypeStruct((BINS, COLS, 256), BF),
            jax.ShapeDtypeStruct((COLS, 128), BF),
            jax.ShapeDtypeStruct((COLS, 128), F32),
        ),
        in_specs=[SMEM] + [VMEM] * 9,
        out_specs=(HBM, VMEM, VMEM),
        scratch_shapes=[
            pltpu.VMEM((2 * COLS * ROWS, 128), F32),
            pltpu.VMEM((BATCH, 2, 48, 128), F32),
            pltpu.VMEM((BATCH, 2, ROWS, 128), F32),
            pltpu.VMEM((COLS, 256), F32),
            pltpu.VMEM((COLS, 256), F32),
            pltpu.VMEM((BINS, COLS, 256), BF),
            pltpu.SemaphoreType.DMA((3,)),
        ],
        compiler_params=pltpu.CompilerParams(vmem_limit_bytes=40 << 20),
        name="microphysics",
    )(
        counts, start, cell_forcing, pair_coef, growth, jnp.asarray(group_matrix()), unsort,
        quadratic, linear, constant,
    )


def coupling_kernel(
    state, heat, echo, sender, heating, spread,
    tracer_next, rows_out,
    field, packs, rows, got_packs, got_rows, sent, first_in, second_out, second_in,
    send, recv, power_send, power_recv,
):
    g, c, up, down, left, right = neighbours()
    barrier = pltpu.get_barrier_semaphore()
    peers = [(lax.rem(g + k, NG), c) for k in range(1, NG)]
    peers += [(g, lax.rem(c + k, NC)) for k in range(1, NC)]
    peers += [(r, s) for s in (left, right) for r in (up, down)]
    for to in peers:
        pl.semaphore_signal(barrier, inc=1, device_id=to, device_id_type=MESH)

    sums = echo[...]
    sums = jnp.concatenate([sums, pltpu.roll(sums, 16, 1)], axis=0)
    sent[...] = dot_exact(sender[...], sums).reshape(NC, NG, 128)
    pl.semaphore_wait(barrier, len(peers))
    for k in range(1, NC):
        to = lax.rem(c + k, NC)
        pltpu.make_async_remote_copy(
            src_ref=sent.at[to],
            dst_ref=first_in.at[c],
            send_sem=power_send.at[0],
            recv_sem=power_recv.at[0],
            device_id=(g, to),
            device_id_type=MESH,
        ).start()
    first_in[c] = sent[c]

    warm = []
    for e in range(2):
        turned = heat[64 * e : 64 * (e + 1), :].astype(F32).T.astype(BF)[0:16]
        warm.append(jnp.dot(turned, spread[...], preferred_element_type=F32).astype(BF))
    warm = jnp.concatenate(warm + warm, axis=0)
    for half in range(2):
        at = slice(half * 128, (half + 1) * 128)
        back = jnp.dot(heating[...], warm[:, at], preferred_element_type=F32)
        field[half * PTS : (half + 1) * PTS, :] = back + state[:, :, at].reshape(PTS, 128)
    pack_edges(field, packs, rows)
    for copy in halo_copies(packs, rows, got_packs, got_rows, send, recv):
        copy.start()

    for sems in (power_recv, power_send):
        wait_bytes(first_in.at[0 : NC - 1], sems.at[0])
    every = first_in[...]
    for to in range(NG):
        second_out[to] = every[:, to, :]
    for k in range(1, NG):
        to = lax.rem(g + k, NG)
        pltpu.make_async_remote_copy(
            src_ref=second_out.at[to],
            dst_ref=second_in.at[g],
            send_sem=power_send.at[1],
            recv_sem=power_recv.at[1],
            device_id=(to, c),
            device_id_type=MESH,
        ).start()
    second_in[g] = second_out[g]

    halo_wait(got_packs, got_rows, send, recv)

    def last(i, means):
        for half in range(2):
            tracer_next[pl.ds(i * 8, 8), :, half * 128 : (half + 1) * 128] = means[half].reshape(8, 8, 128)

    assemble_loop(field, got_packs, got_rows, last)

    for sems in (power_recv, power_send):
        wait_bytes(second_in.at[0 : NG - 1], sems.at[1])
    rows_out[...] = second_in[...].reshape(COLS, 128)


def coupling(state, heat, echo, sender):
    return pl.pallas_call(
        coupling_kernel,
        out_shape=(
            jax.ShapeDtypeStruct(state.shape, F32),
            jax.ShapeDtypeStruct((COLS, 128), F32),
        ),
        in_specs=[VMEM] * 6,
        out_specs=(VMEM,) * 2,
        scratch_shapes=[
            pltpu.VMEM((2 * PTS, 128), F32),
            pltpu.VMEM((2, 8, 128), F32),
            pltpu.VMEM((2, 2 * LEV, 128), F32),
            pltpu.VMEM((6, 8, 128), F32),
            pltpu.VMEM((2, 2 * LEV, 128), F32),
            pltpu.VMEM((NC, NG, 128), F32),
            pltpu.VMEM((NC, NG, 128), F32),
            pltpu.VMEM((NG, NC, 128), F32),
            pltpu.VMEM((NG, NC, 128), F32),
            pltpu.SemaphoreType.DMA((2,)),
            pltpu.SemaphoreType.DMA((2,)),
            pltpu.SemaphoreType.DMA((2,)),
            pltpu.SemaphoreType.DMA((2,)),
        ],
        compiler_params=pltpu.CompilerParams(
            collective_id=1, has_side_effects=True, vmem_limit_bytes=40 << 20
        ),
        name="coupling",
    )(
        state, heat, echo, sender,
        jnp.asarray(heating_table()), jnp.asarray(spread_columns()),
    )


def finish_kernel(mean, rows, slots, tracer_next, power, store):
    copy = pltpu.make_async_copy(mean, tracer_next, store)
    copy.start()
    turned = rows[...].T
    turned = jnp.concatenate([turned[0:16], turned[16:32]], axis=1)
    parts = jnp.dot(jnp.concatenate(split3(turned), axis=0), slots[...], preferred_element_type=F32)
    power[...] = parts[0:16] + parts[16:32] + parts[32:48]
    copy.wait()


def finish(mean, rows):
    return pl.pallas_call(
        finish_kernel,
        out_shape=(
            jax.ShapeDtypeStruct(mean.shape, F32),
            jax.ShapeDtypeStruct((CLEV, 256), F32),
        ),
        in_specs=[VMEM] * 3,
        out_specs=(HBM, VMEM),
        scratch_shapes=[pltpu.SemaphoreType.DMA(())],
        compiler_params=pltpu.CompilerParams(vmem_limit_bytes=8 << 20),
        name="finish",
    )(mean, rows, jnp.asarray(slot_table()))


def shards(tracer, wind_x, wind_y, drops, owner, counts, collision, growth):
    state, cell_forcing, pair_coef, growth_col, start, sorted_counts, unsort, sender, quadratic, linear, constant = dynamics(
        tracer, wind_x, wind_y, drops.transpose(1, 0, 2),
        counts.reshape(1, COLS), growth.reshape(1, BINS), collision, owner.reshape(1, COLS),
    )
    drops_next, heat, echo = microphysics(
        sorted_counts, start, cell_forcing, pair_coef, growth_col, unsort, quadratic, linear, constant
    )
    tracer_next, power = finish(*coupling(state, heat, echo, sender))
    return (tracer_next, drops_next.transpose(1, 0, 2), power)


def solution(mesh):
    return jax.shard_map(
        shards,
        mesh=mesh,
        in_specs=(
            P(None, "gcm", "crm"),
            P(None, "gcm", "crm"),
            P(None, "gcm", "crm"),
            P(("gcm", "crm"), None, None),
            P(("gcm", "crm"), None),
            P(("gcm", "crm")),
            P(),
            P(),
        ),
        out_specs=(P(None, "gcm", "crm"), P(("gcm", "crm"), None, None), P(None, ("gcm", "crm"))),
        check_vma=False,
    )
```

```python
import functools

import jax
import jax.numpy as jnp
import ml_dtypes
import numpy as np
from jax import lax
from jax.experimental import pallas as pl
from jax.experimental.pallas import tpu as pltpu
from jax.sharding import PartitionSpec as P

BF = jnp.bfloat16
F32 = jnp.float32
MESH = pl.DeviceIdType.MESH
HIGH = lax.Precision.HIGHEST
VMEM = pl.BlockSpec(memory_space=pltpu.VMEM)
SMEM = pl.BlockSpec(memory_space=pltpu.SMEM)
HBM = pl.BlockSpec(memory_space=pltpu.HBM)

NG = 8
NC = 16
LEV = 72
BINS = 33
CLEV = 16
COLS = 128
PTS = LEV * 8
PAIRS = 576
DT_DYN = 0.04
DT_CRM = 0.05
DT_PHYS = 0.5
BATCH = 32
ROWS = 40
EARLY = 3


def gll_tables():
    inv_root = 1.0 / np.sqrt(5.0)
    gll_nodes = np.array([-1.0, -inv_root, inv_root, 1.0])
    weights = np.array([1.0, 5.0, 5.0, 1.0]) / 6.0
    legendre = (5.0 * gll_nodes**3 - 3.0 * gll_nodes) / 2.0
    derivative = np.zeros((4, 4))
    for i in range(4):
        for j in range(4):
            if i != j:
                derivative[i, j] = legendre[i] / (legendre[j] * (gll_nodes[i] - gll_nodes[j]))
    derivative[0, 0] = -3.0
    derivative[3, 3] = 3.0
    return (2.0 * derivative, weights)


def level_tables(levels, crm_levels):
    spacing = levels / crm_levels
    centres = (np.arange(crm_levels) + 0.5) * spacing - 0.5
    hats = np.maximum(0.0, 1.0 - np.abs(np.arange(levels)[None, :] - centres[:, None]) / spacing)
    down_map = hats / hats.sum(axis=1, keepdims=True)
    up_map = hats.T / hats.T.sum(axis=1, keepdims=True)
    return (down_map, up_map)


def stencil_tables():
    derivative, _ = gll_tables()
    out = []
    for size in (64, 128):
        whole = np.kron(np.eye(size // 4), -derivative).astype(np.float32)
        if size == 128:
            whole = whole.T
        near = whole.astype(ml_dtypes.bfloat16)
        out += [near, (whole - near.astype(np.float32)).astype(ml_dtypes.bfloat16)]
    by_rows = np.concatenate([out[0], out[0], out[1]], axis=1)
    by_cols = np.block([[out[2], out[3]], [out[2], np.zeros_like(out[2])]])
    return by_rows, by_cols


def forcing_tables():
    _, weights = gll_tables()
    down_map, _ = level_tables(LEV, CLEV)
    rows = np.zeros((2, CLEV, LEV, 8))
    for r in range(8):
        rows[r // 4, :, :, r] = down_map * weights[r % 4] / 2.0 * 0.5
    cols = np.zeros((64, 256))
    for c in range(256):
        cols[c // 4, c] = weights[c % 4] / 2.0
    return rows.reshape(32, PTS).astype(np.float32), cols.astype(np.float32)


def spread_cells():
    out = np.zeros((CLEV, 256), np.float32)
    for c in range(256):
        out[c // 16, c] = 1.0
    return out.astype(ml_dtypes.bfloat16)


def group_matrix():
    out = np.zeros((256, 128), np.float32)
    for c in range(256):
        out[c, c // 16] = 1.0 / 16.0
    return out.astype(ml_dtypes.bfloat16)


def heating_table():
    _, up_map = level_tables(LEV, CLEV)
    half = (DT_PHYS * up_map).astype(np.float32)
    first = half.astype(ml_dtypes.bfloat16)
    second = (half - first.astype(np.float32)).astype(ml_dtypes.bfloat16)
    out = np.zeros((LEV, 8, 2, 2, CLEV), ml_dtypes.bfloat16)
    for r in range(8):
        out[:, r, 0, r // 4, :] = first
        out[:, r, 1, r // 4, :] = second
    return out.reshape(PTS, 64)


def spread_columns():
    out = np.zeros((64, 256), np.float32)
    for c in range(256):
        out[c // 4, c] = 1.0
    return out.astype(ml_dtypes.bfloat16)


def slot_table():
    out = np.zeros((2, 128, 256), np.float32)
    for d in range(128):
        for r in range(2):
            out[r, d, 2 * d + r] = 1.0
    return out.reshape(256, 256).astype(ml_dtypes.bfloat16)


def pair_list():
    out = []
    for back in (0, 8):
        for d in range(8):
            for i in range(32):
                out.append(((i - back) % 32, (i + d) % 32))
    for i in range(16):
        out.append((i, i + 16))
    for i in range(32):
        out.append((i, 32))
    out.append((32, 32))
    return out


def pair_selector():
    out = np.zeros((BINS * BINS, PAIRS), np.float32)
    for q, (i, j) in enumerate(pair_list()):
        out[i * BINS + j, q] = 1.0
        out[j * BINS + i, q] = 1.0
    return out.astype(ml_dtypes.bfloat16)


def pair_members():
    out = np.zeros((2, PAIRS, 128), np.float32)
    for q, pair in enumerate(pair_list()):
        for side in range(2):
            out[side, q, pair[side]] = 1.0
    return out.astype(ml_dtypes.bfloat16)


def split3(x):
    hi = x.astype(BF)
    rest = x - hi.astype(F32)
    mid = rest.astype(BF)
    return hi, mid, (rest - mid.astype(F32)).astype(BF)


def dot_exact(onehot, x):
    acc = None
    for part in split3(x):
        y = jnp.dot(onehot, part, preferred_element_type=F32)
        acc = y if acc is None else acc + y
    return acc


def tendency(q, wind_x, wind_y, by_rows, by_cols):
    near = q.astype(BF)
    rest = (q - near.astype(F32)).astype(BF)
    grad_x = jnp.dot(by_rows, jnp.concatenate([near, rest, near], axis=0), preferred_element_type=F32)
    grad_y = []
    for at in (slice(0, 128), slice(128, 256)):
        both = jnp.concatenate([near[:, at], rest[:, at]], axis=1)
        y = jnp.dot(both, by_cols, preferred_element_type=F32)
        grad_y.append(y[:, 0:128] + y[:, 128:256])
    return wind_x * grad_x + wind_y * jnp.concatenate(grad_y, axis=1)


def pairs_of(grown, doubled):
    for half in range(2):
        doubled[half, 0:32, :] = grown[half][0:32]
        doubled[half, 32:40, :] = grown[half][0:8]

    def beside(parts):
        return jnp.concatenate(parts, axis=1)

    here = beside([now[0:32].astype(BF) for now in grown])
    behind = beside([jnp.concatenate([now[24:32], now[0:24]], axis=0).astype(BF) for now in grown])
    ahead = [beside([doubled[half, d : d + 32, :].astype(BF) for half in range(2)]) for d in range(8)]
    last = beside([jnp.broadcast_to(now[32:33], (32, 128)).astype(BF) for now in grown])
    rows = [here * x for x in ahead] + [behind * x for x in ahead]
    rows += [here[0:16] * here[16:32], here * last, last[0:16] * last[0:16]]
    return jnp.concatenate(rows, axis=0)


def rows_of_sums(blocks):
    row = lax.broadcasted_iota(jnp.int32, (8, 128), 0)
    for step in (4, 2, 1):
        mine = row % (2 * step) < step
        merged = []
        for k in range(step):
            a, b = blocks[k], blocks[k + step]
            other = jnp.where(mine, b, a)
            if step == 4:
                moved = pltpu.roll(other, 4, 0)
            else:
                moved = jnp.where(mine, pltpu.roll(other, 8 - step, 0), pltpu.roll(other, step, 0))
            merged.append(jnp.where(mine, a, b) + moved)
        blocks = merged
    return blocks[0]


def column_rows(col, half):
    return pl.ds(pl.multiple_of((half * COLS + col) * ROWS, 8), ROWS)


def neighbours():
    g = lax.axis_index("gcm")
    c = lax.axis_index("crm")
    up, down = lax.rem(g + NG - 1, NG), lax.rem(g + 1, NG)
    left, right = lax.rem(c + NC - 1, NC), lax.rem(c + 1, NC)
    return g, c, up, down, left, right


def pack_edges(field, packs, rows):
    lane = lax.broadcasted_iota(jnp.int32, (8, 128), 1)

    def one(i, carry):
        low, high = carry
        low, high = pltpu.roll(low, 120, 1), pltpu.roll(high, 120, 1)
        for k in range(8):
            at = pl.multiple_of(i * 64, 64) + 8 * k
            first, last = field[pl.ds(at, 8), :], field[pl.ds(PTS + at, 8), :]
            both = pltpu.roll(jnp.where(lane == 0, first, last), k + 1, 1)
            high = jnp.where(lane == k, both, high)
            low = jnp.where(lane == k + 1, both, low)
        return low, high

    zero = jnp.zeros((8, 128), F32)
    low, high = lax.fori_loop(
        0, 3, lambda n, edges: one(3 * n + 2, one(3 * n + 1, one(3 * n, edges))), (zero, zero)
    )
    packs[0] = pltpu.roll(low, 63, 1)
    packs[1] = pltpu.roll(high, 64, 1)
    for half in range(2):
        rows[0, half * LEV : (half + 1) * LEV, :] = field[pl.ds(half * PTS, LEV, stride=8), :]
        rows[1, half * LEV : (half + 1) * LEV, :] = field[pl.ds(half * PTS + 7, LEV, stride=8), :]


def halo_copies(packs, rows, got_packs, got_rows, send, recv):
    g, c, up, down, left, right = neighbours()
    plan = [
        (rows.at[1], got_rows.at[0], (down, c)),
        (rows.at[0], got_rows.at[1], (up, c)),
        (packs.at[1], got_packs.at[0], (g, right)),
        (packs.at[1], got_packs.at[1], (down, right)),
        (packs.at[1], got_packs.at[2], (up, right)),
        (packs.at[0], got_packs.at[3], (g, left)),
        (packs.at[0], got_packs.at[4], (down, left)),
        (packs.at[0], got_packs.at[5], (up, left)),
    ]
    return [
        pltpu.make_async_remote_copy(
            src_ref=src,
            dst_ref=dst,
            send_sem=send.at[0 if n < 2 else 1],
            recv_sem=recv.at[0 if n < 2 else 1],
            device_id=to,
            device_id_type=MESH,
        )
        for n, (src, dst, to) in enumerate(plan)
    ]


def wait_bytes(ref, sem):
    pltpu.make_async_copy(ref, ref, sem).wait()


def halo_wait(got_packs, got_rows, send, recv):
    for sems in (recv, send):
        wait_bytes(got_rows, sems.at[0])
        wait_bytes(got_packs, sems.at[1])


def assemble_loop(field, got_packs, got_rows, use):
    row = lax.broadcasted_iota(jnp.int32, (8, 128), 0)
    lane = lax.broadcasted_iota(jnp.int32, (8, 128), 1)

    def row_mean(x, above, below):
        up = jnp.where(row == 0, pltpu.roll(above, 1, 0), pltpu.roll(x, 1, 0))
        down = jnp.where(row == 7, pltpu.roll(below, 7, 0), pltpu.roll(x, 7, 0))
        other = jnp.where(row % 4 == 3, down, jnp.where(row % 4 == 0, up, x))
        return 0.5 * (x + other)

    left_halo = row_mean(got_packs[0], got_packs[1], got_packs[2])
    right_halo = row_mean(got_packs[3], got_packs[4], got_packs[5])
    edge_row = ((row == 0) | (row == 7))[None]
    upper = (row < 4)[None]
    is3, is4 = (row == 3)[None], (row == 4)[None]
    lane3, lane0 = (lane % 4 == 3)[None], (lane % 4 == 0)[None]
    first, last = (lane == 0)[None], (lane == 127)[None]

    def one(i, carry):
        left_c, right_c = carry
        means = []
        for half in range(2):
            at = pl.multiple_of(half * PTS + i * 64, 64)
            x = field[pl.ds(at, 64), :].reshape(8, 8, 128)
            lev = pl.multiple_of(half * LEV + i * 8, 8)
            above, below = (
                jnp.stack([got_rows[side, pl.ds(lev + k, 8, stride=0), :] for k in range(8)])
                for side in range(2)
            )
            other = jnp.where(is3, pltpu.roll(x, 7, 1), jnp.where(is4, pltpu.roll(x, 1, 1), x))
            other = jnp.where(edge_row, jnp.where(upper, above, below), other)
            means.append(0.5 * (x + other))
        lefts = [pltpu.roll(m, 1, 2) for m in means]
        rights = [pltpu.roll(m, 127, 2) for m in means]
        halo_l = jnp.stack([pltpu.roll(left_c, (128 - k) % 128, 1) if k else left_c for k in range(8)])
        halo_r = jnp.stack([pltpu.roll(right_c, 127 - k, 1) for k in range(8)])
        near_l = [jnp.where(first, halo_l, lefts[0]), jnp.where(first, lefts[0], lefts[1])]
        near_r = [jnp.where(last, rights[1], rights[0]), jnp.where(last, halo_r, rights[1])]
        done = []
        for half in range(2):
            m = means[half]
            other = jnp.where(lane3, near_r[half], jnp.where(lane0, near_l[half], m))
            done.append((0.5 * (m + other)).reshape(64, 128))
        use(i, done)
        return pltpu.roll(left_c, 120, 1), pltpu.roll(right_c, 120, 1)

    halos = (left_halo, right_halo)
    for i in range(9):
        halos = one(i, halos)


def chunk_of(ref, i):
    return ref[pl.ds(i * 8, 8), :, :].reshape(64, 256)


def put_halves(ref, i, x):
    for half in range(2):
        at = pl.multiple_of(half * PTS + i * 64, 64)
        ref[pl.ds(at, 64), :] = x[:, half * 128 : (half + 1) * 128]


def dynamics_kernel(
    tracer_h, wind_x_h, wind_y_h, drops_h, counts_h, growth_h, collision_h, by_rows_h, by_cols_h, selector_h,
    row_map_h, col_map_h, cells_h, owner_h, members_h,
    state, cell_forcing, pair_coef, growth_col, start, counts_out, unsort, sender, quadratic, linear, constant,
    tracer, wind_x, wind_y, drops, counts, growth, collision, by_rows, by_cols, selector,
    row_map, col_map, cells, owner, members, doubled,
    loads, piece_loads, field, total, packs, rows, got_packs, got_rows, send, recv,
):
    g, c, up, down, left, right = neighbours()
    barrier = pltpu.get_barrier_semaphore()
    around = [(up, c), (down, c)]
    around += [(r, s) for s in (left, right) for r in (g, up, down)]
    sources = [tracer_h, wind_x_h, wind_y_h, by_rows_h, by_cols_h, drops_h, counts_h, owner_h, collision_h,
               selector_h, growth_h, members_h, row_map_h, col_map_h, cells_h]
    targets = [tracer, wind_x, wind_y, by_rows, by_cols, drops, counts, owner, collision,
               selector, growth, members, row_map, col_map, cells]
    thirds = [
        [
            pltpu.make_async_copy(source.at[pl.ds(24 * n, 24)], target.at[pl.ds(24 * n, 24)], piece_loads.at[n, m])
            for m, (source, target) in enumerate(zip(sources[0:3], targets[0:3]))
        ]
        for n in range(3)
    ]
    fetch = [
        pltpu.make_async_copy(source, target, loads.at[n])
        for n, (source, target) in enumerate(zip(sources[3:], targets[3:]))
    ]
    for copy in fetch[0:2] + thirds[0] + thirds[1] + thirds[2] + fetch[2:]:
        copy.start()
    for to in around:
        pl.semaphore_signal(barrier, inc=1, device_id=to, device_id_type=MESH)
    for copy in fetch[0:2]:
        copy.wait()
    for n in range(3):
        for copy in thirds[n]:
            copy.wait()
        for k in range(3):
            i = n * 3 + k
            put_halves(
                field, i,
                tendency(
                    chunk_of(tracer, i), chunk_of(wind_x, i), chunk_of(wind_y, i), by_rows[...], by_cols[...]
                ),
            )
    pack_edges(field, packs.at[0], rows.at[0])
    pl.semaphore_wait(barrier, 8)
    copies = halo_copies(packs.at[0], rows.at[0], got_packs.at[0], got_rows.at[0], send.at[0], recv.at[0])
    for copy in copies:
        copy.start()

    for copy in fetch[2:]:
        copy.wait()
    coef = jnp.dot(collision[...], selector[...], preferred_element_type=F32)
    coef = jnp.concatenate([coef, jnp.zeros((15, PAIRS), F32)], axis=0)
    pair_coef[...] = coef.astype(BF)
    i0 = lax.broadcasted_iota(jnp.int32, (COLS, COLS), 0)
    i1 = lax.broadcasted_iota(jnp.int32, (COLS, COLS), 1)
    wide = jnp.concatenate([growth[...], jnp.zeros((1, COLS - BINS), F32)], axis=1)
    growth_col[...] = jnp.broadcast_to(
        jnp.sum(
            jnp.where((i0 == i1)[0:ROWS], jnp.broadcast_to(wide, (ROWS, COLS)), 0.0), axis=1, keepdims=True
        ),
        (ROWS, COLS),
    )
    stacked = jnp.concatenate([jnp.broadcast_to(x.astype(F32), (16, COLS)) for x in split3(wide)], axis=0)
    slope = jnp.zeros((96, COLS), F32)
    for side in range(2):
        of_pair = lax.dot_general(
            stacked.astype(BF), members[side], (((1,), (1,)), ((), ())), preferred_element_type=F32
        )
        scaled = coef * (of_pair[0:1] + of_pair[16:17] + of_pair[32:33])
        near = scaled.astype(BF)
        terms = jnp.concatenate([near, (scaled - near.astype(F32)).astype(BF)], axis=0)
        slope = slope + jnp.dot(terms, members[1 - side], preferred_element_type=F32)
    slope = slope[0:48] + slope[48:96]
    constant[...] = jnp.broadcast_to(
        0.5 * jnp.sum(slope[0:ROWS] * wide, axis=1, keepdims=True), (ROWS, COLS)
    )
    near = slope.astype(BF)
    linear[...] = jnp.concatenate([near, (slope - near.astype(F32)).astype(BF)], axis=0)
    across = jnp.broadcast_to(counts[...], (COLS, COLS)).astype(F32)
    along = jnp.sum(jnp.where(i0 == i1, across, 0.0), axis=1, keepdims=True)
    before = (across > along) | ((across == along) & (i1 < i0))
    place = jnp.sum(jnp.where(before, 1.0, 0.0), axis=1, keepdims=True).astype(jnp.int32)
    after = (along > across) | ((along == across) & (i0 < i1))
    place_row = jnp.sum(jnp.where(after, 1.0, 0.0), axis=0, keepdims=True).astype(jnp.int32)
    counts_out[...] = jnp.sum(jnp.where(place == i1, along, 0.0), axis=0, keepdims=True).astype(jnp.int32)
    unsort[...] = jnp.where(place == i1, 1.0, 0.0).astype(BF)
    sort = jnp.where(place_row == i0, 1.0, 0.0).astype(BF)
    for b in range(BINS):
        sorted_bin = jnp.dot(sort, drops[b], preferred_element_type=F32)
        for half in range(2):
            start[pl.ds(half * COLS * ROWS + b, COLS, stride=ROWS), :] = sorted_bin[
                :, half * 128 : (half + 1) * 128
            ]

    for b in range(BINS, ROWS):
        for half in range(2):
            start[pl.ds(half * COLS * ROWS + b, COLS, stride=ROWS), :] = jnp.zeros((COLS, 128), F32)
    owners = jnp.broadcast_to(owner[...], (COLS, COLS))
    owned = jnp.sum(jnp.where(i0 == i1, owners.astype(F32), 0.0), axis=1, keepdims=True)
    earlier = (owned == owners.astype(F32)) & (i0 < i1)
    turn = jnp.sum(jnp.where(earlier, 1.0, 0.0), axis=0, keepdims=True)
    key = owners % NC * NG + owners // NC
    sender[...] = jnp.concatenate(
        [jnp.where((key == i0) & (turn == float(r)), 1.0, 0.0) for r in range(2)], axis=1
    ).astype(BF)

    def square(p, _):
        for b in range(16):
            drops_of = [start[column_rows(p * 16 + b, half), :] for half in range(2)]
            found = jnp.dot(pair_coef[...], pairs_of(drops_of, doubled.at[b]), preferred_element_type=F32)
            for half in range(2):
                quadratic[column_rows(p * 16 + b, half), :] = found[0:ROWS, half * 128 : (half + 1) * 128]
        return 0

    lax.fori_loop(0, EARLY, square, 0)
    halo_wait(got_packs.at[0], got_rows.at[0], send.at[0], recv.at[0])

    def second(i, means):
        mean = jnp.concatenate(means, axis=1)
        moved = chunk_of(tracer, i) + DT_DYN * mean
        state[pl.ds(i * 8, 8), :, :] = moved.reshape(8, 8, 256)
        put_halves(total, i, mean)
        put_halves(
            field, i,
            tendency(moved, chunk_of(wind_x, i), chunk_of(wind_y, i), by_rows[...], by_cols[...]),
        )

    assemble_loop(field, got_packs.at[0], got_rows.at[0], second)
    pack_edges(field, packs.at[1], rows.at[1])
    copies = halo_copies(packs.at[1], rows.at[1], got_packs.at[1], got_rows.at[1], send.at[1], recv.at[1])
    for copy in copies:
        copy.start()
    lax.fori_loop(EARLY, COLS // 16, square, 0)
    halo_wait(got_packs.at[1], got_rows.at[1], send.at[1], recv.at[1])

    def third(i, means):
        mean = jnp.concatenate(means, axis=1)
        state[pl.ds(i * 8, 8), :, :] = (chunk_of(state, i) + DT_DYN * mean).reshape(8, 8, 256)
        for half in range(2):
            at = pl.multiple_of(half * PTS + i * 64, 64)
            total[pl.ds(at, 64), :] = total[pl.ds(at, 64), :] + means[half]

    assemble_loop(field, got_packs.at[1], got_rows.at[1], third)
    sums = jnp.concatenate([total[0:PTS, :], total[PTS : 2 * PTS, :]], axis=1)
    near = sums.astype(BF)
    rest = (sums - near.astype(F32)).astype(BF)
    by_row = jnp.dot(row_map[...], near, preferred_element_type=F32)
    by_row = by_row[0:32] + by_row[32:64] + jnp.dot(row_map[0:32, :], rest, preferred_element_type=F32)
    forcing = [
        lax.dot_general(
            col_map[...], by_row[16 * e : 16 * (e + 1)], (((1,), (1,)), ((), ())),
            precision=HIGH, preferred_element_type=F32,
        ).astype(BF)
        for e in range(2)
    ]
    by_cell = jnp.dot(
        jnp.concatenate(forcing, axis=0), cells[...], preferred_element_type=F32
    ).astype(BF)
    cell_forcing[...] = DT_CRM * jnp.dot(sort, by_cell, preferred_element_type=F32)


def dynamics(tracer, wind_x, wind_y, drops, counts_row, growth_row, collision, owner_row):
    row_map, col_map = forcing_tables()
    near = row_map.astype(ml_dtypes.bfloat16)
    row_map = np.concatenate([near, (row_map - near.astype(np.float32)).astype(ml_dtypes.bfloat16)])
    by_rows, by_cols = stencil_tables()
    shape = tracer.shape
    operands = (
        tracer, wind_x, wind_y, drops, counts_row, growth_row, collision,
        jnp.asarray(by_rows), jnp.asarray(by_cols), jnp.asarray(pair_selector()),
        jnp.asarray(row_map), jnp.asarray(col_map), jnp.asarray(spread_cells()), owner_row,
        jnp.asarray(pair_members()),
    )
    return pl.pallas_call(
        dynamics_kernel,
        out_shape=(
            jax.ShapeDtypeStruct(shape, F32),
            jax.ShapeDtypeStruct((COLS, 256), F32),
            jax.ShapeDtypeStruct((48, PAIRS), BF),
            jax.ShapeDtypeStruct((ROWS, 128), F32),
            jax.ShapeDtypeStruct((2 * COLS * ROWS, 128), F32),
            jax.ShapeDtypeStruct((1, COLS), jnp.int32),
            jax.ShapeDtypeStruct((COLS, COLS), BF),
            jax.ShapeDtypeStruct((COLS, 2 * COLS), BF),
            jax.ShapeDtypeStruct((2 * COLS * ROWS, 128), F32),
            jax.ShapeDtypeStruct((96, 128), BF),
            jax.ShapeDtypeStruct((ROWS, 128), F32),
        ),
        in_specs=[HBM] * 15,
        out_specs=(VMEM,) * 11,
        scratch_shapes=[pltpu.VMEM(x.shape, x.dtype) for x in operands]
        + [
            pltpu.VMEM((16, 2, 48, 128), F32),
            pltpu.SemaphoreType.DMA((12,)),
            pltpu.SemaphoreType.DMA((3, 3)),
            pltpu.VMEM((2 * PTS, 128), F32),
            pltpu.VMEM((2 * PTS, 128), F32),
            pltpu.VMEM((2, 2, 8, 128), F32),
            pltpu.VMEM((2, 2, 2 * LEV, 128), F32),
            pltpu.VMEM((2, 6, 8, 128), F32),
            pltpu.VMEM((2, 2, 2 * LEV, 128), F32),
            pltpu.SemaphoreType.DMA((2, 2)),
            pltpu.SemaphoreType.DMA((2, 2)),
        ],
        compiler_params=pltpu.CompilerParams(
            collective_id=0, has_side_effects=True, vmem_limit_bytes=40 << 20
        ),
        name="dynamics",
    )(*[pltpu.with_memory_space_constraint(x, pltpu.HBM) for x in operands])


def micro_kernel(
    counts, start, cell_forcing, pair_coef, growth, group, unsort, quadratic, linear, constant,
    drops_next, heat_out, echo_out,
    cloud, doubled, grow, heat_rows, echo_rows, drops_out, stores,
):
    bins = lax.broadcasted_iota(jnp.int32, (ROWS, 128), 0)
    mass = jnp.where(bins < BINS, (bins.astype(F32) + 1.0) / BINS, 0.0)

    def place(p, b, half):
        return column_rows(p * BATCH + b, half)

    def substep(s, p):
        for b in range(BATCH):
            active = s < counts[0, p * BATCH + b]
            olds = [cloud[place(p, b, half), :] for half in range(2)]
            grown = [olds[half] + grow[b, half] for half in range(2)]
            change = jnp.dot(pair_coef[...], pairs_of(grown, doubled.at[b]), preferred_element_type=F32)
            for half in range(2):
                moved = grown[half] + DT_CRM * change[0:ROWS, half * 128 : (half + 1) * 128]
                cloud[place(p, b, half), :] = jnp.where(active, moved, olds[half])
        return p

    def batch(p, _):
        for b in range(BATCH):
            active = counts[0, p * BATCH + b] > 0
            forced = cell_forcing[pl.ds(p * BATCH + b, 1), :]
            olds = [start[place(p, b, half), :] for half in range(2)]
            rows = [jnp.concatenate([old, old[0:8]], axis=0).astype(BF) for old in olds]
            sloped = jnp.dot(linear[:, 0:48], jnp.concatenate(rows, axis=1), preferred_element_type=F32)
            for half in range(2):
                at = slice(half * 128, (half + 1) * 128)
                f = forced[:, at]
                add = f * growth[...]
                change = quadratic[place(p, b, half), :] + f * (
                    sloped[0:ROWS, at] + sloped[48 : 48 + ROWS, at] + f * constant[...]
                )
                grow[b, half] = add
                moved = olds[half] + add + DT_CRM * change
                cloud[place(p, b, half), :] = jnp.where(active, moved, olds[half])
        lax.fori_loop(1, counts[0, p * BATCH], substep, p)
        for half in range(2):
            at = slice(half * 128, (half + 1) * 128)
            for eight in range(BATCH // 8):
                heats, echos = [], []
                for b in range(8):
                    where = place(p, eight * 8 + b, half)
                    final = cloud[where, :]
                    gain = (final - start[where, :]) * mass
                    weighed = final * mass
                    square = weighed * weighed
                    heats.append(sum(gain[8 * k : 8 * k + 8] for k in range(5)))
                    echos.append(sum(square[8 * k : 8 * k + 8] for k in range(5)))
                heats, echos = rows_of_sums(heats), rows_of_sums(echos)
                rows = pl.ds(pl.multiple_of(p * BATCH + eight * 8, 8), 8)
                heat_rows[rows, at] = heats
                echo_rows[rows, at] = echos
        return 0

    lax.fori_loop(0, COLS // BATCH, batch, 0)

    def group_mean(x):
        acc = None
        for part in split3(x):
            y = jnp.dot(part, group[...], preferred_element_type=F32)
            acc = y if acc is None else acc + y
        return acc

    back = unsort[...]
    pieces = []
    for n in range(3):
        for b in range(11 * n, 11 * n + 11):
            halves = [cloud[pl.ds(half * COLS * ROWS + b, COLS, stride=ROWS), :] for half in range(2)]
            drops_out[b] = jnp.dot(
                back, jnp.concatenate(halves, axis=1).astype(BF), preferred_element_type=F32
            ).astype(BF)
        part = pl.ds(11 * n, 11)
        piece = pltpu.make_async_copy(drops_out.at[part], drops_next.at[part], stores.at[n])
        piece.start()
        pieces.append(piece)
    heat = group_mean(heat_rows[...]).astype(BF)
    heat_out[...] = jnp.dot(back, heat, preferred_element_type=F32).astype(BF)
    echo_out[...] = jnp.log(1.0 + dot_exact(back, group_mean(echo_rows[...])))
    for piece in pieces:
        piece.wait()


def microphysics(counts, start, cell_forcing, pair_coef, growth, unsort, quadratic, linear, constant):
    return pl.pallas_call(
        micro_kernel,
        out_shape=(
            jax.ShapeDtypeStruct((BINS, COLS, 256), BF),
            jax.ShapeDtypeStruct((COLS, 128), BF),
            jax.ShapeDtypeStruct((COLS, 128), F32),
        ),
        in_specs=[SMEM] + [VMEM] * 9,
        out_specs=(HBM, VMEM, VMEM),
        scratch_shapes=[
            pltpu.VMEM((2 * COLS * ROWS, 128), F32),
            pltpu.VMEM((BATCH, 2, 48, 128), F32),
            pltpu.VMEM((BATCH, 2, ROWS, 128), F32),
            pltpu.VMEM((COLS, 256), F32),
            pltpu.VMEM((COLS, 256), F32),
            pltpu.VMEM((BINS, COLS, 256), BF),
            pltpu.SemaphoreType.DMA((3,)),
        ],
        compiler_params=pltpu.CompilerParams(vmem_limit_bytes=40 << 20),
        name="microphysics",
    )(
        counts, start, cell_forcing, pair_coef, growth, jnp.asarray(group_matrix()), unsort,
        quadratic, linear, constant,
    )


def coupling_kernel(
    state, heat, echo, sender, heating, spread,
    tracer_next, rows_out,
    field, packs, rows, got_packs, got_rows, sent, first_in, second_out, second_in,
    send, recv, power_send, power_recv,
):
    g, c, up, down, left, right = neighbours()
    barrier = pltpu.get_barrier_semaphore()
    peers = [(lax.rem(g + k, NG), c) for k in range(1, NG)]
    peers += [(g, lax.rem(c + k, NC)) for k in range(1, NC)]
    peers += [(r, s) for s in (left, right) for r in (up, down)]
    for to in peers:
        pl.semaphore_signal(barrier, inc=1, device_id=to, device_id_type=MESH)

    sums = echo[...]
    sums = jnp.concatenate([sums, pltpu.roll(sums, 16, 1)], axis=0)
    sent[...] = dot_exact(sender[...], sums).reshape(NC, NG, 128)
    pl.semaphore_wait(barrier, len(peers))
    for k in range(1, NC):
        to = lax.rem(c + k, NC)
        pltpu.make_async_remote_copy(
            src_ref=sent.at[to],
            dst_ref=first_in.at[c],
            send_sem=power_send.at[0],
            recv_sem=power_recv.at[0],
            device_id=(g, to),
            device_id_type=MESH,
        ).start()
    first_in[c] = sent[c]

    warm = []
    for e in range(2):
        turned = heat[64 * e : 64 * (e + 1), :].astype(F32).T.astype(BF)[0:16]
        warm.append(jnp.dot(turned, spread[...], preferred_element_type=F32).astype(BF))
    warm = jnp.concatenate(warm + warm, axis=0)
    for half in range(2):
        at = slice(half * 128, (half + 1) * 128)
        back = jnp.dot(heating[...], warm[:, at], preferred_element_type=F32)
        field[half * PTS : (half + 1) * PTS, :] = back + state[:, :, at].reshape(PTS, 128)
    pack_edges(field, packs, rows)
    for copy in halo_copies(packs, rows, got_packs, got_rows, send, recv):
        copy.start()

    for sems in (power_recv, power_send):
        wait_bytes(first_in.at[0 : NC - 1], sems.at[0])
    every = first_in[...]
    for to in range(NG):
        second_out[to] = every[:, to, :]
    for k in range(1, NG):
        to = lax.rem(g + k, NG)
        pltpu.make_async_remote_copy(
            src_ref=second_out.at[to],
            dst_ref=second_in.at[g],
            send_sem=power_send.at[1],
            recv_sem=power_recv.at[1],
            device_id=(to, c),
            device_id_type=MESH,
        ).start()
    second_in[g] = second_out[g]

    halo_wait(got_packs, got_rows, send, recv)

    def last(i, means):
        for half in range(2):
            tracer_next[pl.ds(i * 8, 8), :, half * 128 : (half + 1) * 128] = means[half].reshape(8, 8, 128)

    assemble_loop(field, got_packs, got_rows, last)

    for sems in (power_recv, power_send):
        wait_bytes(second_in.at[0 : NG - 1], sems.at[1])
    rows_out[...] = second_in[...].reshape(COLS, 128)


def coupling(state, heat, echo, sender):
    return pl.pallas_call(
        coupling_kernel,
        out_shape=(
            jax.ShapeDtypeStruct(state.shape, F32),
            jax.ShapeDtypeStruct((COLS, 128), F32),
        ),
        in_specs=[VMEM] * 6,
        out_specs=(VMEM,) * 2,
        scratch_shapes=[
            pltpu.VMEM((2 * PTS, 128), F32),
            pltpu.VMEM((2, 8, 128), F32),
            pltpu.VMEM((2, 2 * LEV, 128), F32),
            pltpu.VMEM((6, 8, 128), F32),
            pltpu.VMEM((2, 2 * LEV, 128), F32),
            pltpu.VMEM((NC, NG, 128), F32),
            pltpu.VMEM((NC, NG, 128), F32),
            pltpu.VMEM((NG, NC, 128), F32),
            pltpu.VMEM((NG, NC, 128), F32),
            pltpu.SemaphoreType.DMA((2,)),
            pltpu.SemaphoreType.DMA((2,)),
            pltpu.SemaphoreType.DMA((2,)),
            pltpu.SemaphoreType.DMA((2,)),
        ],
        compiler_params=pltpu.CompilerParams(
            collective_id=1, has_side_effects=True, vmem_limit_bytes=40 << 20
        ),
        name="coupling",
    )(
        state, heat, echo, sender,
        jnp.asarray(heating_table()), jnp.asarray(spread_columns()),
    )


def finish_kernel(mean, rows, slots, tracer_next, power, store):
    copy = pltpu.make_async_copy(mean, tracer_next, store)
    copy.start()
    turned = rows[...].T
    turned = jnp.concatenate([turned[0:16], turned[16:32]], axis=1)
    parts = jnp.dot(jnp.concatenate(split3(turned), axis=0), slots[...], preferred_element_type=F32)
    power[...] = parts[0:16] + parts[16:32] + parts[32:48]
    copy.wait()


def finish(mean, rows):
    return pl.pallas_call(
        finish_kernel,
        out_shape=(
            jax.ShapeDtypeStruct(mean.shape, F32),
            jax.ShapeDtypeStruct((CLEV, 256), F32),
        ),
        in_specs=[VMEM] * 3,
        out_specs=(HBM, VMEM),
        scratch_shapes=[pltpu.SemaphoreType.DMA(())],
        compiler_params=pltpu.CompilerParams(vmem_limit_bytes=8 << 20),
        name="finish",
    )(mean, rows, jnp.asarray(slot_table()))


def shards(tracer, wind_x, wind_y, drops, owner, counts, collision, growth):
    state, cell_forcing, pair_coef, growth_col, start, sorted_counts, unsort, sender, quadratic, linear, constant = dynamics(
        tracer, wind_x, wind_y, drops.transpose(1, 0, 2),
        counts.reshape(1, COLS), growth.reshape(1, BINS), collision, owner.reshape(1, COLS),
    )
    drops_next, heat, echo = microphysics(
        sorted_counts, start, cell_forcing, pair_coef, growth_col, unsort, quadratic, linear, constant
    )
    tracer_next, power = finish(*coupling(state, heat, echo, sender))
    return (tracer_next, drops_next.transpose(1, 0, 2), power)


def solution(mesh):
    return jax.shard_map(
        shards,
        mesh=mesh,
        in_specs=(
            P(None, "gcm", "crm"),
            P(None, "gcm", "crm"),
            P(None, "gcm", "crm"),
            P(("gcm", "crm"), None, None),
            P(("gcm", "crm"), None),
            P(("gcm", "crm")),
            P(),
            P(),
        ),
        out_specs=(P(None, "gcm", "crm"), P(("gcm", "crm"), None, None), P(None, ("gcm", "crm"))),
        check_vma=False,
    )
```

```python
import functools

import jax
import jax.numpy as jnp
import ml_dtypes
import numpy as np
from jax import lax
from jax.experimental import pallas as pl
from jax.experimental.pallas import tpu as pltpu
from jax.sharding import PartitionSpec as P

BF = jnp.bfloat16
F32 = jnp.float32
MESH = pl.DeviceIdType.MESH
HIGH = lax.Precision.HIGHEST
VMEM = pl.BlockSpec(memory_space=pltpu.VMEM)
SMEM = pl.BlockSpec(memory_space=pltpu.SMEM)
HBM = pl.BlockSpec(memory_space=pltpu.HBM)

NG = 8
NC = 16
LEV = 72
BINS = 33
CLEV = 16
COLS = 128
PTS = LEV * 8
PAIRS = 576
DT_DYN = 0.04
DT_CRM = 0.05
DT_PHYS = 0.5
BATCH = 32
ROWS = 40
EARLY = 3


def gll_tables():
    inv_root = 1.0 / np.sqrt(5.0)
    gll_nodes = np.array([-1.0, -inv_root, inv_root, 1.0])
    weights = np.array([1.0, 5.0, 5.0, 1.0]) / 6.0
    legendre = (5.0 * gll_nodes**3 - 3.0 * gll_nodes) / 2.0
    derivative = np.zeros((4, 4))
    for i in range(4):
        for j in range(4):
            if i != j:
                derivative[i, j] = legendre[i] / (legendre[j] * (gll_nodes[i] - gll_nodes[j]))
    derivative[0, 0] = -3.0
    derivative[3, 3] = 3.0
    return (2.0 * derivative, weights)


def level_tables(levels, crm_levels):
    spacing = levels / crm_levels
    centres = (np.arange(crm_levels) + 0.5) * spacing - 0.5
    hats = np.maximum(0.0, 1.0 - np.abs(np.arange(levels)[None, :] - centres[:, None]) / spacing)
    down_map = hats / hats.sum(axis=1, keepdims=True)
    up_map = hats.T / hats.T.sum(axis=1, keepdims=True)
    return (down_map, up_map)


def stencil_tables():
    derivative, _ = gll_tables()
    out = []
    for size in (64, 128):
        whole = np.kron(np.eye(size // 4), -derivative).astype(np.float32)
        if size == 128:
            whole = whole.T
        near = whole.astype(ml_dtypes.bfloat16)
        out += [near, (whole - near.astype(np.float32)).astype(ml_dtypes.bfloat16)]
    by_rows = np.concatenate([out[0], out[0], out[1]], axis=1)
    by_cols = np.block([[out[2], out[3]], [out[2], np.zeros_like(out[2])]])
    return by_rows, by_cols


def forcing_tables():
    _, weights = gll_tables()
    down_map, _ = level_tables(LEV, CLEV)
    rows = np.zeros((2, CLEV, LEV, 8))
    for r in range(8):
        rows[r // 4, :, :, r] = down_map * weights[r % 4] / 2.0 * 0.5
    cols = np.zeros((64, 256))
    for c in range(256):
        cols[c // 4, c] = weights[c % 4] / 2.0
    return rows.reshape(32, PTS).astype(np.float32), cols.astype(np.float32)


def spread_cells():
    out = np.zeros((CLEV, 256), np.float32)
    for c in range(256):
        out[c // 16, c] = 1.0
    return out.astype(ml_dtypes.bfloat16)


def group_matrix():
    out = np.zeros((256, 128), np.float32)
    for c in range(256):
        out[c, c // 16] = 1.0 / 16.0
    return out.astype(ml_dtypes.bfloat16)


def heating_table():
    _, up_map = level_tables(LEV, CLEV)
    half = (DT_PHYS * up_map).astype(np.float32)
    first = half.astype(ml_dtypes.bfloat16)
    second = (half - first.astype(np.float32)).astype(ml_dtypes.bfloat16)
    out = np.zeros((LEV, 8, 2, 2, CLEV), ml_dtypes.bfloat16)
    for r in range(8):
        out[:, r, 0, r // 4, :] = first
        out[:, r, 1, r // 4, :] = second
    return out.reshape(PTS, 64)


def spread_columns():
    out = np.zeros((64, 256), np.float32)
    for c in range(256):
        out[c // 4, c] = 1.0
    return out.astype(ml_dtypes.bfloat16)


def slot_table():
    out = np.zeros((2, 128, 256), np.float32)
    for d in range(128):
        for r in range(2):
            out[r, d, 2 * d + r] = 1.0
    return out.reshape(256, 256).astype(ml_dtypes.bfloat16)


def pair_list():
    out = []
    for back in (0, 8):
        for d in range(8):
            for i in range(32):
                out.append(((i - back) % 32, (i + d) % 32))
    for i in range(16):
        out.append((i, i + 16))
    for i in range(32):
        out.append((i, 32))
    out.append((32, 32))
    return out


def pair_selector():
    out = np.zeros((BINS * BINS, PAIRS), np.float32)
    for q, (i, j) in enumerate(pair_list()):
        out[i * BINS + j, q] = 1.0
        out[j * BINS + i, q] = 1.0
    return out.astype(ml_dtypes.bfloat16)


def pair_members():
    out = np.zeros((2, PAIRS, 128), np.float32)
    for q, pair in enumerate(pair_list()):
        for side in range(2):
            out[side, q, pair[side]] = 1.0
    return out.astype(ml_dtypes.bfloat16)


def split3(x):
    hi = x.astype(BF)
    rest = x - hi.astype(F32)
    mid = rest.astype(BF)
    return hi, mid, (rest - mid.astype(F32)).astype(BF)


def dot_exact(onehot, x):
    acc = None
    for part in split3(x):
        y = jnp.dot(onehot, part, preferred_element_type=F32)
        acc = y if acc is None else acc + y
    return acc


def tendency(q, wind_x, wind_y, by_rows, by_cols):
    near = q.astype(BF)
    rest = (q - near.astype(F32)).astype(BF)
    grad_x = jnp.dot(by_rows, jnp.concatenate([near, rest, near], axis=0), preferred_element_type=F32)
    grad_y = []
    for at in (slice(0, 128), slice(128, 256)):
        both = jnp.concatenate([near[:, at], rest[:, at]], axis=1)
        y = jnp.dot(both, by_cols, preferred_element_type=F32)
        grad_y.append(y[:, 0:128] + y[:, 128:256])
    return wind_x * grad_x + wind_y * jnp.concatenate(grad_y, axis=1)


def pairs_of(grown, doubled):
    for half in range(2):
        doubled[half, 0:32, :] = grown[half][0:32]
        doubled[half, 32:40, :] = grown[half][0:8]

    def beside(parts):
        return jnp.concatenate(parts, axis=1)

    here = beside([now[0:32].astype(BF) for now in grown])
    behind = beside([jnp.concatenate([now[24:32], now[0:24]], axis=0).astype(BF) for now in grown])
    ahead = [beside([doubled[half, d : d + 32, :].astype(BF) for half in range(2)]) for d in range(8)]
    last = beside([jnp.broadcast_to(now[32:33], (32, 128)).astype(BF) for now in grown])
    rows = [here * x for x in ahead] + [behind * x for x in ahead]
    rows += [here[0:16] * here[16:32], here * last, last[0:16] * last[0:16]]
    return jnp.concatenate(rows, axis=0)


def rows_of_sums(blocks):
    row = lax.broadcasted_iota(jnp.int32, (8, 128), 0)
    for step in (4, 2, 1):
        mine = row % (2 * step) < step
        merged = []
        for k in range(step):
            a, b = blocks[k], blocks[k + step]
            other = jnp.where(mine, b, a)
            if step == 4:
                moved = pltpu.roll(other, 4, 0)
            else:
                moved = jnp.where(mine, pltpu.roll(other, 8 - step, 0), pltpu.roll(other, step, 0))
            merged.append(jnp.where(mine, a, b) + moved)
        blocks = merged
    return blocks[0]


def column_rows(col, half):
    return pl.ds(pl.multiple_of((half * COLS + col) * ROWS, 8), ROWS)


def neighbours():
    g = lax.axis_index("gcm")
    c = lax.axis_index("crm")
    up, down = lax.rem(g + NG - 1, NG), lax.rem(g + 1, NG)
    left, right = lax.rem(c + NC - 1, NC), lax.rem(c + 1, NC)
    return g, c, up, down, left, right


def pack_edges(field, packs, rows):
    lane = lax.broadcasted_iota(jnp.int32, (8, 128), 1)

    def one(i, carry):
        low, high = carry
        low, high = pltpu.roll(low, 120, 1), pltpu.roll(high, 120, 1)
        for k in range(8):
            at = pl.multiple_of(i * 64, 64) + 8 * k
            first, last = field[pl.ds(at, 8), :], field[pl.ds(PTS + at, 8), :]
            both = pltpu.roll(jnp.where(lane == 0, first, last), k + 1, 1)
            high = jnp.where(lane == k, both, high)
            low = jnp.where(lane == k + 1, both, low)
        return low, high

    zero = jnp.zeros((8, 128), F32)
    low, high = zero, zero
    for i in range(9):
        low, high = one(i, (low, high))
    packs[0] = pltpu.roll(low, 63, 1)
    packs[1] = pltpu.roll(high, 64, 1)
    for half in range(2):
        rows[0, half * LEV : (half + 1) * LEV, :] = field[pl.ds(half * PTS, LEV, stride=8), :]
        rows[1, half * LEV : (half + 1) * LEV, :] = field[pl.ds(half * PTS + 7, LEV, stride=8), :]


def halo_copies(packs, rows, got_packs, got_rows, send, recv):
    g, c, up, down, left, right = neighbours()
    plan = [
        (rows.at[1], got_rows.at[0], (down, c)),
        (rows.at[0], got_rows.at[1], (up, c)),
        (packs.at[1], got_packs.at[0], (g, right)),
        (packs.at[1], got_packs.at[1], (down, right)),
        (packs.at[1], got_packs.at[2], (up, right)),
        (packs.at[0], got_packs.at[3], (g, left)),
        (packs.at[0], got_packs.at[4], (down, left)),
        (packs.at[0], got_packs.at[5], (up, left)),
    ]
    return [
        pltpu.make_async_remote_copy(
            src_ref=src,
            dst_ref=dst,
            send_sem=send.at[0 if n < 2 else 1],
            recv_sem=recv.at[0 if n < 2 else 1],
            device_id=to,
            device_id_type=MESH,
        )
        for n, (src, dst, to) in enumerate(plan)
    ]


def wait_bytes(ref, sem):
    pltpu.make_async_copy(ref, ref, sem).wait()


def halo_wait(got_packs, got_rows, send, recv):
    for sems in (recv, send):
        wait_bytes(got_rows, sems.at[0])
        wait_bytes(got_packs, sems.at[1])


def assemble_loop(field, got_packs, got_rows, use):
    row = lax.broadcasted_iota(jnp.int32, (8, 128), 0)
    lane = lax.broadcasted_iota(jnp.int32, (8, 128), 1)

    def row_mean(x, above, below):
        up = jnp.where(row == 0, pltpu.roll(above, 1, 0), pltpu.roll(x, 1, 0))
        down = jnp.where(row == 7, pltpu.roll(below, 7, 0), pltpu.roll(x, 7, 0))
        other = jnp.where(row % 4 == 3, down, jnp.where(row % 4 == 0, up, x))
        return 0.5 * (x + other)

    left_halo = row_mean(got_packs[0], got_packs[1], got_packs[2])
    right_halo = row_mean(got_packs[3], got_packs[4], got_packs[5])
    edge_row = ((row == 0) | (row == 7))[None]
    upper = (row < 4)[None]
    is3, is4 = (row == 3)[None], (row == 4)[None]
    lane3, lane0 = (lane % 4 == 3)[None], (lane % 4 == 0)[None]
    first, last = (lane == 0)[None], (lane == 127)[None]

    def one(i, carry):
        left_c, right_c = carry
        means = []
        for half in range(2):
            at = pl.multiple_of(half * PTS + i * 64, 64)
            x = field[pl.ds(at, 64), :].reshape(8, 8, 128)
            lev = pl.multiple_of(half * LEV + i * 8, 8)
            above, below = (
                jnp.stack([got_rows[side, pl.ds(lev + k, 8, stride=0), :] for k in range(8)])
                for side in range(2)
            )
            other = jnp.where(is3, pltpu.roll(x, 7, 1), jnp.where(is4, pltpu.roll(x, 1, 1), x))
            other = jnp.where(edge_row, jnp.where(upper, above, below), other)
            means.append(0.5 * (x + other))
        lefts = [pltpu.roll(m, 1, 2) for m in means]
        rights = [pltpu.roll(m, 127, 2) for m in means]
        halo_l = jnp.stack([pltpu.roll(left_c, (128 - k) % 128, 1) if k else left_c for k in range(8)])
        halo_r = jnp.stack([pltpu.roll(right_c, 127 - k, 1) for k in range(8)])
        near_l = [jnp.where(first, halo_l, lefts[0]), jnp.where(first, lefts[0], lefts[1])]
        near_r = [jnp.where(last, rights[1], rights[0]), jnp.where(last, halo_r, rights[1])]
        done = []
        for half in range(2):
            m = means[half]
            other = jnp.where(lane3, near_r[half], jnp.where(lane0, near_l[half], m))
            done.append((0.5 * (m + other)).reshape(64, 128))
        use(i, done)
        return pltpu.roll(left_c, 120, 1), pltpu.roll(right_c, 120, 1)

    halos = (left_halo, right_halo)
    for i in range(9):
        halos = one(i, halos)


def chunk_of(ref, i):
    return ref[pl.ds(i * 8, 8), :, :].reshape(64, 256)


def put_halves(ref, i, x):
    for half in range(2):
        at = pl.multiple_of(half * PTS + i * 64, 64)
        ref[pl.ds(at, 64), :] = x[:, half * 128 : (half + 1) * 128]


def dynamics_kernel(
    tracer_h, wind_x_h, wind_y_h, drops_h, counts_h, growth_h, collision_h, by_rows_h, by_cols_h, selector_h,
    row_map_h, col_map_h, cells_h, owner_h, members_h,
    state, cell_forcing, pair_coef, growth_col, start, counts_out, unsort, sender, quadratic, linear, constant,
    tracer, wind_x, wind_y, drops, counts, growth, collision, by_rows, by_cols, selector,
    row_map, col_map, cells, owner, members, doubled,
    loads, piece_loads, field, total, packs, rows, got_packs, got_rows, send, recv,
):
    g, c, up, down, left, right = neighbours()
    barrier = pltpu.get_barrier_semaphore()
    around = [(up, c), (down, c)]
    around += [(r, s) for s in (left, right) for r in (g, up, down)]
    sources = [tracer_h, wind_x_h, wind_y_h, by_rows_h, by_cols_h, drops_h, counts_h, owner_h, collision_h,
               selector_h, growth_h, members_h, row_map_h, col_map_h, cells_h]
    targets = [tracer, wind_x, wind_y, by_rows, by_cols, drops, counts, owner, collision,
               selector, growth, members, row_map, col_map, cells]
    thirds = [
        [
            pltpu.make_async_copy(source.at[pl.ds(24 * n, 24)], target.at[pl.ds(24 * n, 24)], piece_loads.at[n, m])
            for m, (source, target) in enumerate(zip(sources[0:3], targets[0:3]))
        ]
        for n in range(3)
    ]
    fetch = [
        pltpu.make_async_copy(source, target, loads.at[n])
        for n, (source, target) in enumerate(zip(sources[3:], targets[3:]))
    ]
    for copy in thirds[0] + fetch[0:2]:
        copy.start()
    for to in around:
        pl.semaphore_signal(barrier, inc=1, device_id=to, device_id_type=MESH)
    for copy in thirds[1] + thirds[2] + fetch[2:]:
        copy.start()
    for copy in fetch[0:2]:
        copy.wait()
    for n in range(3):
        for copy in thirds[n]:
            copy.wait()
        for k in range(3):
            i = n * 3 + k
            put_halves(
                field, i,
                tendency(
                    chunk_of(tracer, i), chunk_of(wind_x, i), chunk_of(wind_y, i), by_rows[...], by_cols[...]
                ),
            )
    pack_edges(field, packs.at[0], rows.at[0])
    pl.semaphore_wait(barrier, 8)
    copies = halo_copies(packs.at[0], rows.at[0], got_packs.at[0], got_rows.at[0], send.at[0], recv.at[0])
    for copy in copies:
        copy.start()

    for copy in fetch[2:]:
        copy.wait()
    coef = jnp.dot(collision[...], selector[...], preferred_element_type=F32)
    coef = jnp.concatenate([coef, jnp.zeros((15, PAIRS), F32)], axis=0)
    pair_coef[...] = coef.astype(BF)
    i0 = lax.broadcasted_iota(jnp.int32, (COLS, COLS), 0)
    i1 = lax.broadcasted_iota(jnp.int32, (COLS, COLS), 1)
    wide = jnp.concatenate([growth[...], jnp.zeros((1, COLS - BINS), F32)], axis=1)
    growth_col[...] = jnp.broadcast_to(
        jnp.sum(
            jnp.where((i0 == i1)[0:ROWS], jnp.broadcast_to(wide, (ROWS, COLS)), 0.0), axis=1, keepdims=True
        ),
        (ROWS, COLS),
    )
    stacked = jnp.concatenate([jnp.broadcast_to(x.astype(F32), (16, COLS)) for x in split3(wide)], axis=0)
    slope = jnp.zeros((96, COLS), F32)
    for side in range(2):
        of_pair = lax.dot_general(
            stacked.astype(BF), members[side], (((1,), (1,)), ((), ())), preferred_element_type=F32
        )
        scaled = coef * (of_pair[0:1] + of_pair[16:17] + of_pair[32:33])
        near = scaled.astype(BF)
        terms = jnp.concatenate([near, (scaled - near.astype(F32)).astype(BF)], axis=0)
        slope = slope + jnp.dot(terms, members[1 - side], preferred_element_type=F32)
    slope = slope[0:48] + slope[48:96]
    constant[...] = jnp.broadcast_to(
        0.5 * jnp.sum(slope[0:ROWS] * wide, axis=1, keepdims=True), (ROWS, COLS)
    )
    near = slope.astype(BF)
    linear[...] = jnp.concatenate([near, (slope - near.astype(F32)).astype(BF)], axis=0)
    across = jnp.broadcast_to(counts[...], (COLS, COLS)).astype(F32)
    along = jnp.sum(jnp.where(i0 == i1, across, 0.0), axis=1, keepdims=True)
    before = (across > along) | ((across == along) & (i1 < i0))
    place = jnp.sum(jnp.where(before, 1.0, 0.0), axis=1, keepdims=True).astype(jnp.int32)
    after = (along > across) | ((along == across) & (i0 < i1))
    place_row = jnp.sum(jnp.where(after, 1.0, 0.0), axis=0, keepdims=True).astype(jnp.int32)
    counts_out[...] = jnp.sum(jnp.where(place == i1, along, 0.0), axis=0, keepdims=True).astype(jnp.int32)
    unsort[...] = jnp.where(place == i1, 1.0, 0.0).astype(BF)
    sort = jnp.where(place_row == i0, 1.0, 0.0).astype(BF)
    for b in range(BINS):
        sorted_bin = jnp.dot(sort, drops[b], preferred_element_type=F32)
        for half in range(2):
            start[pl.ds(half * COLS * ROWS + b, COLS, stride=ROWS), :] = sorted_bin[
                :, half * 128 : (half + 1) * 128
            ]

    for b in range(BINS, ROWS):
        for half in range(2):
            start[pl.ds(half * COLS * ROWS + b, COLS, stride=ROWS), :] = jnp.zeros((COLS, 128), F32)
    owners = jnp.broadcast_to(owner[...], (COLS, COLS))
    owned = jnp.sum(jnp.where(i0 == i1, owners.astype(F32), 0.0), axis=1, keepdims=True)
    earlier = (owned == owners.astype(F32)) & (i0 < i1)
    turn = jnp.sum(jnp.where(earlier, 1.0, 0.0), axis=0, keepdims=True)
    key = owners % NC * NG + owners // NC
    sender[...] = jnp.concatenate(
        [jnp.where((key == i0) & (turn == float(r)), 1.0, 0.0) for r in range(2)], axis=1
    ).astype(BF)

    def square(p, _):
        for b in range(16):
            drops_of = [start[column_rows(p * 16 + b, half), :] for half in range(2)]
            found = jnp.dot(pair_coef[...], pairs_of(drops_of, doubled.at[b]), preferred_element_type=F32)
            for half in range(2):
                quadratic[column_rows(p * 16 + b, half), :] = found[0:ROWS, half * 128 : (half + 1) * 128]
        return 0

    lax.fori_loop(0, EARLY, square, 0)
    halo_wait(got_packs.at[0], got_rows.at[0], send.at[0], recv.at[0])

    def second(i, means):
        mean = jnp.concatenate(means, axis=1)
        moved = chunk_of(tracer, i) + DT_DYN * mean
        state[pl.ds(i * 8, 8), :, :] = moved.reshape(8, 8, 256)
        put_halves(total, i, mean)
        put_halves(
            field, i,
            tendency(moved, chunk_of(wind_x, i), chunk_of(wind_y, i), by_rows[...], by_cols[...]),
        )

    assemble_loop(field, got_packs.at[0], got_rows.at[0], second)
    pack_edges(field, packs.at[1], rows.at[1])
    copies = halo_copies(packs.at[1], rows.at[1], got_packs.at[1], got_rows.at[1], send.at[1], recv.at[1])
    for copy in copies:
        copy.start()
    lax.fori_loop(EARLY, COLS // 16, square, 0)
    halo_wait(got_packs.at[1], got_rows.at[1], send.at[1], recv.at[1])

    def third(i, means):
        mean = jnp.concatenate(means, axis=1)
        state[pl.ds(i * 8, 8), :, :] = (chunk_of(state, i) + DT_DYN * mean).reshape(8, 8, 256)
        for half in range(2):
            at = pl.multiple_of(half * PTS + i * 64, 64)
            total[pl.ds(at, 64), :] = total[pl.ds(at, 64), :] + means[half]

    assemble_loop(field, got_packs.at[1], got_rows.at[1], third)
    sums = jnp.concatenate([total[0:PTS, :], total[PTS : 2 * PTS, :]], axis=1)
    near = sums.astype(BF)
    rest = (sums - near.astype(F32)).astype(BF)
    by_row = jnp.dot(row_map[...], near, preferred_element_type=F32)
    by_row = by_row[0:32] + by_row[32:64] + jnp.dot(row_map[0:32, :], rest, preferred_element_type=F32)
    forcing = [
        lax.dot_general(
            col_map[...], by_row[16 * e : 16 * (e + 1)], (((1,), (1,)), ((), ())),
            precision=HIGH, preferred_element_type=F32,
        ).astype(BF)
        for e in range(2)
    ]
    by_cell = jnp.dot(
        jnp.concatenate(forcing, axis=0), cells[...], preferred_element_type=F32
    ).astype(BF)
    cell_forcing[...] = DT_CRM * jnp.dot(sort, by_cell, preferred_element_type=F32)


def dynamics(tracer, wind_x, wind_y, drops, counts_row, growth_row, collision, owner_row):
    row_map, col_map = forcing_tables()
    near = row_map.astype(ml_dtypes.bfloat16)
    row_map = np.concatenate([near, (row_map - near.astype(np.float32)).astype(ml_dtypes.bfloat16)])
    by_rows, by_cols = stencil_tables()
    shape = tracer.shape
    operands = (
        tracer, wind_x, wind_y, drops, counts_row, growth_row, collision,
        jnp.asarray(by_rows), jnp.asarray(by_cols), jnp.asarray(pair_selector()),
        jnp.asarray(row_map), jnp.asarray(col_map), jnp.asarray(spread_cells()), owner_row,
        jnp.asarray(pair_members()),
    )
    return pl.pallas_call(
        dynamics_kernel,
        out_shape=(
            jax.ShapeDtypeStruct(shape, F32),
            jax.ShapeDtypeStruct((COLS, 256), F32),
            jax.ShapeDtypeStruct((48, PAIRS), BF),
            jax.ShapeDtypeStruct((ROWS, 128), F32),
            jax.ShapeDtypeStruct((2 * COLS * ROWS, 128), F32),
            jax.ShapeDtypeStruct((1, COLS), jnp.int32),
            jax.ShapeDtypeStruct((COLS, COLS), BF),
            jax.ShapeDtypeStruct((COLS, 2 * COLS), BF),
            jax.ShapeDtypeStruct((2 * COLS * ROWS, 128), F32),
            jax.ShapeDtypeStruct((96, 128), BF),
            jax.ShapeDtypeStruct((ROWS, 128), F32),
        ),
        in_specs=[HBM] * 15,
        out_specs=(VMEM,) * 11,
        scratch_shapes=[pltpu.VMEM(x.shape, x.dtype) for x in operands]
        + [
            pltpu.VMEM((16, 2, 48, 128), F32),
            pltpu.SemaphoreType.DMA((12,)),
            pltpu.SemaphoreType.DMA((3, 3)),
            pltpu.VMEM((2 * PTS, 128), F32),
            pltpu.VMEM((2 * PTS, 128), F32),
            pltpu.VMEM((2, 2, 8, 128), F32),
            pltpu.VMEM((2, 2, 2 * LEV, 128), F32),
            pltpu.VMEM((2, 6, 8, 128), F32),
            pltpu.VMEM((2, 2, 2 * LEV, 128), F32),
            pltpu.SemaphoreType.DMA((2, 2)),
            pltpu.SemaphoreType.DMA((2, 2)),
        ],
        compiler_params=pltpu.CompilerParams(
            collective_id=0, has_side_effects=True, vmem_limit_bytes=40 << 20
        ),
        name="dynamics",
    )(*[pltpu.with_memory_space_constraint(x, pltpu.HBM) for x in operands])


def micro_kernel(
    counts, start, cell_forcing, pair_coef, growth, group, unsort, quadratic, linear, constant,
    drops_next, heat_out, echo_out,
    cloud, doubled, grow, heat_rows, echo_rows, drops_out, stores,
):
    bins = lax.broadcasted_iota(jnp.int32, (ROWS, 128), 0)
    mass = jnp.where(bins < BINS, (bins.astype(F32) + 1.0) / BINS, 0.0)

    def place(p, b, half):
        return column_rows(p * BATCH + b, half)

    def advance(col, b, active=None):
        olds = [cloud[column_rows(col, half), :] for half in range(2)]
        grown = [olds[half] + grow[b, half] for half in range(2)]
        change = jnp.dot(pair_coef[...], pairs_of(grown, doubled.at[b]), preferred_element_type=F32)
        for half in range(2):
            moved = grown[half] + DT_CRM * change[0:ROWS, half * 128 : (half + 1) * 128]
            if active is not None:
                moved = jnp.where(active, moved, olds[half])
            cloud[column_rows(col, half), :] = moved

    def substep(_, p):
        for b in range(BATCH):
            advance(p * BATCH + b, b)
        return p

    def ragged(s, p):
        def part(h, _):
            @pl.when(s < counts[0, p * BATCH + h * 16])
            def _():
                for k in range(16):
                    col = p * BATCH + h * 16 + k
                    advance(col, h * 16 + k, s < counts[0, col])

            return 0

        lax.fori_loop(0, BATCH // 16, part, 0)
        return p

    def batch(p, _):
        for b in range(BATCH):
            active = counts[0, p * BATCH + b] > 0
            forced = cell_forcing[pl.ds(p * BATCH + b, 1), :]
            olds = [start[place(p, b, half), :] for half in range(2)]
            rows = [jnp.concatenate([old, old[0:8]], axis=0).astype(BF) for old in olds]
            sloped = jnp.dot(linear[:, 0:48], jnp.concatenate(rows, axis=1), preferred_element_type=F32)
            for half in range(2):
                at = slice(half * 128, (half + 1) * 128)
                f = forced[:, at]
                add = f * growth[...]
                change = quadratic[place(p, b, half), :] + f * (
                    sloped[0:ROWS, at] + sloped[48 : 48 + ROWS, at] + f * constant[...]
                )
                grow[b, half] = add
                moved = olds[half] + add + DT_CRM * change
                cloud[place(p, b, half), :] = jnp.where(active, moved, olds[half])
        common = jnp.maximum(counts[0, p * BATCH + BATCH - 1], 1)
        lax.fori_loop(1, common, substep, p)
        lax.fori_loop(common, counts[0, p * BATCH], ragged, p)
        for half in range(2):
            at = slice(half * 128, (half + 1) * 128)
            for eight in range(BATCH // 8):
                heats, echos = [], []
                for b in range(8):
                    where = place(p, eight * 8 + b, half)
                    final = cloud[where, :]
                    gain = (final - start[where, :]) * mass
                    weighed = final * mass
                    square = weighed * weighed
                    heats.append(sum(gain[8 * k : 8 * k + 8] for k in range(5)))
                    echos.append(sum(square[8 * k : 8 * k + 8] for k in range(5)))
                heats, echos = rows_of_sums(heats), rows_of_sums(echos)
                rows = pl.ds(pl.multiple_of(p * BATCH + eight * 8, 8), 8)
                heat_rows[rows, at] = heats
                echo_rows[rows, at] = echos
        return 0

    lax.fori_loop(0, COLS // BATCH, batch, 0)

    def group_mean(x):
        acc = None
        for part in split3(x):
            y = jnp.dot(part, group[...], preferred_element_type=F32)
            acc = y if acc is None else acc + y
        return acc

    back = unsort[...]
    pieces = []
    for n in range(3):
        for b in range(11 * n, 11 * n + 11):
            halves = [cloud[pl.ds(half * COLS * ROWS + b, COLS, stride=ROWS), :] for half in range(2)]
            drops_out[b] = jnp.dot(
                back, jnp.concatenate(halves, axis=1).astype(BF), preferred_element_type=F32
            ).astype(BF)
        part = pl.ds(11 * n, 11)
        piece = pltpu.make_async_copy(drops_out.at[part], drops_next.at[part], stores.at[n])
        piece.start()
        pieces.append(piece)
    heat = group_mean(heat_rows[...]).astype(BF)
    heat_out[...] = jnp.dot(back, heat, preferred_element_type=F32).astype(BF)
    echo_out[...] = jnp.log(1.0 + dot_exact(back, group_mean(echo_rows[...])))
    for piece in pieces:
        piece.wait()


def microphysics(counts, start, cell_forcing, pair_coef, growth, unsort, quadratic, linear, constant):
    return pl.pallas_call(
        micro_kernel,
        out_shape=(
            jax.ShapeDtypeStruct((BINS, COLS, 256), BF),
            jax.ShapeDtypeStruct((COLS, 128), BF),
            jax.ShapeDtypeStruct((COLS, 128), F32),
        ),
        in_specs=[SMEM] + [VMEM] * 9,
        out_specs=(HBM, VMEM, VMEM),
        scratch_shapes=[
            pltpu.VMEM((2 * COLS * ROWS, 128), F32),
            pltpu.VMEM((BATCH, 2, 48, 128), F32),
            pltpu.VMEM((BATCH, 2, ROWS, 128), F32),
            pltpu.VMEM((COLS, 256), F32),
            pltpu.VMEM((COLS, 256), F32),
            pltpu.VMEM((BINS, COLS, 256), BF),
            pltpu.SemaphoreType.DMA((3,)),
        ],
        compiler_params=pltpu.CompilerParams(vmem_limit_bytes=40 << 20),
        name="microphysics",
    )(
        counts, start, cell_forcing, pair_coef, growth, jnp.asarray(group_matrix()), unsort,
        quadratic, linear, constant,
    )


def coupling_kernel(
    state, heat, echo, sender, heating, spread,
    tracer_next, rows_out,
    field, packs, rows, got_packs, got_rows, sent, first_in, second_out, second_in,
    send, recv, power_send, power_recv,
):
    g, c, up, down, left, right = neighbours()
    barrier = pltpu.get_barrier_semaphore()
    peers = [(lax.rem(g + k, NG), c) for k in range(1, NG)]
    peers += [(g, lax.rem(c + k, NC)) for k in range(1, NC)]
    peers += [(r, s) for s in (left, right) for r in (up, down)]
    for to in peers:
        pl.semaphore_signal(barrier, inc=1, device_id=to, device_id_type=MESH)

    sums = echo[...]
    sums = jnp.concatenate([sums, pltpu.roll(sums, 16, 1)], axis=0)
    sent[...] = dot_exact(sender[...], sums).reshape(NC, NG, 128)
    pl.semaphore_wait(barrier, len(peers))
    for k in range(1, NC):
        to = lax.rem(c + k, NC)
        pltpu.make_async_remote_copy(
            src_ref=sent.at[to],
            dst_ref=first_in.at[c],
            send_sem=power_send.at[0],
            recv_sem=power_recv.at[0],
            device_id=(g, to),
            device_id_type=MESH,
        ).start()
    first_in[c] = sent[c]

    warm = []
    for e in range(2):
        turned = heat[64 * e : 64 * (e + 1), :].astype(F32).T.astype(BF)[0:16]
        warm.append(jnp.dot(turned, spread[...], preferred_element_type=F32).astype(BF))
    warm = jnp.concatenate(warm + warm, axis=0)
    for half in range(2):
        at = slice(half * 128, (half + 1) * 128)
        back = jnp.dot(heating[...], warm[:, at], preferred_element_type=F32)
        field[half * PTS : (half + 1) * PTS, :] = back + state[:, :, at].reshape(PTS, 128)
    pack_edges(field, packs, rows)
    for copy in halo_copies(packs, rows, got_packs, got_rows, send, recv):
        copy.start()

    for sems in (power_recv, power_send):
        wait_bytes(first_in.at[0 : NC - 1], sems.at[0])
    every = first_in[...]
    for to in range(NG):
        second_out[to] = every[:, to, :]
    for k in range(1, NG):
        to = lax.rem(g + k, NG)
        pltpu.make_async_remote_copy(
            src_ref=second_out.at[to],
            dst_ref=second_in.at[g],
            send_sem=power_send.at[1],
            recv_sem=power_recv.at[1],
            device_id=(to, c),
            device_id_type=MESH,
        ).start()
    second_in[g] = second_out[g]

    halo_wait(got_packs, got_rows, send, recv)

    def last(i, means):
        for half in range(2):
            tracer_next[pl.ds(i * 8, 8), :, half * 128 : (half + 1) * 128] = means[half].reshape(8, 8, 128)

    assemble_loop(field, got_packs, got_rows, last)

    for sems in (power_recv, power_send):
        wait_bytes(second_in.at[0 : NG - 1], sems.at[1])
    rows_out[...] = second_in[...].reshape(COLS, 128)


def coupling(state, heat, echo, sender):
    return pl.pallas_call(
        coupling_kernel,
        out_shape=(
            jax.ShapeDtypeStruct(state.shape, F32),
            jax.ShapeDtypeStruct((COLS, 128), F32),
        ),
        in_specs=[VMEM] * 6,
        out_specs=(VMEM,) * 2,
        scratch_shapes=[
            pltpu.VMEM((2 * PTS, 128), F32),
            pltpu.VMEM((2, 8, 128), F32),
            pltpu.VMEM((2, 2 * LEV, 128), F32),
            pltpu.VMEM((6, 8, 128), F32),
            pltpu.VMEM((2, 2 * LEV, 128), F32),
            pltpu.VMEM((NC, NG, 128), F32),
            pltpu.VMEM((NC, NG, 128), F32),
            pltpu.VMEM((NG, NC, 128), F32),
            pltpu.VMEM((NG, NC, 128), F32),
            pltpu.SemaphoreType.DMA((2,)),
            pltpu.SemaphoreType.DMA((2,)),
            pltpu.SemaphoreType.DMA((2,)),
            pltpu.SemaphoreType.DMA((2,)),
        ],
        compiler_params=pltpu.CompilerParams(
            collective_id=1, has_side_effects=True, vmem_limit_bytes=40 << 20
        ),
        name="coupling",
    )(
        state, heat, echo, sender,
        jnp.asarray(heating_table()), jnp.asarray(spread_columns()),
    )


def finish_kernel(mean, rows, slots, tracer_next, power, store):
    copy = pltpu.make_async_copy(mean, tracer_next, store)
    copy.start()
    turned = rows[...].T
    turned = jnp.concatenate([turned[0:16], turned[16:32]], axis=1)
    parts = jnp.dot(jnp.concatenate(split3(turned), axis=0), slots[...], preferred_element_type=F32)
    power[...] = parts[0:16] + parts[16:32] + parts[32:48]
    copy.wait()


def finish(mean, rows):
    return pl.pallas_call(
        finish_kernel,
        out_shape=(
            jax.ShapeDtypeStruct(mean.shape, F32),
            jax.ShapeDtypeStruct((CLEV, 256), F32),
        ),
        in_specs=[VMEM] * 3,
        out_specs=(HBM, VMEM),
        scratch_shapes=[pltpu.SemaphoreType.DMA(())],
        compiler_params=pltpu.CompilerParams(vmem_limit_bytes=8 << 20),
        name="finish",
    )(mean, rows, jnp.asarray(slot_table()))


def shards(tracer, wind_x, wind_y, drops, owner, counts, collision, growth):
    state, cell_forcing, pair_coef, growth_col, start, sorted_counts, unsort, sender, quadratic, linear, constant = dynamics(
        tracer, wind_x, wind_y, drops.transpose(1, 0, 2),
        counts.reshape(1, COLS), growth.reshape(1, BINS), collision, owner.reshape(1, COLS),
    )
    drops_next, heat, echo = microphysics(
        sorted_counts, start, cell_forcing, pair_coef, growth_col, unsort, quadratic, linear, constant
    )
    tracer_next, power = finish(*coupling(state, heat, echo, sender))
    return (tracer_next, drops_next.transpose(1, 0, 2), power)


def solution(mesh):
    return jax.shard_map(
        shards,
        mesh=mesh,
        in_specs=(
            P(None, "gcm", "crm"),
            P(None, "gcm", "crm"),
            P(None, "gcm", "crm"),
            P(("gcm", "crm"), None, None),
            P(("gcm", "crm"), None),
            P(("gcm", "crm")),
            P(),
            P(),
        ),
        out_specs=(P(None, "gcm", "crm"), P(("gcm", "crm"), None, None), P(None, ("gcm", "crm"))),
        check_vma=False,
    )
```
